32 devices in a mesh: seq: 4 (over x, core), fsdp: 8 (over z, y).
Axes of the slice: x: 2, y: 2, z: 4, core: 2. Of those that a mesh axis runs over, the one named last changes fastest.
Arguments:
- inputs: bfloat16 [8, 8192, 1024], P('fsdp', 'seq'), may hold values from -8 to 8
- cotangent: bfloat16 [8, 8192, 1024], P('fsdp', 'seq'), may hold values from -6 to 6
- routed: int32 [8, 4, 256], P('fsdp'), may hold values from 0 to 2047, as said below
- doc_starts: int32 [8, 16], P('fsdp'), may hold values from 0 to 8191, as said below
- router: bfloat16 [1024], P('fsdp'), may hold values from -0.1875 to 0.1875
- attn_gain: bfloat16 [1024], P('fsdp'), may hold values from 0.5 to 1.5
- qkv_weight: bfloat16 [1024, 3072], P('fsdp'), may hold values from -0.1875 to 0.1875
- out_weight: bfloat16 [1024, 1024], P('fsdp'), may hold values from -1.5 to 1.5
- mlp_gain: bfloat16 [1024], P('fsdp'), may hold values from 0.5 to 1.5
- up_weight: bfloat16 [1024, 4096], P('fsdp'), may hold values from -0.1875 to 0.1875
- down_weight: bfloat16 [4096, 1024], P('fsdp'), may hold values from -0.09375 to 0.09375
Outputs:
- output: bfloat16 [8, 8192, 1024], P('fsdp', 'seq')
- input_grad: bfloat16 [8, 8192, 1024], P('fsdp', 'seq')
- router_grad: float32 [1024], P(('seq', 'fsdp'))
- attn_gain_grad: float32 [1024], P(('seq', 'fsdp'))
- qkv_grad: float32 [1024, 3072], P(('seq', 'fsdp'))
- out_grad: float32 [1024, 1024], P(('seq', 'fsdp'))
- mlp_gain_grad: float32 [1024], P(('seq', 'fsdp'))
- up_grad: float32 [1024, 4096], P(('seq', 'fsdp'))
- down_grad: float32 [4096, 1024], P(('seq', 'fsdp'))
The draws below stay inside these ranges and needn't reach their ends.
Inputs may be any that keep to these rules, and one draw needn't show every extreme that they name: `routed`: each window of 2048 positions of a stream routes 256 distinct positions, counted from the window's first position and listed in ascending order. `doc_starts`: the first positions of the documents of each stream, in non-decreasing order, the first one 0; equal entries leave empty documents.
All inputs are finite; a program needn't handle non-finite values.
Results may differ from the reference program's by a relative error of at most 0.011.
Values may be sent and summed in bfloat16 or wider, within the bound.
No kernel may reach another device: no remote copies, remote signals or barrier semaphores. Data moves between devices by JAX's collectives and lax.ppermute only.
A program may use at most 256 MiB of HBM per device.

```python
import math
from functools import partial
import jax
import jax.numpy as jnp
from jax import lax

D = 1024
H = 16
HD = 64
FF = 4096
WIN = 2048
CAP = 256
DOCS = 16
STREAMS = 8
LENGTH = 8192
WINS = 4
ROUTED = 1024


def draw_inputs(key, part):
    key_base, key_rows, key_cols = jax.random.split(key, 3)
    base = jax.random.normal(key_base, (STREAMS, LENGTH, D), jnp.float32)
    row_scale = jnp.exp(jax.random.uniform(key_rows, (STREAMS, LENGTH, 1), jnp.float32, math.log(0.3), math.log(3.0)))
    col_scale = jnp.exp(jax.random.uniform(key_cols, (1, 1, D), jnp.float32, math.log(0.5), math.log(2.0)))
    return jnp.clip(base * row_scale * col_scale, -8.0, 8.0).astype(jnp.bfloat16)


def draw_routed(key, part):
    count = STREAMS * WINS
    scores = jax.random.randint(key, (count, WIN), 0, 2 ** 19, dtype=jnp.int32) * WIN + jnp.arange(WIN, dtype=jnp.int32)[None, :]
    scores = scores.at[0, 0].set(-2).at[0, WIN - 1].set(-1)
    chosen = jnp.argsort(scores, axis=1)[:, :CAP]
    return jnp.sort(chosen, axis=1).astype(jnp.int32).reshape(STREAMS, WINS, CAP)


def draw_doc_starts(key, part):
    inner = jnp.sort(jax.random.randint(key, (STREAMS, DOCS - 1), 1, LENGTH, dtype=jnp.int32), axis=1)
    starts = jnp.concatenate([jnp.zeros((STREAMS, 1), jnp.int32), inner.astype(jnp.int32)], axis=1)
    return starts.at[0, DOCS - 1].set(LENGTH - 1)


def levels(key, dims, cuts, low, top_value):
    def one(dim, parts):
        heights = jax.random.uniform(jax.random.fold_in(jax.random.fold_in(key, 6), dim), (parts,), jnp.float32, low / len(cuts), top_value / len(cuts))
        return jnp.repeat(jnp.exp(heights), dims[dim] // parts).reshape((-1,) + (1,) * (len(dims) - dim - 1))

    level = one(*cuts[0])
    for cut in cuts[1:]:
        level = level * one(*cut)
    return level


def normal_values(rng, shape, scale, limit, cuts=(), kind=jnp.bfloat16):
    factor_of = levels(rng, shape, cuts, -0.22, 0.18) if cuts else 1.0
    drawn = jax.random.normal(rng, shape, jnp.float32) * scale * factor_of
    return jnp.minimum(jnp.maximum(drawn, -limit), limit).astype(kind)


def setup_inputs(seed: int = 0) -> dict:
    streams_of = jax.random.split(jax.random.key(seed), 12)
    return {
        "inputs": draw_inputs(jax.random.fold_in(streams_of[11], 71), 0),
        "cotangent": normal_values(streams_of[1], (STREAMS, LENGTH, D), 1.0, 6.0, ((0, 8), (1, 4))),
        "routed": draw_routed(jax.random.fold_in(streams_of[11], 71), 0),
        "doc_starts": draw_doc_starts(jax.random.fold_in(streams_of[11], 71), 0),
        "router": normal_values(streams_of[4], (D,), D ** -0.5, 0.1875, ((0, 8),)),
        "attn_gain": jnp.clip(1.0 + 0.1 * jax.random.normal(streams_of[5], (D,), jnp.float32), 0.5, 1.5).astype(jnp.bfloat16),
        "qkv_weight": normal_values(streams_of[6], (D, 3 * D), D ** -0.5, 0.1875, ((0, 8),)),
        "out_weight": normal_values(streams_of[7], (D, D), (D // 64) ** -0.5, 1.5, ((0, 8),)),
        "mlp_gain": jnp.clip(1.0 + 0.1 * jax.random.normal(streams_of[8], (D,), jnp.float32), 0.5, 1.5).astype(jnp.bfloat16),
        "up_weight": normal_values(streams_of[9], (D, FF), D ** -0.5, 0.1875, ((0, 8),)),
        "down_weight": normal_values(streams_of[10], (FF, D), FF ** -0.5, 0.09375, ((0, 8),)),
    }


EPS = 1e-05
NEG_FILL = -1e+30
HIGH = lax.Precision.HIGHEST

@jax.custom_vjp
def low(v):
    return lax.optimization_barrier(v.astype(jnp.bfloat16)).astype(jnp.float32)

@jax.custom_vjp
def low_back(v):
    return v

def low_keep(v):
    return (low(v), None)

def low_pass(kept, grad):
    return (grad,)

def back_keep(v):
    return (v, None)

def back_low(kept, grad):
    return (low(grad),)
low.defvjp(low_keep, low_pass)
low_back.defvjp(back_keep, back_low)

def normed(values, gain_vec):
    return values * lax.rsqrt(lax.optimization_barrier(jnp.mean(values * values, axis=-1, keepdims=True)) + EPS) * gain_vec

def attend_head(query, keyed, valued, segment):
    head_scale = HD ** (-0.5)
    scores = low_back(jnp.dot(query, keyed.T, precision=HIGH) * head_scale)
    ranks = jnp.arange(query.shape[0], dtype=jnp.int32)
    allowed = (segment[:, None] == segment[None, :]) & (ranks[:, None] >= ranks[None, :])
    scores = jnp.where(allowed, scores, NEG_FILL)
    row_max = lax.optimization_barrier(jnp.max(scores, axis=-1, keepdims=True))
    exponent = jnp.exp(scores - row_max)
    weights_p = exponent / lax.optimization_barrier(jnp.sum(exponent, axis=-1, keepdims=True))
    return jnp.dot(low(weights_p), valued, precision=HIGH)

def split_heads(columns):
    return columns.reshape(columns.shape[0], H, HD).transpose(1, 0, 2)

def stream_forward(picked, router_w, gain_a, w_qkv, w_out, gain_m, w_up, w_down, segment):
    routed_len = picked.shape[0]
    logit = jnp.dot(picked, router_w, precision=HIGH)
    router_rate = jax.nn.sigmoid(logit)
    normal_a = low(normed(picked, gain_a))
    projected = low_back(low(jnp.dot(normal_a, w_qkv, precision=HIGH)))
    heads_q = split_heads(projected[:, :D])
    heads_k = split_heads(projected[:, D:2 * D])
    heads_v = split_heads(projected[:, 2 * D:])

    def one_head(trio):
        return attend_head(trio[0], trio[1], trio[2], segment)
    attended = lax.map(jax.checkpoint(one_head), (heads_q, heads_k, heads_v))
    attended = attended.transpose(1, 0, 2).reshape(routed_len, D)
    attended = low_back(low(attended))
    branch_a = low_back(jnp.dot(attended, w_out, precision=HIGH))
    middle = picked + branch_a
    normal_m = low(normed(middle, gain_m))
    pre_act = low_back(jnp.dot(normal_m, w_up, precision=HIGH))
    activated = low(jax.nn.gelu(pre_act, approximate=False))
    branch_f = low_back(jnp.dot(activated, w_down, precision=HIGH))
    return picked + router_rate[:, None] * (branch_a + branch_f)

def reference(inputs, cotangent, routed, doc_starts, router, attn_gain, qkv_weight, out_weight, mlp_gain, up_weight, down_weight):
    positions = (jnp.arange(WINS, dtype=jnp.int32) * WIN)[None, :, None] + routed.astype(jnp.int32)
    positions = positions.reshape(STREAMS, ROUTED).astype(jnp.int32)
    segments = lax.optimization_barrier(jnp.sum((doc_starts[:, None, :] <= positions[:, :, None]).astype(jnp.int32), axis=2))
    picked = jnp.take_along_axis(inputs, positions[:, :, None], axis=1).astype(jnp.float32)
    grad_rows = jnp.take_along_axis(cotangent, positions[:, :, None], axis=1).astype(jnp.float32)
    weights = tuple((weight_arr.astype(jnp.float32) for weight_arr in (router, attn_gain, qkv_weight, out_weight, mlp_gain, up_weight, down_weight)))

    def per_stream(sums, item):
        picked_s, grad_s, segment_s = item
        result, pull = jax.vjp(partial(stream_forward, segment=segment_s), picked_s, *weights)
        grads = pull(grad_s)
        sums = tuple((total + grad for total, grad in zip(sums, grads[1:])))
        return (sums, (result, grads[0]))
    start_sums = tuple((jnp.zeros(weight_arr.shape, jnp.float32) for weight_arr in weights))
    sums, (results, input_rows) = lax.scan(per_stream, start_sums, (picked, grad_rows, segments))
    flat = ((jnp.arange(STREAMS, dtype=jnp.int32) * LENGTH)[:, None] + positions).reshape(-1).astype(jnp.int32)
    output = inputs.reshape(STREAMS * LENGTH, D).at[flat].set(results.reshape(-1, D).astype(jnp.bfloat16)).reshape(STREAMS, LENGTH, D)
    input_grad = cotangent.reshape(STREAMS * LENGTH, D).at[flat].set(input_rows.reshape(-1, D).astype(jnp.bfloat16)).reshape(STREAMS, LENGTH, D)
    return (output, input_grad, sums[0], sums[1], sums[2], sums[3], sums[4], sums[5], sums[6])
```

```python
from functools import partial

import jax
import jax.numpy as jnp
from jax import lax
from jax.experimental import pallas as pl
from jax.experimental.pallas import tpu as pltpu
from jax.sharding import PartitionSpec as P

H = 16
HD = 64
WIN = 2048
EPS = 1e-05
NEG_FILL = -1e30
PAIR = 2 * HD
LANES = 128
BF16 = jnp.bfloat16
F32 = jnp.float32


def mm(a, b, dims):
    return lax.dot_general(a, b, (dims, ((), ())), preferred_element_type=F32)


NN = ((1,), (0,))
NT = ((1,), (1,))
TN = ((0,), (0,))


def flip(values, axis, bit):
    count = lax.axis_size(axis)
    return lax.ppermute(values, axis, [(j, j ^ bit) for j in range(count)])


def bits_down(count):
    bit = count // 2
    while bit:
        yield bit
        bit //= 2


def gather_blocks(own, axis):
    blocks = {0: own}
    for bit in bits_down(lax.axis_size(axis)):
        for key in list(blocks):
            blocks[key ^ bit] = flip(blocks[key], axis, bit)
    return [blocks[key] for key in sorted(blocks)]


def scatter_blocks(blocks, axis):
    parts = dict(enumerate(blocks))
    bit = 1
    while bit < lax.axis_size(axis):
        for key in [k for k in parts if k & bit]:
            got = flip(parts.pop(key).astype(BF16), axis, bit)
            parts[key ^ bit] = parts[key ^ bit] + got.astype(F32)
        bit *= 2
    return parts[0]


def head_lanes(rows):
    return lax.broadcasted_iota(jnp.int32, (rows, PAIR), 1) < HD


def allowed_tile(cols_ref, where, rows_pos, rows_start):
    cols = cols_ref[where]
    return (cols <= rows_pos) & (cols >= rows_start)


def attention_forward_kernel(
    window_ref, place_ref, first_ref, q_ref, k_ref, v_ref, pos_ref, start_ref, cols_ref, o_ref, lse_ref
):
    block = pl.program_id(0)
    tile = q_ref.shape[0]
    pairs = q_ref.shape[1] // PAIR
    low_lanes = head_lanes(tile)
    rows_pos = pos_ref[...]
    rows_start = start_ref[...]
    last = window_ref[block]
    count = last - first_ref[block] + 1
    lane = lax.broadcasted_iota(jnp.int32, (tile, LANES), 1)
    lse = jnp.zeros((tile, LANES), F32)
    for pair in range(pairs):
        lanes = pl.ds(pair * PAIR, PAIR)
        q_pair = q_ref[:, lanes] * jnp.asarray(HD**-0.5, BF16)
        halves = []
        for half in range(2):
            q_half = jnp.where(low_lanes == (half == 0), q_pair, jnp.zeros_like(q_pair))

            def step(i, carry):
                top, total, acc = carry
                where = place_ref[last - i]
                scores = mm(q_half, k_ref[where, :, lanes], NT)
                scores = jnp.where(
                    allowed_tile(cols_ref, where, rows_pos, rows_start), scores, NEG_FILL
                )
                new_top = jnp.maximum(top, jnp.max(scores, axis=1, keepdims=True))
                shrink = jnp.exp(top - new_top)
                exponent = jnp.exp(scores - new_top)
                total = total * shrink + jnp.sum(exponent, axis=1, keepdims=True)
                acc = acc * shrink + mm(exponent.astype(BF16), v_ref[where, :, lanes], NN)
                return (new_top, total, acc)

            top, total, acc = lax.fori_loop(
                0,
                count,
                step,
                (
                    jnp.full((tile, 1), NEG_FILL, F32),
                    jnp.zeros((tile, 1), F32),
                    jnp.zeros((tile, PAIR), F32),
                ),
            )
            halves.append(acc / total)
            lse = jnp.where(lane == 2 * pair + half, top + jnp.log(total), lse)
        o_ref[:, lanes] = jnp.where(low_lanes, halves[0], halves[1]).astype(BF16)
    lse_ref[...] = lse


def attention_backward_kernel(
    window_ref,
    place_ref,
    first_ref,
    q_ref,
    k_ref,
    v_ref,
    g_ref,
    lse_ref,
    pos_ref,
    start_ref,
    cols_ref,
    dq_ref,
    dk_ref,
    dv_ref,
    dk_sum,
    dv_sum,
    prob_keep,
    grad_keep,
):
    block = pl.program_id(0)
    tile = q_ref.shape[0]
    pairs = q_ref.shape[1] // PAIR
    scale = HD**-0.5
    low_lanes = head_lanes(tile)
    rows_pos = pos_ref[...]
    rows_start = start_ref[...]
    last = window_ref[block]
    count = last - first_ref[block] + 1

    @pl.when(block == 0)
    def _():
        dk_sum[...] = jnp.zeros_like(dk_sum)
        dv_sum[...] = jnp.zeros_like(dv_sum)

    for pair in range(pairs):
        lanes = pl.ds(pair * PAIR, PAIR)
        q_pair = q_ref[:, lanes] * jnp.asarray(scale, BF16)
        g_pair = g_ref[:, lanes]
        halves = []
        for half in range(2):
            keep = low_lanes == (half == 0)
            q_half = jnp.where(keep, q_pair, jnp.zeros_like(q_pair))
            g_half = jnp.where(keep, g_pair, jnp.zeros_like(g_pair))
            lse = lse_ref[:, 2 * pair + half : 2 * pair + half + 1]

            def first_pass(i, inner):
                where = place_ref[last - i]
                scores = mm(q_half, k_ref[where, :, lanes], NT)
                prob = jnp.where(
                    allowed_tile(cols_ref, where, rows_pos, rows_start),
                    jnp.exp(scores - lse),
                    0.0,
                )
                grad_prob = mm(g_half, v_ref[where, :, lanes], NT)
                prob_keep[i] = prob
                grad_keep[i] = grad_prob
                dv_sum[where, :, lanes] += mm(prob.astype(BF16), g_half, TN)
                return inner + jnp.sum(prob * grad_prob, axis=1, keepdims=True)

            inner = lax.fori_loop(0, count, first_pass, jnp.zeros((tile, 1), F32))

            def second_pass(i, acc):
                where = place_ref[last - i]
                grad_scores = (prob_keep[i] * (grad_keep[i] - inner)).astype(BF16)
                dk_sum[where, :, lanes] += mm(grad_scores, q_half, TN)
                return acc + mm(grad_scores, k_ref[where, :, lanes], NN)

            acc = lax.fori_loop(0, count, second_pass, jnp.zeros((tile, PAIR), F32))
            halves.append(acc * scale)
        dq_ref[:, lanes] = jnp.where(low_lanes, halves[0], halves[1]).astype(BF16)

    @pl.when(block == pl.num_programs(0) - 1)
    def _():
        dk_ref[...] = dk_sum[...].astype(BF16)
        dv_ref[...] = dv_sum[...].astype(BF16)


VMEM_LIMIT = 48 * 1024 * 1024


def attention_specs(blocks, tile, width):
    by_rows = lambda cols: pl.BlockSpec((tile, cols), lambda b, *_: (b, 0))
    whole = lambda *dims: pl.BlockSpec(dims, lambda b, *_: (0,) * len(dims))
    keys = whole(blocks, tile, width)
    return by_rows, keys, whole(blocks, 1, tile)


def attention_forward(tables, q, k, v, pos, start, tile):
    rows, width = q.shape
    blocks = rows // tile
    by_rows, keys, cols = attention_specs(blocks, tile, width)
    return pl.pallas_call(
        attention_forward_kernel,
        grid_spec=pltpu.PrefetchScalarGridSpec(
            num_scalar_prefetch=3,
            grid=(blocks,),
            in_specs=[by_rows(width), keys, keys, by_rows(1), by_rows(1), cols],
            out_specs=[by_rows(width), by_rows(LANES)],
        ),
        out_shape=[
            jax.ShapeDtypeStruct((rows, width), BF16),
            jax.ShapeDtypeStruct((rows, LANES), F32),
        ],
        compiler_params=pltpu.CompilerParams(vmem_limit_bytes=VMEM_LIMIT),
        cost_estimate=pl.CostEstimate(
            flops=2 * rows * rows * width,
            transcendentals=rows * rows * width // HD // 2,
            bytes_accessed=8 * rows * width,
        ),
        name="attention_forward",
    )(
        *tables,
        q,
        k.reshape(blocks, tile, width),
        v.reshape(blocks, tile, width),
        pos[:, None],
        start[:, None],
        pos.reshape(blocks, 1, tile),
    )


def attention_backward(tables, q, k, v, grad, lse, pos, start, tile):
    rows, width = q.shape
    blocks = rows // tile
    by_rows, keys, cols = attention_specs(blocks, tile, width)
    dq, dk, dv = pl.pallas_call(
        attention_backward_kernel,
        grid_spec=pltpu.PrefetchScalarGridSpec(
            num_scalar_prefetch=3,
            grid=(blocks,),
            in_specs=[by_rows(width), keys, keys, by_rows(width), by_rows(LANES), by_rows(1), by_rows(1), cols],
            out_specs=[by_rows(width), keys, keys],
            scratch_shapes=[
                pltpu.VMEM((blocks, tile, width), F32),
                pltpu.VMEM((blocks, tile, width), F32),
                pltpu.VMEM((blocks, tile, tile), F32),
                pltpu.VMEM((blocks, tile, tile), F32),
            ],
        ),
        out_shape=[
            jax.ShapeDtypeStruct((rows, width), BF16),
            jax.ShapeDtypeStruct((blocks, tile, width), BF16),
            jax.ShapeDtypeStruct((blocks, tile, width), BF16),
        ],
        compiler_params=pltpu.CompilerParams(vmem_limit_bytes=VMEM_LIMIT),
        cost_estimate=pl.CostEstimate(
            flops=5 * rows * rows * width,
            transcendentals=rows * rows * width // HD // 2,
            bytes_accessed=14 * rows * width,
        ),
        name="attention_backward",
    )(
        *tables,
        q,
        k.reshape(blocks, tile, width),
        v.reshape(blocks, tile, width),
        grad,
        lse,
        pos[:, None],
        start[:, None],
        pos.reshape(blocks, 1, tile),
    )
    return dq, dk.reshape(rows, width), dv.reshape(rows, width)


def norm_back(values, scale, gain, grad):
    weighted = grad * gain
    inner = jnp.mean(weighted * values, axis=1, keepdims=True)
    return scale * weighted - values * (scale * scale * scale) * inner


def shards(
    inputs,
    cotangent,
    routed,
    doc_starts,
    router,
    attn_gain,
    qkv_weight,
    out_weight,
    mlp_gain,
    up_weight,
    down_weight,
):
    seqs = lax.axis_size("seq")
    fsdps = lax.axis_size("fsdp")
    me = lax.axis_index("seq")
    width = inputs.shape[2]
    tok_count = inputs.shape[1]
    own_windows = tok_count // WIN
    windows = routed.shape[1]
    tile = routed.shape[2]
    own_rows = own_windows * tile
    rows = windows * tile
    heads_width = width // seqs
    hidden = up_weight.shape[1]
    own_hidden = hidden // seqs

    order = jnp.arange(seqs, dtype=jnp.int32) ^ me
    window_of = (order[:, None] * own_windows + jnp.arange(own_windows, dtype=jnp.int32)).reshape(-1)
    stream_pos = jnp.arange(windows, dtype=jnp.int32)[:, None] * WIN + routed[0]
    pos = stream_pos[window_of].reshape(-1)
    starts = doc_starts[0]
    start = jnp.max(jnp.where(starts[None, :] <= pos[:, None], starts[None, :], 0), axis=1)
    first_window = start.reshape(windows, tile)[:, 0] // WIN
    place_of = jnp.zeros((windows,), jnp.int32).at[window_of].set(jnp.arange(windows, dtype=jnp.int32))
    tables = (window_of, place_of, first_window)

    own_routes = lax.dynamic_slice_in_dim(routed[0], me * own_windows, own_windows, 0)
    row_ids = ((jnp.arange(own_windows, dtype=jnp.int32) * WIN)[:, None] + own_routes).reshape(-1)
    stream_in = inputs[0]
    grad_in = cotangent[0]
    picked = jnp.concatenate([stream_in[row_ids], grad_in[row_ids]], axis=1)

    heads = lambda w: lax.dynamic_slice_in_dim(w, me * heads_width, heads_width, 1)
    qkv_own = jnp.concatenate(
        [heads(qkv_weight[:, i * width : (i + 1) * width]) for i in range(3)]
        + [
            jnp.stack([router, attn_gain, mlp_gain], axis=1),
            jnp.zeros((router.shape[0], LANES - 3), BF16),
        ],
        axis=1,
    )
    qkv_full = lax.all_gather(qkv_own, "fsdp", axis=0, tiled=True)
    w_qkv = qkv_full[:, : 3 * heads_width]
    vectors = qkv_full[:, 3 * heads_width : 3 * heads_width + 3].astype(F32).T
    router_w, gain_a, gain_m = vectors[0:1], vectors[1:2], vectors[2:3]
    w_out = lax.all_gather(out_weight, "fsdp", axis=0, tiled=True)
    w_up = lax.all_gather(
        lax.dynamic_slice_in_dim(up_weight, me * own_hidden, own_hidden, 1), "fsdp", axis=0, tiled=True
    )
    piece = hidden // (seqs * fsdps)
    down_piece = lax.dynamic_slice_in_dim(down_weight, me * piece, piece, 0)
    down_piece = lax.ppermute(
        down_piece,
        ("seq", "fsdp"),
        [(s * fsdps + f, f * seqs + s) for s in range(seqs) for f in range(fsdps)],
    )
    w_down = lax.all_gather(down_piece, "fsdp", axis=0, tiled=True)

    both = gather_blocks(picked, "seq")
    x_rows = jnp.concatenate([b[:, :width] for b in both], axis=0)
    g_rows = jnp.concatenate([b[:, width:] for b in both], axis=0).astype(F32)
    x_f = x_rows.astype(F32)
    rate = jax.nn.sigmoid(mm(x_rows, router_w.astype(BF16), NT))
    scale_a = lax.rsqrt(jnp.mean(x_f * x_f, axis=1, keepdims=True) + EPS)
    normal_a = (x_f * scale_a * gain_a).astype(BF16)
    proj = mm(normal_a, w_qkv, NN).astype(BF16)
    q, k, v = (proj[:, i * heads_width : (i + 1) * heads_width] for i in range(3))
    att_own, lse = attention_forward(tables, q, k, v, pos, start, tile)

    att_blocks = gather_blocks(att_own, "seq")
    out_blocks = [
        lax.dynamic_slice_in_dim(w_out, (me ^ b) * heads_width, heads_width, 0) for b in range(seqs)
    ]
    cut = lambda a, b: a[b * own_rows : (b + 1) * own_rows]
    att = jnp.concatenate(
        [
            jnp.concatenate([cut(blk, j ^ b) for j in range(seqs)], axis=0)
            for b, blk in enumerate(att_blocks)
        ],
        axis=1,
    )
    out_ordered = jnp.concatenate(out_blocks, axis=0)
    branch_a = mm(att, out_ordered, NN)
    middle = x_f + branch_a
    scale_m = lax.rsqrt(jnp.mean(middle * middle, axis=1, keepdims=True) + EPS)
    normal_m = (middle * scale_m * gain_m).astype(BF16)
    pre_act = mm(normal_m, w_up, NN)
    cdf = 0.5 * (1.0 + lax.erf(pre_act * (0.5**0.5)))
    activated = (pre_act * cdf).astype(BF16)
    slope = cdf + pre_act * (jnp.exp(-0.5 * pre_act * pre_act) * (2.0 * jnp.pi) ** -0.5)

    carried = rate * g_rows
    carried_b = carried.astype(BF16)
    grad_act = mm(carried_b, w_down, NT)
    grad_pre = (grad_act * slope).astype(BF16)
    grad_normal_m = scatter_blocks([mm(cut(grad_pre, b), w_up, NT) for b in range(seqs)], "seq")
    middle_o = cut(middle, 0)
    scale_mo = cut(scale_m, 0)
    grad_middle = norm_back(middle_o, scale_mo, gain_m, grad_normal_m)
    gain_m_part = jnp.sum(grad_normal_m * middle_o * scale_mo, axis=0)
    grad_a_own = (cut(carried, 0) + grad_middle).astype(BF16)
    grad_a = jnp.concatenate(gather_blocks(grad_a_own, "seq"), axis=0)
    grad_att = mm(grad_a, out_blocks[0], NT).astype(BF16)
    dq, dk, dv = attention_backward(tables, q, k, v, grad_att, lse, pos, start, tile)
    grad_proj = jnp.concatenate([dq, dk, dv], axis=1)
    grad_normal_a = scatter_blocks([mm(cut(grad_proj, b), w_qkv, NT) for b in range(seqs)], "seq")

    branch_f = scatter_blocks([mm(cut(activated, b), w_down, NN) for b in range(seqs)], "seq")

    x_o, g_o, rate_o, scale_ao = (cut(a, 0) for a in (x_f, g_rows, rate, scale_a))
    branch_sum = cut(branch_a, 0) + branch_f
    result = x_o + rate_o * branch_sum
    output = stream_in.at[row_ids].set(result.astype(BF16))
    grad_norm_x = norm_back(x_o, scale_ao, gain_a, grad_normal_a)
    gain_a_part = jnp.sum(grad_normal_a * x_o * scale_ao, axis=0)
    grad_logit = jnp.sum(g_o * branch_sum, axis=1, keepdims=True) * rate_o * (1.0 - rate_o)
    router_part = jnp.sum(x_o * grad_logit, axis=0)
    grad_picked = g_o + grad_middle + grad_norm_x + grad_logit * router_w
    input_grad = grad_in.at[row_ids].set(grad_picked.astype(BF16))

    def reduce_rows(parts):
        cols = parts.shape[1]
        per = width // (seqs * fsdps)
        parts = parts.reshape(seqs, fsdps, per, cols).transpose(1, 0, 2, 3)
        mine = lax.psum_scatter(parts.astype(BF16), "fsdp", scatter_dimension=0, tiled=False)
        return lax.all_to_all(mine, "seq", split_axis=0, concat_axis=0, tiled=True)

    down_sum = lax.psum_scatter(
        mm(activated, carried_b, TN).astype(BF16), "fsdp", scatter_dimension=0, tiled=True
    ).astype(F32)
    up_sum = reduce_rows(mm(normal_m, grad_pre, TN))
    up_sum = up_sum.transpose(1, 0, 2).reshape(-1, hidden).astype(F32)
    out_sum = lax.psum_scatter(
        mm(att_own, grad_a, TN).astype(BF16), "fsdp", scatter_dimension=0, tiled=True
    ).astype(F32)
    small = jnp.stack([router_part, gain_a_part, gain_m_part], axis=1)
    small = jnp.concatenate([small, jnp.zeros((width, LANES - 3), F32)], axis=1)
    qkv_sum = reduce_rows(jnp.concatenate([mm(normal_a, grad_proj, TN), small], axis=1))
    per = qkv_sum.shape[1]
    tiny = jnp.sum(qkv_sum[:, :, 3 * heads_width : 3 * heads_width + 3].astype(F32), axis=0)
    qkv_sum = qkv_sum[:, :, : 3 * heads_width].reshape(seqs, per, 3, heads_width)
    qkv_sum = qkv_sum.transpose(1, 2, 0, 3).reshape(per, 3 * width).astype(F32)
    return (
        output[None],
        input_grad[None],
        tiny[:, 0],
        tiny[:, 1],
        qkv_sum,
        out_sum,
        tiny[:, 2],
        up_sum,
        down_sum,
    )


def solution(mesh):
    return jax.shard_map(
        shards,
        mesh=mesh,
        in_specs=(
            P("fsdp", "seq", None),
            P("fsdp", "seq", None),
            P("fsdp", None, None),
            P("fsdp", None),
            P("fsdp"),
            P("fsdp"),
            P("fsdp", None),
            P("fsdp", None),
            P("fsdp"),
            P("fsdp", None),
            P("fsdp", None),
        ),
        out_specs=(
            P("fsdp", "seq", None),
            P("fsdp", "seq", None),
            P(("seq", "fsdp")),
            P(("seq", "fsdp")),
            P(("seq", "fsdp"), None),
            P(("seq", "fsdp"), None),
            P(("seq", "fsdp")),
            P(("seq", "fsdp"), None),
            P(("seq", "fsdp"), None),
        ),
        check_vma=False,
    )
```

```python
from functools import partial

import jax
import jax.numpy as jnp
from jax import lax
from jax.experimental import pallas as pl
from jax.experimental.pallas import tpu as pltpu
from jax.sharding import PartitionSpec as P

H = 16
HD = 64
WIN = 2048
EPS = 1e-05
NEG_FILL = -1e30
PAIR = 2 * HD
LANES = 128
BF16 = jnp.bfloat16
F32 = jnp.float32
VMEM_LIMIT = 48 * 1024 * 1024


def mm(a, b, dims):
    return lax.dot_general(a, b, (dims, ((), ())), preferred_element_type=F32)


NN = ((1,), (0,))
NT = ((1,), (1,))
TN = ((0,), (0,))


def flip(values, axis, bit):
    count = lax.axis_size(axis)
    return lax.ppermute(values, axis, [(j, j ^ bit) for j in range(count)])


def bits_down(count):
    bit = count // 2
    while bit:
        yield bit
        bit //= 2


def gather_blocks(own, axis):
    blocks = {0: own}
    for bit in bits_down(lax.axis_size(axis)):
        for key in list(blocks):
            blocks[key ^ bit] = flip(blocks[key], axis, bit)
    return [blocks[key] for key in sorted(blocks)]


def scatter_blocks(blocks, axis):
    parts = dict(enumerate(blocks))
    bit = 1
    while bit < lax.axis_size(axis):
        for key in [k for k in parts if k & bit]:
            got = flip(parts.pop(key).astype(BF16), axis, bit)
            parts[key ^ bit] = parts[key ^ bit] + got.astype(F32)
        bit *= 2
    return parts[0]


def after(values, *earlier):
    earlier = [e for e in earlier if e is not None]
    return lax.optimization_barrier((values, *earlier))[0] if earlier else values


def fsdp_sizes():
    count = lax.axis_size("fsdp")
    fast = 2 ** ((count.bit_length() - 1) // 2)
    return count // fast, fast


def gather_slow(own, *waits):
    slow, fast = fsdp_sizes()
    own_late = after(own, *waits)
    return [own_late] + [flip(own_late, "fsdp", k * fast) for k in range(1, slow)]


def gather_fast(held, joined):
    _, fast = fsdp_sizes()
    held = [jnp.stack(held)] if joined else [h[None] for h in held]
    return held + [flip(h, "fsdp", k) for k in range(1, fast) for h in held]


def order_rows_kernel(me_ref, *refs, fast):
    slow = refs[-1].shape[0] // fast
    done = 0
    for ref in refs[:-1]:
        for i in range(ref.shape[0]):
            block = lax.rem(done, slow) * fast + lax.div(done, slow)
            refs[-1][me_ref[0] ^ block] = ref[i]
            done += 1


def order_rows(pieces):
    slow, fast = fsdp_sizes()
    rows, cols = pieces[0].shape[1:]
    whole = lambda shape: pl.BlockSpec(shape, lambda i, *_: (0,) * len(shape))
    out = pl.pallas_call(
        partial(order_rows_kernel, fast=fast),
        grid_spec=pltpu.PrefetchScalarGridSpec(
            num_scalar_prefetch=1,
            grid=(1,),
            in_specs=[whole(p.shape) for p in pieces],
            out_specs=whole((slow * fast, rows, cols)),
        ),
        out_shape=jax.ShapeDtypeStruct((slow * fast, rows, cols), BF16),
        compiler_params=pltpu.CompilerParams(vmem_limit_bytes=VMEM_LIMIT),
        cost_estimate=pl.CostEstimate(
            flops=0, transcendentals=0, bytes_accessed=4 * slow * fast * rows * cols
        ),
        name="order_rows",
    )(lax.axis_index("fsdp")[None], *pieces)
    return out.reshape(-1, cols)


def low_bits(count):
    bit = 1
    while bit < count:
        yield bit
        bit *= 2


def reduce_blocks(send, keep, first, waits):
    bits = [first] + [b for b in low_bits(lax.axis_size("fsdp")) if b != first]
    total = None
    for i, bit in enumerate(bits):
        got = flip(send, "fsdp", bit)
        total = keep.astype(F32) + got.astype(F32)
        if bit != bits[-1]:
            send = after(total[1::2].astype(BF16), *waits[min(i, len(waits) - 1)])
            keep = total[0::2]
    return total[0]


def join_columns_kernel(me_ref, *refs, groups, span):
    count = len(refs) - (1 if span * groups == refs[0].shape[1] else 2)
    tail = 0.0
    for k in range(count):
        for g in range(groups):
            start = pl.multiple_of((g * count + (me_ref[0] ^ k)) * span, span)
            refs[count][:, pl.ds(start, span)] = refs[k][:, g * span : (g + 1) * span].astype(F32)
        if refs[count + 1 :]:
            tail = tail + refs[k][:, groups * span :].astype(F32)
    for ref in refs[count + 1 :]:
        ref[...] = tail


def exchange_columns(blocks, groups, span):
    count, rows, cols = blocks.shape
    got = [blocks[0]] + [flip(blocks[k].astype(BF16), "seq", k) for k in range(1, count)]
    if span % LANES:
        me = lax.axis_index("seq")
        joined = jnp.zeros((rows, groups, count, span), F32)
        for k in range(count):
            part = got[k].astype(F32).reshape(rows, groups, 1, span)
            joined = lax.dynamic_update_slice_in_dim(joined, part, me ^ k, axis=2)
        return (joined.reshape(rows, -1),)
    out_shape = [jax.ShapeDtypeStruct((rows, count * groups * span), F32)]
    if cols > groups * span:
        out_shape.append(jax.ShapeDtypeStruct((rows, cols - groups * span), F32))
    return pl.pallas_call(
        partial(join_columns_kernel, groups=groups, span=span),
        grid_spec=pltpu.PrefetchScalarGridSpec(
            num_scalar_prefetch=1,
            grid=(1,),
            in_specs=[pl.BlockSpec((rows, cols), lambda i, *_: (0, 0))] * count,
            out_specs=[pl.BlockSpec(o.shape, lambda i, *_: (0, 0)) for o in out_shape],
        ),
        out_shape=out_shape,
        compiler_params=pltpu.CompilerParams(vmem_limit_bytes=VMEM_LIMIT),
        name="join_columns",
    )(lax.axis_index("seq")[None], *got)


GRAD_TILE = 512


def store_blocks(product, tail, column, place_ref, per, fsdps, first, refs):
    whole = product.astype(BF16)
    cols = product.shape[1]
    pieces = product.shape[0] // per
    for t in range(pieces):
        piece = column * pieces + t
        block = lax.rem(piece, fsdps)
        part = lax.div(piece, fsdps) ^ place_ref[1]
        rows = slice(t * per, (t + 1) * per)

        def store(ref, slot):
            ref[slot, part, :, :cols] = whole[rows]
            if tail is not None:
                ref[slot, part, :, cols:] = tail[rows]

        if first is None:
            store(refs[0], block)
            continue
        block = block ^ place_ref[0]
        slot = lax.div(block, 2 * first) * first + lax.rem(block, first)
        sent = lax.rem(lax.div(block, first), 2)
        pl.when(sent == 1)(partial(store, refs[0], slot))
        pl.when(sent == 0)(partial(store, refs[1], slot))


def weight_grad_kernel(place_ref, a_ref, b_ref, *refs, per, fsdps, first, gain_lane, with_logits, tail_out):
    column = pl.program_id(0)
    product = mm(a_ref[...], b_ref[...], TN)
    refs = list(refs)
    tail = None
    if gain_lane is not None:
        w_ref, vec_ref, other_ref = refs[:3]
        refs = refs[3:]
        lane = lax.broadcasted_iota(jnp.int32, (product.shape[0], LANES), 1)
        gain = vec_ref[...].astype(F32)[:, gain_lane : gain_lane + 1]
        gain_grad = jnp.sum(product * w_ref[...].astype(F32), axis=1, keepdims=True) / gain
        tail = jnp.where(lane == gain_lane, gain_grad, 0.0) + other_ref[...]
    if with_logits:
        x_ref, logit_ref = refs[:2]
        refs = refs[2:]
        tail = tail + mm(x_ref[...], logit_ref[...], TN)
    if tail_out:
        refs.pop()[...] = tail
    tail = tail.astype(BF16) if with_logits else None
    store_blocks(product, tail, column, place_ref, per, fsdps, first, refs)


def weight_grad(place, a, b, parts, first, gain=None, logits=None):
    rows, total = a.shape
    cols = b.shape[1]
    fsdps = lax.axis_size("fsdp")
    per = total // (parts * fsdps)
    tile = min(GRAD_TILE, total)
    wide = cols + (LANES if logits is not None else 0)
    columns = lambda n: pl.BlockSpec((n, tile), lambda c, *_: (0, c))
    lines = lambda n, at=0: pl.BlockSpec((tile, n), lambda c, *_: (c, at))
    whole = lambda *dims: pl.BlockSpec(dims, lambda c, *_: (0,) * len(dims))
    args, in_specs = [a, b], [columns(rows), whole(rows, cols)]
    copies = 1 if first is None else 2
    block = (fsdps // copies, parts, per, wide)
    out_shape = [jax.ShapeDtypeStruct(block, BF16)] * copies
    out_specs = [whole(*block)] * copies
    lane = None
    if gain is not None:
        weight, vectors, at, lane, other = gain
        args += [weight, vectors, other]
        in_specs += [lines(cols), lines(LANES, at), lines(LANES)]
    tail_out = gain is not None and logits is None
    if tail_out:
        out_shape = out_shape + [jax.ShapeDtypeStruct((total, LANES), F32)]
        out_specs = out_specs + [lines(LANES)]
    if logits is not None:
        args += list(logits)
        in_specs += [columns(logits[0].shape[0]), whole(*logits[1].shape)]
    return pl.pallas_call(
        partial(
            weight_grad_kernel,
            per=per,
            fsdps=fsdps,
            first=first,
            gain_lane=lane,
            with_logits=logits is not None,
            tail_out=tail_out,
        ),
        grid_spec=pltpu.PrefetchScalarGridSpec(
            num_scalar_prefetch=1,
            grid=(total // tile,),
            in_specs=in_specs,
            out_specs=out_specs,
        ),
        out_shape=out_shape,
        compiler_params=pltpu.CompilerParams(vmem_limit_bytes=VMEM_LIMIT),
        cost_estimate=pl.CostEstimate(
            flops=2 * rows * total * cols,
            transcendentals=0,
            bytes_accessed=2 * (rows * total + rows * cols + total * wide),
        ),
        name="weight_grad",
    )(place, *args)


def hidden_grads_kernel(
    place_ref, act_ref, carried_ref, norm_ref, pre_ref, w_ref, vec_ref, both_ref, tail_ref, *, per, down_per, fsdps, gain_lane
):
    column = pl.program_id(0)
    down = mm(act_ref[...], carried_ref[...], TN).astype(BF16)
    for t in range(down.shape[0] // down_per):
        both_ref[column * (down.shape[0] // down_per) + t, 1] = down[t * down_per : (t + 1) * down_per]
    product = mm(norm_ref[...], pre_ref[...], TN)
    lane = lax.broadcasted_iota(jnp.int32, (product.shape[0], LANES), 1)
    gain = vec_ref[...].astype(F32)[:, gain_lane : gain_lane + 1]
    gain_grad = jnp.sum(product * w_ref[...].astype(F32), axis=1, keepdims=True) / gain
    tail_ref[...] = jnp.where(lane == gain_lane, gain_grad, 0.0)
    up = product.astype(BF16)
    pieces = product.shape[0] // per
    for t in range(pieces):
        piece = column * pieces + t
        part = lax.div(piece, fsdps) ^ place_ref[1]
        line = pl.multiple_of(part * per, per)
        both_ref[lax.rem(piece, fsdps), 0, pl.ds(line, per), :] = up[t * per : (t + 1) * per]


def hidden_grads(place, activated, carried_b, normal_m, grad_pre, w_up, vectors, at, lane):
    rows, total = activated.shape
    cols = carried_b.shape[1]
    fsdps = lax.axis_size("fsdp")
    seqs = lax.axis_size("seq")
    tile = min(GRAD_TILE, total)
    columns = pl.BlockSpec((rows, tile), lambda c, *_: (0, c))
    lines = lambda n, at=0: pl.BlockSpec((tile, n), lambda c, *_: (c, at))
    whole = lambda *dims: pl.BlockSpec(dims, lambda c, *_: (0,) * len(dims))
    both = (fsdps, 2, total // fsdps, cols)
    return pl.pallas_call(
        partial(
            hidden_grads_kernel,
            per=total // (seqs * fsdps),
            down_per=total // fsdps,
            fsdps=fsdps,
            gain_lane=lane,
        ),
        grid_spec=pltpu.PrefetchScalarGridSpec(
            num_scalar_prefetch=1,
            grid=(total // tile,),
            in_specs=[columns, whole(rows, cols), columns, whole(rows, cols), lines(cols), lines(LANES, at)],
            out_specs=[whole(*both), lines(LANES)],
        ),
        out_shape=[jax.ShapeDtypeStruct(both, BF16), jax.ShapeDtypeStruct((total, LANES), F32)],
        compiler_params=pltpu.CompilerParams(vmem_limit_bytes=VMEM_LIMIT),
        cost_estimate=pl.CostEstimate(
            flops=4 * rows * total * cols,
            transcendentals=0,
            bytes_accessed=4 * (rows * total + rows * cols + total * cols),
        ),
        name="hidden_grads",
    )(place, activated, carried_b, normal_m, grad_pre, w_up, vectors)


def order_out_kernel(place_ref, *refs):
    out_ref = refs[-1]
    group, seqs = out_ref.shape[1:3]
    for k in range(seqs):
        for block in range(refs[k].shape[0]):
            shard = place_ref[0] ^ block
            at = lax.div(shard, group) ^ place_ref[1]
            out_ref[at, lax.rem(shard, group), place_ref[1] ^ k] = refs[k][block]


def order_out(place, blocks):
    seqs = len(blocks)
    fsdps, per, width = blocks[0].shape
    full = (seqs, fsdps // seqs, seqs, per, width)
    whole = lambda shape: pl.BlockSpec(shape, lambda i, *_: (0,) * len(shape))
    out = pl.pallas_call(
        order_out_kernel,
        grid_spec=pltpu.PrefetchScalarGridSpec(
            num_scalar_prefetch=1,
            grid=(1,),
            in_specs=[whole(blocks[0].shape)] * seqs,
            out_specs=whole(full),
        ),
        out_shape=jax.ShapeDtypeStruct(full, BF16),
        compiler_params=pltpu.CompilerParams(vmem_limit_bytes=VMEM_LIMIT),
        cost_estimate=pl.CostEstimate(flops=0, transcendentals=0, bytes_accessed=4 * width * width),
        name="order_out",
    )(place, *blocks)
    return out.reshape(-1, width)


ROW_TILE = 512


def pick_rows_kernel(ids_ref, from_ref, to_ref, total):
    chunk = pl.program_id(0)
    ids = ids_ref[...] - chunk * ROW_TILE
    hit = ids == lax.broadcasted_iota(jnp.int32, (ids.shape[0], ROW_TILE), 1)
    found = mm(jnp.where(hit, 1.0, 0.0).astype(BF16), from_ref[...], NN)

    @pl.when(chunk == 0)
    def _():
        total[...] = found

    @pl.when(chunk > 0)
    def _():
        total[...] += found

    to_ref[...] = total[...].astype(BF16)


def pick_rows(source, ids):
    length, width = source.shape
    rows = ids.shape[0]
    return pl.pallas_call(
        pick_rows_kernel,
        grid=(length // ROW_TILE,),
        in_specs=[
            pl.BlockSpec((rows, 1), lambda c: (0, 0)),
            pl.BlockSpec((ROW_TILE, width), lambda c: (c, 0)),
        ],
        out_specs=pl.BlockSpec((rows, width), lambda c: (0, 0)),
        out_shape=jax.ShapeDtypeStruct((rows, width), BF16),
        scratch_shapes=[pltpu.VMEM((rows, width), F32)],
        compiler_params=pltpu.CompilerParams(vmem_limit_bytes=VMEM_LIMIT),
        cost_estimate=pl.CostEstimate(
            flops=2 * rows * length * width, transcendentals=0, bytes_accessed=2 * length * width
        ),
        name="pick_rows",
    )(ids[:, None], source)


def place_rows_kernel(ids_ref, new_ref, from_ref, to_ref):
    ids = ids_ref[...] - pl.program_id(0) * ROW_TILE
    hit = ids == lax.broadcasted_iota(jnp.int32, (ROW_TILE, ids.shape[1]), 0)
    ones = jnp.where(hit, 1.0, 0.0)
    routed = jnp.max(ones, axis=1, keepdims=True) > 0.0
    new = mm(ones.astype(BF16), new_ref[...], NN).astype(BF16)
    to_ref[...] = jnp.where(routed, new, from_ref[...])


def place_rows(source, ids, new):
    length, width = source.shape
    rows = ids.shape[0]
    tiles = pl.BlockSpec((ROW_TILE, width), lambda c: (c, 0))
    return pl.pallas_call(
        place_rows_kernel,
        grid=(length // ROW_TILE,),
        in_specs=[
            pl.BlockSpec((1, rows), lambda c: (0, 0)),
            pl.BlockSpec((rows, width), lambda c: (0, 0)),
            tiles,
        ],
        out_specs=tiles,
        out_shape=jax.ShapeDtypeStruct((length, width), BF16),
        compiler_params=pltpu.CompilerParams(vmem_limit_bytes=VMEM_LIMIT),
        cost_estimate=pl.CostEstimate(
            flops=2 * rows * length * width, transcendentals=0, bytes_accessed=4 * length * width
        ),
        name="place_rows",
    )(ids[None, :], new, source)


def half_lanes(values, half):
    lane = lax.broadcasted_iota(jnp.int32, values.shape, 1)
    keep = lane < HD if half == 0 else lane >= HD
    return jnp.where(keep, values, jnp.zeros_like(values))


def allowed_tile(keys_ref, where, pos_row, start_row):
    keys = keys_ref[where]
    return (keys <= pos_row) & (keys >= start_row)


def attention_forward_kernel(
    window_ref, place_ref, first_ref, q_ref, k_ref, v_ref, pos_ref, start_ref, keys_ref, o_ref, lse_ref
):
    block = pl.program_id(0)
    tile, width = q_ref.shape
    heads = width // HD
    pos_row, start_row = pos_ref[0], start_ref[0]
    last = window_ref[block]
    count = last - first_ref[block] + 1
    lanes = [slice(h // 2 * PAIR, (h // 2 + 1) * PAIR) for h in range(heads)]
    scale = jnp.asarray(HD**-0.5, BF16)
    queries = [half_lanes(q_ref[:, lanes[h]] * scale, h % 2) for h in range(heads)]

    def step(i, carry):
        where = place_ref[last - i]
        allowed = allowed_tile(keys_ref, where, pos_row, start_row)
        new = []
        for h, (top, total, acc) in enumerate(carry):
            scores = jnp.where(allowed, mm(k_ref[where, :, lanes[h]], queries[h], NT), NEG_FILL)
            new_top = jnp.maximum(top, jnp.max(scores, axis=0, keepdims=True))
            shrink = jnp.exp(top - new_top)
            exponent = jnp.exp(scores - new_top)
            total = total * shrink + jnp.sum(exponent, axis=0, keepdims=True)
            acc = acc * shrink + mm(v_ref[where, :, lanes[h]], exponent.astype(BF16), TN)
            new.append((new_top, total, acc))
        return tuple(new)

    empty = (jnp.full((1, tile), NEG_FILL, F32), jnp.zeros((1, tile), F32), jnp.zeros((PAIR, tile), F32))
    done = lax.fori_loop(0, count, step, (empty,) * heads)
    for h in range(0, heads, 2):
        pair = [acc * (1.0 / total) for _, total, acc in done[h : h + 2]]
        joined = jnp.concatenate([pair[0][:HD], pair[1][HD:]], axis=0)
        o_ref[:, lanes[h]] = joined.T.astype(BF16)
    row = lax.broadcasted_iota(jnp.int32, (8, tile), 0)
    lse = jnp.zeros((8, tile), F32)
    for h, (top, total, _) in enumerate(done):
        lse = jnp.where(row == h, top + jnp.log(total), lse)
    lse_ref[...] = lse


def attention_backward_kernel(
    window_ref,
    place_ref,
    first_ref,
    q_ref,
    k_ref,
    v_ref,
    g_ref,
    o_ref,
    lse_ref,
    pos_ref,
    start_ref,
    keys_ref,
    dq_ref,
    dkv_ref,
    dk_sum,
    dv_sum,
):
    block = pl.program_id(0)
    tile, width = q_ref.shape
    heads = width // HD
    pos_row, start_row = pos_ref[0], start_ref[0]
    last = window_ref[block]
    count = last - first_ref[block] + 1
    lanes = [slice(h // 2 * PAIR, (h // 2 + 1) * PAIR) for h in range(heads)]
    scale = HD**-0.5

    @pl.when(block == 0)
    def _():
        dk_sum[...] = jnp.zeros_like(dk_sum)
        dv_sum[...] = jnp.zeros_like(dv_sum)

    queries = [half_lanes(q_ref[:, lanes[h]] * jnp.asarray(scale, BF16), h % 2) for h in range(heads)]
    grads = [half_lanes(g_ref[:, lanes[h]], h % 2) for h in range(heads)]
    inner = []
    for h in range(0, heads, 2):
        both = (g_ref[:, lanes[h]].astype(F32) * o_ref[:, lanes[h]].astype(F32)).T
        inner += [jnp.sum(part, axis=0, keepdims=True) for part in (both[:HD], both[HD:])]

    def step(i, carry):
        where = place_ref[last - i]
        allowed = allowed_tile(keys_ref, where, pos_row, start_row)
        new = []
        for h, acc in enumerate(carry):
            keys = k_ref[where, :, lanes[h]]
            scores = mm(keys, queries[h], NT)
            prob = jnp.where(allowed, jnp.exp(scores - lse_ref[h : h + 1, :]), 0.0)
            grad_prob = mm(v_ref[where, :, lanes[h]], grads[h], NT)
            grad_scores = (prob * (grad_prob - inner[h])).astype(BF16)
            dv_sum[where, :, lanes[h]] += mm(prob.astype(BF16), grads[h], NN)
            dk_sum[where, :, lanes[h]] += mm(grad_scores, queries[h], NN)
            new.append(acc + mm(keys, grad_scores, TN))
        return tuple(new)

    done = lax.fori_loop(0, count, step, (jnp.zeros((PAIR, tile), F32),) * heads)
    for h in range(0, heads, 2):
        joined = jnp.concatenate([done[h][:HD], done[h + 1][HD:]], axis=0) * scale
        dq_ref[:, lanes[h]] = joined.T.astype(BF16)

    @pl.when(block == pl.num_programs(0) - 1)
    def _():
        dkv_ref[:, :, :width] = dk_sum[...].astype(BF16)
        dkv_ref[:, :, width:] = dv_sum[...].astype(BF16)


def attention_specs(blocks, tile, width):
    by_rows = pl.BlockSpec((tile, width), lambda b, *_: (b, 0))
    keys = lambda at: pl.BlockSpec((blocks, tile, width), lambda b, *_: (0, 0, at))
    row = pl.BlockSpec((1, 1, tile), lambda b, *_: (b, 0, 0))
    lse = pl.BlockSpec((8, tile), lambda b, *_: (0, b))
    return by_rows, keys, row, lse, pl.BlockSpec((blocks, tile, 1), lambda b, *_: (0, 0, 0))


def attention_forward(tables, q, kv, pos, start, tile):
    rows, width = q.shape
    blocks = rows // tile
    by_rows, keys, row, lse, cols = attention_specs(blocks, tile, width)
    return pl.pallas_call(
        attention_forward_kernel,
        grid_spec=pltpu.PrefetchScalarGridSpec(
            num_scalar_prefetch=3,
            grid=(blocks,),
            in_specs=[by_rows, keys(0), keys(1), row, row, cols],
            out_specs=[by_rows, lse],
        ),
        out_shape=[jax.ShapeDtypeStruct((rows, width), BF16), jax.ShapeDtypeStruct((8, rows), F32)],
        compiler_params=pltpu.CompilerParams(vmem_limit_bytes=VMEM_LIMIT),
        cost_estimate=pl.CostEstimate(
            flops=2 * rows * rows * width,
            transcendentals=rows * rows * width // HD // 2,
            bytes_accessed=8 * rows * width,
        ),
        name="attention_forward",
    )(
        *tables,
        q,
        kv.reshape(blocks, tile, 2 * width),
        kv.reshape(blocks, tile, 2 * width),
        pos.reshape(blocks, 1, tile),
        start.reshape(blocks, 1, tile),
        pos.reshape(blocks, tile, 1),
    )


def attention_backward(tables, q, kv, grad, out, lse_rows, pos, start, tile):
    rows, width = q.shape
    blocks = rows // tile
    by_rows, keys, row, lse, cols = attention_specs(blocks, tile, width)
    dq, dkv = pl.pallas_call(
        attention_backward_kernel,
        grid_spec=pltpu.PrefetchScalarGridSpec(
            num_scalar_prefetch=3,
            grid=(blocks,),
            in_specs=[by_rows, keys(0), keys(1), by_rows, by_rows, lse, row, row, cols],
            out_specs=[by_rows, pl.BlockSpec((blocks, tile, 2 * width), lambda b, *_: (0, 0, 0))],
            scratch_shapes=[pltpu.VMEM((blocks, tile, width), F32)] * 2,
        ),
        out_shape=[
            jax.ShapeDtypeStruct((rows, width), BF16),
            jax.ShapeDtypeStruct((blocks, tile, 2 * width), BF16),
        ],
        compiler_params=pltpu.CompilerParams(vmem_limit_bytes=VMEM_LIMIT),
        cost_estimate=pl.CostEstimate(
            flops=5 * rows * rows * width,
            transcendentals=rows * rows * width // HD // 2,
            bytes_accessed=14 * rows * width,
        ),
        name="attention_backward",
    )(
        *tables,
        q,
        kv.reshape(blocks, tile, 2 * width),
        kv.reshape(blocks, tile, 2 * width),
        grad,
        out,
        lse_rows,
        pos.reshape(blocks, 1, tile),
        start.reshape(blocks, 1, tile),
        pos.reshape(blocks, tile, 1),
    )
    return dq, dkv.reshape(rows, 2 * width)


def whole_spec(shape):
    return pl.BlockSpec(shape, lambda i, *_: (0,) * len(shape))


def one_step(kernel, name, place, args, out_shape, flops):
    size = lambda x: x.size * x.dtype.itemsize
    return pl.pallas_call(
        kernel,
        grid_spec=pltpu.PrefetchScalarGridSpec(
            num_scalar_prefetch=1,
            grid=(1,),
            in_specs=[whole_spec(x.shape) for x in args],
            out_specs=[whole_spec(x.shape) for x in out_shape],
        ),
        out_shape=out_shape,
        compiler_params=pltpu.CompilerParams(vmem_limit_bytes=VMEM_LIMIT),
        cost_estimate=pl.CostEstimate(
            flops=flops, transcendentals=0, bytes_accessed=sum(size(x) for x in (*args, *out_shape))
        ),
        name=name,
    )(place, *args)


def norm_scale(values):
    return lax.rsqrt(jnp.mean(values * values, axis=1, keepdims=True) + EPS)


def project_kernel(place_ref, *refs, seqs, slow, fast):
    x_refs, pieces = refs[:seqs], refs[seqs:-6]
    w_ref, vec_ref, normal_ref, q_ref, kv_ref, rate_ref = refs[-6:]
    per, cols = pieces[0].shape[1:]
    span = q_ref.shape[1]
    done = 0
    for ref in pieces:
        for i in range(ref.shape[0]):
            shard = place_ref[0] ^ (done % slow * fast + done // slow)
            w_ref[pl.ds(pl.multiple_of(shard * per, per), per), :] = ref[i]
            done += 1
    tails = w_ref[:, 3 * span :]
    vec = tails.astype(F32).T
    vec_ref[...] = vec[:8]
    gain = vec[1:2]
    weight = w_ref[:, : 3 * span]
    rows = x_refs[0].shape[0]
    for k in range(seqs):
        here = slice(k * rows, (k + 1) * rows)
        x = x_refs[k][...]
        x_f = x.astype(F32)
        normal = (x_f * norm_scale(x_f) * gain).astype(BF16)
        normal_ref[here, :] = normal
        proj = mm(normal, weight, NN).astype(BF16)
        kv_ref[here, :] = proj[:, : 2 * span]
        q_ref[here, :] = proj[:, 2 * span :]
        rate_ref[here, :] = jax.nn.sigmoid(mm(x, tails, NN)[:, :1])


def project(place, x_blocks, pieces, span):
    slow, fast = fsdp_sizes()
    rows, width = x_blocks[0].shape
    total = rows * len(x_blocks)
    cols = pieces[0].shape[2]
    out_shape = [
        jax.ShapeDtypeStruct((width, cols), BF16),
        jax.ShapeDtypeStruct((8, width), F32),
        jax.ShapeDtypeStruct((total, width), BF16),
        jax.ShapeDtypeStruct((total, span), BF16),
        jax.ShapeDtypeStruct((total, 2 * span), BF16),
        jax.ShapeDtypeStruct((total, 1), F32),
    ]
    kernel = partial(project_kernel, seqs=len(x_blocks), slow=slow, fast=fast)
    return one_step(
        kernel, "project", place, [*x_blocks, *pieces], out_shape, 2 * total * width * cols
    )


def branch_kernel(place_ref, *refs, seqs):
    x_refs, g_refs, att_refs = (refs[i * seqs : (i + 1) * seqs] for i in range(3))
    w_ref, vec_ref, rate_ref, branch_ref, normal_ref, carried_ref = refs[3 * seqs :]
    rows = x_refs[0].shape[0]
    span = att_refs[0].shape[1]
    gain = vec_ref[2:3, :]
    for j in range(seqs):
        here = slice(j * rows, (j + 1) * rows)
        branch = 0.0
        for b in range(seqs):
            there = slice((j ^ b) * rows, ((j ^ b) + 1) * rows)
            branch = branch + mm(att_refs[b][there, :], w_ref[b * span : (b + 1) * span, :], NN)
        if j == 0:
            branch_ref[...] = branch
        middle = x_refs[j][...].astype(F32) + branch
        normal_ref[here, :] = (middle * norm_scale(middle) * gain).astype(BF16)
        carried_ref[here, :] = (rate_ref[here, :] * g_refs[j][...].astype(F32)).astype(BF16)


def attention_branch(place, x_blocks, g_blocks, att_blocks, w_out, vectors, rate):
    rows, width = x_blocks[0].shape
    seqs = len(x_blocks)
    out_shape = [
        jax.ShapeDtypeStruct((rows, width), F32),
        jax.ShapeDtypeStruct((rows * seqs, width), BF16),
        jax.ShapeDtypeStruct((rows * seqs, width), BF16),
    ]
    args = [*x_blocks, *g_blocks, *att_blocks, w_out, vectors, rate]
    return one_step(
        partial(branch_kernel, seqs=seqs),
        "attention_branch",
        place,
        args,
        out_shape,
        2 * rows * seqs * width * width,
    )


def attention_grad_kernel(place_ref, *refs, seqs):
    w_ref, joined_ref, out_ref = refs[seqs:]
    rows = refs[0].shape[0]
    for j in range(seqs):
        here = slice(j * rows, (j + 1) * rows)
        block = refs[j][...]
        joined_ref[here, :] = block
        out_ref[here, :] = mm(block, w_ref[...], NT).astype(BF16)


def attention_grad(place, blocks, w_out):
    rows, width = blocks[0].shape
    total = rows * len(blocks)
    span = w_out.shape[0]
    out_shape = [jax.ShapeDtypeStruct((total, width), BF16), jax.ShapeDtypeStruct((total, span), BF16)]
    return one_step(
        partial(attention_grad_kernel, seqs=len(blocks)),
        "attention_grad",
        place,
        [*blocks, w_out],
        out_shape,
        2 * total * width * span,
    )


def norm_back(values, scale, gain, grad):
    weighted = grad * gain
    inner = jnp.mean(weighted * values, axis=1, keepdims=True)
    return scale * weighted - values * (scale * scale * scale) * inner


def shards(
    inputs,
    cotangent,
    routed,
    doc_starts,
    router,
    attn_gain,
    qkv_weight,
    out_weight,
    mlp_gain,
    up_weight,
    down_weight,
):
    seqs = lax.axis_size("seq")
    fsdps = lax.axis_size("fsdp")
    me = lax.axis_index("seq")
    width = inputs.shape[2]
    tok_count = inputs.shape[1]
    own_windows = tok_count // WIN
    windows = routed.shape[1]
    tile = routed.shape[2]
    own_rows = own_windows * tile
    rows = windows * tile
    heads_width = width // seqs
    hidden = up_weight.shape[1]
    own_hidden = hidden // seqs

    order = jnp.arange(seqs, dtype=jnp.int32) ^ me
    window_of = (order[:, None] * own_windows + jnp.arange(own_windows, dtype=jnp.int32)).reshape(-1)
    stream_pos = jnp.arange(windows, dtype=jnp.int32)[:, None] * WIN + routed[0]
    pos = stream_pos[window_of].reshape(-1)
    starts = doc_starts[0]
    start = jnp.max(jnp.where(starts[None, :] <= pos[:, None], starts[None, :], 0), axis=1)
    first_window = start.reshape(windows, tile)[:, 0] // WIN
    place_of = jnp.zeros((windows,), jnp.int32).at[window_of].set(jnp.arange(windows, dtype=jnp.int32))
    tables = (window_of, place_of, first_window)

    own_routes = lax.dynamic_slice_in_dim(routed[0], me * own_windows, own_windows, 0)
    row_ids = ((jnp.arange(own_windows, dtype=jnp.int32) * WIN)[:, None] + own_routes).reshape(-1)
    stream_in = inputs[0]
    grad_in = cotangent[0]

    place = jnp.stack([lax.axis_index("fsdp"), me])
    heads = lambda i: lax.dynamic_slice_in_dim(qkv_weight, i * width + me * heads_width, heads_width, 1)
    vectors = jnp.stack([router, attn_gain, mlp_gain], axis=1)
    tails = jnp.pad(vectors, ((0, 0), (0, LANES - vectors.shape[1])))
    qkv_own = jnp.concatenate([heads(1), heads(2), heads(0), tails], axis=1)
    qkv_slow = gather_slow(qkv_own)
    x_own = pick_rows(stream_in, after(row_ids, qkv_own))
    x_blocks = gather_blocks(x_own, "seq")

    span = down_weight.shape[0] // seqs
    up_late = after(up_weight, x_own)
    up_own = jnp.concatenate(
        [
            lax.dynamic_slice_in_dim(up_late, (i * seqs + me) * span, span, 1)
            for i in range(fsdps)
        ],
        axis=1,
    )
    down_own = lax.dynamic_slice_in_dim(down_weight, me * span, span, 0)
    square = own_hidden == width
    shard_rows = up_weight.shape[0]
    if square:
        hidden_own = jnp.concatenate([up_own, down_own], axis=0)
        up_own = hidden_own
        hidden_all = lax.all_gather(after(hidden_own, *qkv_slow[1:]), "fsdp", axis=0)
        w_up = hidden_all[:, :shard_rows].reshape(width, own_hidden)
        w_down = hidden_all[:, shard_rows:].reshape(own_hidden, width)
    else:
        w_up = lax.all_gather(up_own, "fsdp", axis=0, tiled=True)
        w_down = lax.all_gather(down_own, "fsdp", axis=0, tiled=True)

    out_piece = width // (seqs * fsdps)
    out_own = lax.dynamic_slice_in_dim(out_weight, me * out_piece, out_piece, 0)
    out_slow = gather_slow(out_own, *qkv_slow[1:])
    qkv_pieces = gather_fast([qkv_slow[0], *after(tuple(qkv_slow[1:]), up_own)], False)
    out_part = jnp.stack(gather_fast(out_slow, True), axis=1).reshape(fsdps, out_piece, width)

    w_qkv, vectors, normal_a, q, kv, rate = project(place, x_blocks, qkv_pieces, heads_width)
    router_w, gain_a, gain_m = vectors[0:1], vectors[1:2], vectors[2:3]
    w_kv = w_qkv[:, : 2 * heads_width]
    w_q = w_qkv[:, 2 * heads_width :]
    tail_at = heads_width // LANES
    out_blocks = gather_blocks(after(out_part, q), "seq")
    g_own = pick_rows(grad_in, after(row_ids, q))
    g_blocks = gather_blocks(g_own, "seq")
    att_own, lse = attention_forward(tables, q, kv, pos, start, tile)
    att_blocks = gather_blocks(att_own, "seq")
    out_ordered = order_out(place, out_blocks)
    w_out = out_ordered[:heads_width]
    branch_o, normal_m, carried_b = attention_branch(
        place, x_blocks, g_blocks, att_blocks, out_ordered, vectors, rate
    )
    pre_act = mm(normal_m, w_up, NN)
    cdf = 0.5 * (1.0 + lax.erf(pre_act * (0.5**0.5)))
    activated = (pre_act * cdf).astype(BF16)
    slope = cdf + pre_act * (jnp.exp(-0.5 * pre_act * pre_act) * (2.0 * jnp.pi) ** -0.5)

    grad_act = mm(carried_b, w_down, NT)
    grad_pre = (grad_act * slope).astype(BF16)
    cut = lambda a, b: a[b * own_rows : (b + 1) * own_rows]
    normal_grads = [mm(cut(grad_pre, b), w_up, NT) for b in range(seqs)]
    grad_normal_m = scatter_blocks(normal_grads, "seq")
    flat = place * jnp.array([1, 0], jnp.int32)
    scatter = lambda g: lax.psum_scatter(g, "fsdp", scatter_dimension=0)
    activated_late = after(activated, *normal_grads)
    if square:
        both, gains = hidden_grads(
            place, activated_late, carried_b, normal_m, grad_pre, w_up, w_q, tail_at, 2
        )
        grad_normal_m = after(grad_normal_m, both)
        both = scatter(both)
        up_part, down_part = both[0].reshape(seqs, -1, own_hidden), both[1]
    else:
        (down_grad,) = weight_grad(flat, activated_late, carried_b, 1, None)
        up_grad, gains = weight_grad(
            place,
            normal_m,
            grad_pre,
            seqs,
            None,
            (w_up, w_q, tail_at, 2, jnp.zeros((width, LANES), F32)),
        )
        up_part, down_part = scatter(up_grad), scatter(down_grad)[0]

    x_o = x_blocks[0].astype(F32)
    g_o = g_blocks[0].astype(F32)
    rate_o = cut(rate, 0)
    middle_o = x_o + branch_o
    grad_middle = norm_back(middle_o, norm_scale(middle_o), gain_m, grad_normal_m)
    grad_a_own = (rate_o * g_o + grad_middle).astype(BF16)
    grad_a_blocks = gather_blocks(grad_a_own, "seq")
    branch_parts = [mm(cut(after(activated, grad_a_own), b), w_down, NN) for b in range(seqs)]
    branch_f = scatter_blocks(branch_parts, "seq")
    grad_a, grad_att = attention_grad(place, grad_a_blocks, w_out)
    fast = 1
    slow = fsdp_sizes()[1]
    out_send, out_keep = weight_grad(flat, att_own, after(grad_a, *branch_parts), 1, fast)
    dq, dkv = attention_backward(
        tables, q, kv, after(grad_att, out_send), att_own, lse, pos, start, tile
    )
    kv_send, kv_keep, gains = weight_grad(
        place, normal_a, dkv, seqs, fast, (w_kv, w_q, tail_at, 1, gains)
    )
    branch_sum = branch_o + branch_f
    result = x_o + rate_o * branch_sum
    grad_logit = jnp.sum(g_o * branch_sum, axis=1, keepdims=True) * rate_o * (1.0 - rate_o)
    logit_high = grad_logit.astype(BF16)
    logit_low = (grad_logit - logit_high.astype(F32)).astype(BF16)
    lane = jnp.arange(LANES)[None, :]
    logits = jnp.where(lane == 0, logit_high, jnp.where(lane == 3, logit_low, jnp.zeros((), BF16)))
    q_send, q_keep = weight_grad(
        place, after(normal_a, kv_send), dq, seqs, slow, (w_q, w_q, tail_at, 1, gains), (x_own, logits)
    )
    out_sum = reduce_blocks(out_send, out_keep, fast, [(q_send,)])[0]
    kv_part = reduce_blocks(kv_send, kv_keep, fast, [()])
    q_part = reduce_blocks(q_send, q_keep, slow, [()])
    dq_late, dkv_late = after((dq, dkv), q_send)
    grad_normal_a = scatter_blocks(
        [
            mm(cut(dkv_late, b), w_kv, NT) + mm(cut(dq_late, b), w_q[:, :heads_width], NT)
            for b in range(seqs)
        ],
        "seq",
    )
    output = place_rows(stream_in, row_ids, after(result.astype(BF16), q_send))
    grad_norm_x = norm_back(x_o, norm_scale(x_o), gain_a, grad_normal_a)
    grad_picked = g_o + grad_middle + grad_norm_x + grad_logit * router_w
    input_grad = place_rows(grad_in, row_ids, grad_picked.astype(BF16))
    qkv_sum, tiny = exchange_columns(
        jnp.concatenate([q_part[:, :, :heads_width], kv_part, q_part[:, :, heads_width:]], axis=2),
        3,
        heads_width,
    )
    down_sum = lax.ppermute(
        down_part,
        ("seq", "fsdp"),
        [(s * fsdps + f, f * seqs + s) for s in range(seqs) for f in range(fsdps)],
    ).astype(F32)
    up_sum = exchange_columns(up_part, fsdps, span)[0]
    return (
        output[None],
        input_grad[None],
        tiny[:, 0] + tiny[:, 3],
        tiny[:, 1],
        qkv_sum,
        out_sum,
        tiny[:, 2],
        up_sum,
        down_sum,
    )


def solution(mesh):
    return jax.shard_map(
        shards,
        mesh=mesh,
        in_specs=(
            P("fsdp", "seq", None),
            P("fsdp", "seq", None),
            P("fsdp", None, None),
            P("fsdp", None),
            P("fsdp"),
            P("fsdp"),
            P("fsdp", None),
            P("fsdp", None),
            P("fsdp"),
            P("fsdp", None),
            P("fsdp", None),
        ),
        out_specs=(
            P("fsdp", "seq", None),
            P("fsdp", "seq", None),
            P(("seq", "fsdp")),
            P(("seq", "fsdp")),
            P(("seq", "fsdp"), None),
            P(("seq", "fsdp"), None),
            P(("seq", "fsdp")),
            P(("seq", "fsdp"), None),
            P(("seq", "fsdp"), None),
        ),
        check_vma=False,
    )
```

```python
from functools import partial

import jax
import jax.numpy as jnp
from jax import lax
from jax.experimental import pallas as pl
from jax.experimental.pallas import tpu as pltpu
from jax.sharding import PartitionSpec as P

H = 16
HD = 64
WIN = 2048
EPS = 1e-05
NEG_FILL = -1e30
PAIR = 2 * HD
LANES = 128
BF16 = jnp.bfloat16
F32 = jnp.float32
VMEM_LIMIT = 48 * 1024 * 1024


def mm(a, b, dims):
    return lax.dot_general(a, b, (dims, ((), ())), preferred_element_type=F32)


NN = ((1,), (0,))
NT = ((1,), (1,))
TN = ((0,), (0,))


def flip(values, axis, bit):
    count = lax.axis_size(axis)
    return lax.ppermute(values, axis, [(j, j ^ bit) for j in range(count)])


def bits_down(count):
    bit = count // 2
    while bit:
        yield bit
        bit //= 2


def gather_blocks(own, axis, *waits):
    blocks = {0: own}
    top = lax.axis_size(axis) // 2
    for bit in bits_down(lax.axis_size(axis)):
        for key in list(blocks):
            block = blocks[key] if bit == top else after(blocks[key], *waits)
            blocks[key ^ bit] = flip(block, axis, bit)
    return [blocks[key] for key in sorted(blocks)]


def scatter_blocks(blocks, axis, *waits):
    parts = dict(enumerate(blocks))
    bit = 1
    while bit < lax.axis_size(axis):
        for key in [k for k in parts if k & bit]:
            part = parts.pop(key).astype(BF16)
            got = flip(part if bit == 1 else after(part, *waits), axis, bit)
            parts[key ^ bit] = parts[key ^ bit] + got.astype(F32)
        bit *= 2
    return parts[0]


def after(values, *earlier):
    earlier = [e for e in earlier if e is not None]
    return lax.optimization_barrier((values, *earlier))[0] if earlier else values


def fsdp_sizes():
    count = lax.axis_size("fsdp")
    fast = 2 ** ((count.bit_length() - 1) // 2)
    return count // fast, fast


def gather_slow(own, *waits):
    slow, fast = fsdp_sizes()
    own_late = after(own, *waits)
    return [own_late] + [flip(own_late, "fsdp", k * fast) for k in range(1, slow)]


def own_fast(own):
    _, fast = fsdp_sizes()
    return [flip(own[None], "fsdp", k) for k in range(1, fast)]


def gather_fast(own, others, own_got):
    _, fast = fsdp_sizes()
    others = jnp.stack(others)
    pieces = [own[None], others]
    for k in range(1, fast):
        pieces += [own_got[k - 1], flip(others, "fsdp", k)]
    return pieces


def low_bits(count):
    bit = 1
    while bit < count:
        yield bit
        bit *= 2


def reduce_blocks(send, keep, first, waits):
    bits = [first] + [b for b in low_bits(lax.axis_size("fsdp")) if b != first]
    total = None
    for i, bit in enumerate(bits):
        got = flip(send, "fsdp", bit)
        total = keep.astype(F32) + got.astype(F32)
        if bit != bits[-1]:
            send = after(total[1::2].astype(BF16), *waits[min(i, len(waits) - 1)])
            keep = total[0::2]
    return total[0]


def join_columns_kernel(me_ref, *refs, up_span, span):
    up_ref, qkv_ref, tail_ref = refs[-3:]
    count = len(refs) - 3
    own_hidden = up_ref.shape[1] // count
    tail = 0.0
    for k in range(count):
        block = refs[k][...].astype(F32)
        at = me_ref[0] ^ k
        for ref, first, groups, cols in ((up_ref, 0, own_hidden // up_span, up_span), (qkv_ref, own_hidden, 3, span)):
            for g in range(groups):
                start = pl.multiple_of((g * count + at) * cols, cols)
                ref[:, pl.ds(start, cols)] = block[:, first + g * cols : first + (g + 1) * cols]
        tail = tail + block[:, own_hidden + 3 * span :]
    tail_ref[...] = tail


def exchange_columns(up, qkv, up_span, span):
    count, rows, own_hidden = up.shape
    both = jnp.concatenate([up.astype(BF16), qkv.astype(BF16)], axis=2)
    got = [both[0]] + [flip(both[k], "seq", k) for k in range(1, count)]
    shapes = [(rows, count * own_hidden), (rows, 3 * count * span), (rows, LANES)]
    if up_span % LANES:
        me = lax.axis_index("seq")
        groups = own_hidden // up_span
        joined = jnp.zeros((rows, groups, count, up_span), F32)
        for k in range(count):
            part = got[k][:, :own_hidden].astype(F32).reshape(rows, groups, 1, up_span)
            joined = lax.dynamic_update_slice_in_dim(joined, part, me ^ k, axis=2)
        alone = [g[:, own_hidden:] for g in got]
        zero = [jnp.concatenate([jnp.zeros((rows, LANES), BF16), a], axis=1) for a in alone]
        rest = join_columns(zero, [(rows, count * LANES), *shapes[1:]], LANES, span)
        return (joined.reshape(rows, -1), *rest[1:])
    return join_columns(got, shapes, up_span, span)


def join_columns(got, shapes, up_span, span):
    whole = lambda shape: pl.BlockSpec(shape, lambda i, *_: (0, 0))
    return pl.pallas_call(
        partial(join_columns_kernel, up_span=up_span, span=span),
        grid_spec=pltpu.PrefetchScalarGridSpec(
            num_scalar_prefetch=1,
            grid=(1,),
            in_specs=[whole(got[0].shape)] * len(got),
            out_specs=[whole(shape) for shape in shapes],
        ),
        out_shape=[jax.ShapeDtypeStruct(shape, F32) for shape in shapes],
        compiler_params=pltpu.CompilerParams(vmem_limit_bytes=VMEM_LIMIT),
        name="join_columns",
    )(lax.axis_index("seq")[None], *got)


GRAD_TILE = 512


def store_blocks(product, tail, column, place_ref, per, fsdps, first, refs):
    whole = product.astype(BF16)
    cols = product.shape[1]
    pieces = product.shape[0] // per
    for t in range(pieces):
        piece = column * pieces + t
        block = lax.rem(piece, fsdps)
        part = lax.div(piece, fsdps) ^ place_ref[1]
        rows = slice(t * per, (t + 1) * per)

        def store(ref, slot):
            ref[slot, part, :, :cols] = whole[rows]
            if tail is not None:
                ref[slot, part, :, cols:] = tail[rows]

        if first is None:
            store(refs[0], block)
            continue
        block = block ^ place_ref[0]
        slot = lax.div(block, 2 * first) * first + lax.rem(block, first)
        sent = lax.rem(lax.div(block, first), 2)
        pl.when(sent == 1)(partial(store, refs[0], slot))
        pl.when(sent == 0)(partial(store, refs[1], slot))


def weight_grad_kernel(place_ref, a_ref, b_ref, *refs, per, fsdps, first, gain_lane, with_logits, tail_out):
    column = pl.program_id(0)
    product = mm(a_ref[...], b_ref[...], TN)
    refs = list(refs)
    tail = None
    if gain_lane is not None:
        w_ref, vec_ref, other_ref = refs[:3]
        refs = refs[3:]
        lane = lax.broadcasted_iota(jnp.int32, (product.shape[0], LANES), 1)
        gain = vec_ref[...].astype(F32)[:, gain_lane : gain_lane + 1]
        gain_grad = jnp.sum(product * w_ref[...].astype(F32), axis=1, keepdims=True) / gain
        tail = jnp.where(lane == gain_lane, gain_grad, 0.0) + other_ref[...]
    if with_logits:
        x_ref, logit_ref = refs[:2]
        refs = refs[2:]
        tail = tail + mm(x_ref[...], logit_ref[...], TN)
    if tail_out:
        refs.pop()[...] = tail
    tail = tail.astype(BF16) if with_logits else None
    store_blocks(product, tail, column, place_ref, per, fsdps, first, refs)


def weight_grad(place, a, b, parts, first, gain=None, logits=None, cols=None, at_b=0):
    rows, total = a.shape
    cols = cols or b.shape[1]
    fsdps = lax.axis_size("fsdp")
    per = total // (parts * fsdps)
    tile = min(GRAD_TILE, total)
    wide = cols + (LANES if logits is not None else 0)
    columns = lambda n: pl.BlockSpec((n, tile), lambda c, *_: (0, c))
    lines = lambda n, at=0: pl.BlockSpec((tile, n), lambda c, *_: (c, at))
    whole = lambda *dims: pl.BlockSpec(dims, lambda c, *_: (0,) * len(dims))
    args, in_specs = [a, b], [columns(rows), pl.BlockSpec((rows, cols), lambda c, *_: (0, at_b))]
    copies = 1 if first is None else 2
    block = (fsdps // copies, parts, per, wide)
    out_shape = [jax.ShapeDtypeStruct(block, BF16)] * copies
    out_specs = [whole(*block)] * copies
    lane = None
    if gain is not None:
        weight, weight_at, vectors, at, lane, other = gain
        args += [weight, vectors, other]
        in_specs += [lines(cols, weight_at), lines(LANES, at), lines(LANES)]
    tail_out = gain is not None and logits is None
    if tail_out:
        out_shape = out_shape + [jax.ShapeDtypeStruct((total, LANES), F32)]
        out_specs = out_specs + [lines(LANES)]
    if logits is not None:
        args += list(logits)
        in_specs += [columns(logits[0].shape[0]), whole(*logits[1].shape)]
    return pl.pallas_call(
        partial(
            weight_grad_kernel,
            per=per,
            fsdps=fsdps,
            first=first,
            gain_lane=lane,
            with_logits=logits is not None,
            tail_out=tail_out,
        ),
        grid_spec=pltpu.PrefetchScalarGridSpec(
            num_scalar_prefetch=1,
            grid=(total // tile,),
            in_specs=in_specs,
            out_specs=out_specs,
        ),
        out_shape=out_shape,
        compiler_params=pltpu.CompilerParams(vmem_limit_bytes=VMEM_LIMIT),
        cost_estimate=pl.CostEstimate(
            flops=2 * rows * total * cols,
            transcendentals=0,
            bytes_accessed=2 * (rows * total + rows * cols + total * wide),
        ),
        name="weight_grad",
    )(place, *args)


def hidden_grads_kernel(
    place_ref, act_ref, carried_ref, norm_ref, pre_ref, w_ref, vec_ref, both_ref, tail_ref, *, per, down_per, fsdps, gain_lane
):
    column = pl.program_id(0)
    down = mm(act_ref[...], carried_ref[...], TN).astype(BF16)
    for t in range(down.shape[0] // down_per):
        both_ref[column * (down.shape[0] // down_per) + t, 1] = down[t * down_per : (t + 1) * down_per]
    product = mm(norm_ref[...], pre_ref[...], TN)
    lane = lax.broadcasted_iota(jnp.int32, (product.shape[0], LANES), 1)
    gain = vec_ref[...].astype(F32)[:, gain_lane : gain_lane + 1]
    gain_grad = jnp.sum(product * w_ref[...].astype(F32), axis=1, keepdims=True) / gain
    tail_ref[...] = jnp.where(lane == gain_lane, gain_grad, 0.0)
    up = product.astype(BF16)
    pieces = product.shape[0] // per
    for t in range(pieces):
        piece = column * pieces + t
        part = lax.div(piece, fsdps) ^ place_ref[1]
        line = pl.multiple_of(part * per, per)
        both_ref[lax.rem(piece, fsdps), 0, pl.ds(line, per), :] = up[t * per : (t + 1) * per]


def hidden_grads(place, activated, carried_b, normal_m, grad_pre, w_up, vectors, at, lane):
    rows, total = activated.shape
    cols = carried_b.shape[1]
    fsdps = lax.axis_size("fsdp")
    seqs = lax.axis_size("seq")
    tile = min(GRAD_TILE, total)
    columns = pl.BlockSpec((rows, tile), lambda c, *_: (0, c))
    lines = lambda n, at=0: pl.BlockSpec((tile, n), lambda c, *_: (c, at))
    whole = lambda *dims: pl.BlockSpec(dims, lambda c, *_: (0,) * len(dims))
    both = (fsdps, 2, total // fsdps, cols)
    return pl.pallas_call(
        partial(
            hidden_grads_kernel,
            per=total // (seqs * fsdps),
            down_per=total // fsdps,
            fsdps=fsdps,
            gain_lane=lane,
        ),
        grid_spec=pltpu.PrefetchScalarGridSpec(
            num_scalar_prefetch=1,
            grid=(total // tile,),
            in_specs=[columns, whole(rows, cols), columns, whole(rows, cols), lines(cols), lines(LANES, at)],
            out_specs=[whole(*both), lines(LANES)],
        ),
        out_shape=[jax.ShapeDtypeStruct(both, BF16), jax.ShapeDtypeStruct((total, LANES), F32)],
        compiler_params=pltpu.CompilerParams(vmem_limit_bytes=VMEM_LIMIT),
        cost_estimate=pl.CostEstimate(
            flops=4 * rows * total * cols,
            transcendentals=0,
            bytes_accessed=4 * (rows * total + rows * cols + total * cols),
        ),
        name="hidden_grads",
    )(place, activated, carried_b, normal_m, grad_pre, w_up, vectors)


def order_out_kernel(place_ref, *refs):
    out_ref = refs[-1]
    group, seqs = out_ref.shape[1:3]
    for k in range(seqs):
        for block in range(refs[k].shape[0]):
            shard = place_ref[0] ^ block
            at = lax.div(shard, group) ^ place_ref[1]
            out_ref[at, lax.rem(shard, group), place_ref[1] ^ k] = refs[k][block]


def order_out(place, blocks):
    seqs = len(blocks)
    fsdps, per, width = blocks[0].shape
    full = (seqs, fsdps // seqs, seqs, per, width)
    whole = lambda shape: pl.BlockSpec(shape, lambda i, *_: (0,) * len(shape))
    out = pl.pallas_call(
        order_out_kernel,
        grid_spec=pltpu.PrefetchScalarGridSpec(
            num_scalar_prefetch=1,
            grid=(1,),
            in_specs=[whole(blocks[0].shape)] * seqs,
            out_specs=whole(full),
        ),
        out_shape=jax.ShapeDtypeStruct(full, BF16),
        compiler_params=pltpu.CompilerParams(vmem_limit_bytes=VMEM_LIMIT),
        cost_estimate=pl.CostEstimate(flops=0, transcendentals=0, bytes_accessed=4 * width * width),
        name="order_out",
    )(place, *blocks)
    return out.reshape(-1, width)


ROW_TILE = 512


def pick_rows_kernel(ids_ref, from_ref, to_ref, total):
    chunk = pl.program_id(0)
    ids = ids_ref[...] - chunk * ROW_TILE
    hit = ids == lax.broadcasted_iota(jnp.int32, (ids.shape[0], ROW_TILE), 1)
    found = mm(jnp.where(hit, 1.0, 0.0).astype(BF16), from_ref[...], NN)

    @pl.when(chunk == 0)
    def _():
        total[...] = found

    @pl.when(chunk > 0)
    def _():
        total[...] += found

    to_ref[...] = total[...].astype(BF16)


def pick_rows(source, ids):
    length, width = source.shape
    rows = ids.shape[0]
    return pl.pallas_call(
        pick_rows_kernel,
        grid=(length // ROW_TILE,),
        in_specs=[
            pl.BlockSpec((rows, 1), lambda c: (0, 0)),
            pl.BlockSpec((ROW_TILE, width), lambda c: (c, 0)),
        ],
        out_specs=pl.BlockSpec((rows, width), lambda c: (0, 0)),
        out_shape=jax.ShapeDtypeStruct((rows, width), BF16),
        scratch_shapes=[pltpu.VMEM((rows, width), F32)],
        compiler_params=pltpu.CompilerParams(vmem_limit_bytes=VMEM_LIMIT),
        cost_estimate=pl.CostEstimate(
            flops=2 * rows * length * width, transcendentals=0, bytes_accessed=2 * length * width
        ),
        name="pick_rows",
    )(ids[:, None], source)


def place_rows_kernel(ids_ref, new_ref, from_ref, to_ref):
    ids = ids_ref[...] - pl.program_id(0) * ROW_TILE
    hit = ids == lax.broadcasted_iota(jnp.int32, (ROW_TILE, ids.shape[1]), 0)
    ones = jnp.where(hit, 1.0, 0.0)
    routed = jnp.max(ones, axis=1, keepdims=True) > 0.0
    new = mm(ones.astype(BF16), new_ref[...], NN).astype(BF16)
    to_ref[...] = jnp.where(routed, new, from_ref[...])


def place_rows(source, ids, new):
    length, width = source.shape
    rows = ids.shape[0]
    tiles = pl.BlockSpec((ROW_TILE, width), lambda c: (c, 0))
    return pl.pallas_call(
        place_rows_kernel,
        grid=(length // ROW_TILE,),
        in_specs=[
            pl.BlockSpec((1, rows), lambda c: (0, 0)),
            pl.BlockSpec((rows, width), lambda c: (0, 0)),
            tiles,
        ],
        out_specs=tiles,
        out_shape=jax.ShapeDtypeStruct((length, width), BF16),
        compiler_params=pltpu.CompilerParams(vmem_limit_bytes=VMEM_LIMIT),
        cost_estimate=pl.CostEstimate(
            flops=2 * rows * length * width, transcendentals=0, bytes_accessed=4 * length * width
        ),
        name="place_rows",
    )(ids[None, :], new, source)


def half_lanes(values, half):
    lane = lax.broadcasted_iota(jnp.int32, values.shape, 1)
    keep = lane < HD if half == 0 else lane >= HD
    return jnp.where(keep, values, jnp.zeros_like(values))


def allowed_tile(keys_ref, where, pos_row, start_row):
    keys = keys_ref[where]
    return (keys <= pos_row) & (keys >= start_row)


def attention_forward_kernel(
    window_ref, place_ref, first_ref, q_ref, k_ref, v_ref, pos_ref, start_ref, keys_ref, o_ref, lse_ref
):
    block = pl.program_id(0)
    tile, width = q_ref.shape
    heads = width // HD
    pos_row, start_row = pos_ref[0], start_ref[0]
    last = window_ref[block]
    count = last - first_ref[block] + 1
    lanes = [slice(h // 2 * PAIR, (h // 2 + 1) * PAIR) for h in range(heads)]
    scale = jnp.asarray(HD**-0.5, BF16)
    queries = [half_lanes(q_ref[:, lanes[h]] * scale, h % 2) for h in range(heads)]

    def step(i, carry):
        where = place_ref[last - i]
        allowed = allowed_tile(keys_ref, where, pos_row, start_row)
        each = range(heads)
        raw = [mm(k_ref[where, :, lanes[h]], queries[h], NT) for h in each]
        scores = [jnp.where(allowed, raw[h], NEG_FILL) for h in each]
        tops = [jnp.maximum(carry[h][0], jnp.max(scores[h], axis=0, keepdims=True)) for h in each]
        exponents = [jnp.exp(scores[h] - tops[h]) for h in each]
        values = [mm(v_ref[where, :, lanes[h]], exponents[h].astype(BF16), TN) for h in each]
        shrinks = [jnp.exp(carry[h][0] - tops[h]) for h in each]
        sums = [jnp.sum(exponents[h], axis=0, keepdims=True) for h in each]
        return tuple(
            (tops[h], carry[h][1] * shrinks[h] + sums[h], carry[h][2] * shrinks[h] + values[h])
            for h in each
        )

    empty = (jnp.full((1, tile), NEG_FILL, F32), jnp.zeros((1, tile), F32), jnp.zeros((PAIR, tile), F32))
    done = lax.fori_loop(0, count, step, (empty,) * heads)
    for h in range(0, heads, 2):
        pair = [acc * (1.0 / total) for _, total, acc in done[h : h + 2]]
        joined = jnp.concatenate([pair[0][:HD], pair[1][HD:]], axis=0)
        o_ref[:, lanes[h]] = joined.T.astype(BF16)
    row = lax.broadcasted_iota(jnp.int32, (8, tile), 0)
    lse = jnp.zeros((8, tile), F32)
    for h, (top, total, _) in enumerate(done):
        lse = jnp.where(row == h, top + jnp.log(total), lse)
    lse_ref[...] = lse


def attention_backward_kernel(
    window_ref,
    place_ref,
    first_ref,
    q_ref,
    k_ref,
    v_ref,
    g_ref,
    o_ref,
    lse_ref,
    pos_ref,
    start_ref,
    keys_ref,
    grad_ref,
    dk_sum,
    dv_sum,
):
    block = pl.program_id(0)
    tile, width = q_ref.shape
    heads = width // HD
    pos_row, start_row = pos_ref[0], start_ref[0]
    last = window_ref[block]
    count = last - first_ref[block] + 1
    lanes = [slice(h // 2 * PAIR, (h // 2 + 1) * PAIR) for h in range(heads)]
    scale = HD**-0.5

    @pl.when(block == 0)
    def _():
        dk_sum[...] = jnp.zeros_like(dk_sum)
        dv_sum[...] = jnp.zeros_like(dv_sum)

    queries = [half_lanes(q_ref[:, lanes[h]] * jnp.asarray(scale, BF16), h % 2) for h in range(heads)]
    grads = [half_lanes(g_ref[:, lanes[h]], h % 2) for h in range(heads)]
    inner = []
    for h in range(0, heads, 2):
        both = (g_ref[:, lanes[h]].astype(F32) * o_ref[:, lanes[h]].astype(F32)).T
        inner += [jnp.sum(part, axis=0, keepdims=True) for part in (both[:HD], both[HD:])]

    def step(i, carry):
        where = place_ref[last - i]
        allowed = allowed_tile(keys_ref, where, pos_row, start_row)
        each = range(heads)
        keys = [k_ref[where, :, lanes[h]] for h in each]
        scores = [mm(keys[h], queries[h], NT) for h in each]
        grad_prob = [mm(v_ref[where, :, lanes[h]], grads[h], NT) for h in each]
        prob = [jnp.where(allowed, jnp.exp(scores[h] - lse_ref[h : h + 1, :]), 0.0) for h in each]
        grad_scores = [(prob[h] * (grad_prob[h] - inner[h])).astype(BF16) for h in each]
        values = [mm(prob[h].astype(BF16), grads[h], NN) for h in each]
        moved = [mm(grad_scores[h], queries[h], NN) for h in each]
        for h in range(0, heads, 2):
            dv_sum[where, :, lanes[h]] += values[h] + values[h + 1]
            dk_sum[where, :, lanes[h]] += moved[h] + moved[h + 1]
        return tuple(carry[h] + mm(keys[h], grad_scores[h], TN) for h in each)

    done = lax.fori_loop(0, count, step, (jnp.zeros((PAIR, tile), F32),) * heads)
    for h in range(0, heads, 2):
        joined = jnp.concatenate([done[h][:HD], done[h + 1][HD:]], axis=0) * scale
        at = 2 * width + h * HD
        grad_ref[block, :, at : at + PAIR] = joined.T.astype(BF16)

    @pl.when(block == pl.num_programs(0) - 1)
    def _():
        grad_ref[:, :, :width] = dk_sum[...].astype(BF16)
        grad_ref[:, :, width : 2 * width] = dv_sum[...].astype(BF16)


def attention_specs(blocks, tile, width):
    by_rows = pl.BlockSpec((tile, width), lambda b, *_: (b, 0))
    keys = lambda at: pl.BlockSpec((blocks, tile, width), lambda b, *_: (0, 0, at))
    row = pl.BlockSpec((1, 1, tile), lambda b, *_: (b, 0, 0))
    lse = pl.BlockSpec((8, tile), lambda b, *_: (0, b))
    return by_rows, keys, row, lse, pl.BlockSpec((blocks, tile, 1), lambda b, *_: (0, 0, 0))


def attention_forward(tables, q, kv, pos, start, tile):
    rows, width = q.shape
    blocks = rows // tile
    by_rows, keys, row, lse, cols = attention_specs(blocks, tile, width)
    return pl.pallas_call(
        attention_forward_kernel,
        grid_spec=pltpu.PrefetchScalarGridSpec(
            num_scalar_prefetch=3,
            grid=(blocks,),
            in_specs=[by_rows, keys(0), keys(1), row, row, cols],
            out_specs=[by_rows, lse],
        ),
        out_shape=[jax.ShapeDtypeStruct((rows, width), BF16), jax.ShapeDtypeStruct((8, rows), F32)],
        compiler_params=pltpu.CompilerParams(vmem_limit_bytes=VMEM_LIMIT),
        cost_estimate=pl.CostEstimate(
            flops=2 * rows * rows * width,
            transcendentals=rows * rows * width // HD // 2,
            bytes_accessed=8 * rows * width,
        ),
        name="attention_forward",
    )(
        *tables,
        q,
        kv.reshape(blocks, tile, 2 * width),
        kv.reshape(blocks, tile, 2 * width),
        pos.reshape(blocks, 1, tile),
        start.reshape(blocks, 1, tile),
        pos.reshape(blocks, tile, 1),
    )


def attention_backward(tables, q, kv, grad, out, lse_rows, pos, start, tile):
    rows, width = q.shape
    blocks = rows // tile
    by_rows, keys, row, lse, cols = attention_specs(blocks, tile, width)
    grads = pl.pallas_call(
        attention_backward_kernel,
        grid_spec=pltpu.PrefetchScalarGridSpec(
            num_scalar_prefetch=3,
            grid=(blocks,),
            in_specs=[by_rows, keys(0), keys(1), by_rows, by_rows, lse, row, row, cols],
            out_specs=pl.BlockSpec((blocks, tile, 3 * width), lambda b, *_: (0, 0, 0)),
            scratch_shapes=[pltpu.VMEM((blocks, tile, width), F32)] * 2,
        ),
        out_shape=jax.ShapeDtypeStruct((blocks, tile, 3 * width), BF16),
        compiler_params=pltpu.CompilerParams(vmem_limit_bytes=VMEM_LIMIT),
        cost_estimate=pl.CostEstimate(
            flops=5 * rows * rows * width,
            transcendentals=rows * rows * width // HD // 2,
            bytes_accessed=14 * rows * width,
        ),
        name="attention_backward",
    )(
        *tables,
        q,
        kv.reshape(blocks, tile, 2 * width),
        kv.reshape(blocks, tile, 2 * width),
        grad,
        out,
        lse_rows,
        pos.reshape(blocks, 1, tile),
        start.reshape(blocks, 1, tile),
        pos.reshape(blocks, tile, 1),
    )
    return grads.reshape(rows, 3 * width)


def whole_spec(shape):
    return pl.BlockSpec(shape, lambda i, *_: (0,) * len(shape))


def one_step(kernel, name, place, args, out_shape, flops):
    size = lambda x: x.size * x.dtype.itemsize
    return pl.pallas_call(
        kernel,
        grid_spec=pltpu.PrefetchScalarGridSpec(
            num_scalar_prefetch=1,
            grid=(1,),
            in_specs=[whole_spec(x.shape) for x in args],
            out_specs=[whole_spec(x.shape) for x in out_shape],
        ),
        out_shape=out_shape,
        compiler_params=pltpu.CompilerParams(vmem_limit_bytes=VMEM_LIMIT),
        cost_estimate=pl.CostEstimate(
            flops=flops, transcendentals=0, bytes_accessed=sum(size(x) for x in (*args, *out_shape))
        ),
        name=name,
    )(place, *args)


def norm_scale(values):
    return lax.rsqrt(jnp.mean(values * values, axis=1, keepdims=True) + EPS)


def first_shard_kernel(place_ref, q_ref, k_ref, v_ref, tails_ref, out_ref, own_ref):
    span = q_ref.shape[1]
    for i, ref in enumerate((k_ref, v_ref, q_ref)):
        own_ref[:, i * span : (i + 1) * span] = ref[...]
    own_ref[:, 3 * span : 3 * span + LANES] = tails_ref[...]
    lines = out_ref.shape[1]
    for j in range(out_ref.shape[2] // span):
        own_ref[j * lines : (j + 1) * lines, 3 * span + LANES :] = out_ref[0, :, j * span : (j + 1) * span]


def first_shard(place, qkv, tails, out, span):
    rows, width = out.shape
    seqs = width // span
    out = out.reshape(seqs, rows // seqs, width)
    heads = lambda i: pl.BlockSpec((rows, span), lambda g, at: (0, i * seqs + at[1]))
    cols = 4 * span + LANES
    return pl.pallas_call(
        first_shard_kernel,
        grid_spec=pltpu.PrefetchScalarGridSpec(
            num_scalar_prefetch=1,
            grid=(1,),
            in_specs=[
                heads(0),
                heads(1),
                heads(2),
                pl.BlockSpec((rows, LANES), lambda g, at: (0, 0)),
                pl.BlockSpec((1, rows // seqs, width), lambda g, at: (at[1], 0, 0)),
            ],
            out_specs=pl.BlockSpec((rows, cols), lambda g, at: (0, 0)),
        ),
        out_shape=jax.ShapeDtypeStruct((rows, cols), BF16),
        compiler_params=pltpu.CompilerParams(vmem_limit_bytes=VMEM_LIMIT),
        cost_estimate=pl.CostEstimate(flops=0, transcendentals=0, bytes_accessed=4 * rows * cols),
        name="first_shard",
    )(place, qkv, qkv, qkv, tails, out)


def hidden_shard_kernel(place_ref, up_ref, down_ref, both_ref):
    rows = up_ref.shape[0]
    both_ref[:rows, :] = up_ref[...]
    both_ref[rows:, :] = down_ref[...]


def hidden_shard(place, up, down, span):
    rows, width = up.shape[0], down.shape[1]
    seqs = lax.axis_size("seq")
    return pl.pallas_call(
        hidden_shard_kernel,
        grid_spec=pltpu.PrefetchScalarGridSpec(
            num_scalar_prefetch=1,
            grid=(width // span,),
            in_specs=[
                pl.BlockSpec((rows, span), lambda i, at: (0, i * seqs + at[1])),
                pl.BlockSpec((span, span), lambda i, at: (at[1], i)),
            ],
            out_specs=pl.BlockSpec((rows + span, span), lambda i, at: (0, i)),
        ),
        out_shape=jax.ShapeDtypeStruct((rows + span, width), BF16),
        compiler_params=pltpu.CompilerParams(vmem_limit_bytes=VMEM_LIMIT),
        cost_estimate=pl.CostEstimate(flops=0, transcendentals=0, bytes_accessed=8 * rows * width),
        name="hidden_shard",
    )(place, up, down)


def project_kernel(place_ref, *refs, seqs, slow, fast):
    x_refs, pieces = refs[:seqs], refs[seqs:-7]
    out_ref, w_ref, vec_ref, normal_ref, q_ref, kv_ref, rate_ref = refs[-7:]
    per, cols = pieces[0].shape[1], w_ref.shape[1]
    span = q_ref.shape[1]
    lines = out_ref.shape[1]
    done = 0
    for ref in pieces:
        for i in range(ref.shape[0]):
            block = done % slow * fast + done // slow
            shard = place_ref[0] ^ block
            w_ref[pl.ds(pl.multiple_of(shard * per, per), per), :] = ref[i, :, :cols]
            for j in range(seqs):
                out_ref[block, :, j * span : (j + 1) * span] = ref[i, j * lines : (j + 1) * lines, cols:]
            done += 1
    tails = w_ref[:, 3 * span :]
    vec = tails.astype(F32).T
    vec_ref[...] = vec[:8]
    gain = vec[1:2]
    weight = w_ref[:, : 3 * span]
    rows = x_refs[0].shape[0]
    for k in range(seqs):
        here = slice(k * rows, (k + 1) * rows)
        x = x_refs[k][...]
        x_f = x.astype(F32)
        normal = (x_f * norm_scale(x_f) * gain).astype(BF16)
        normal_ref[here, :] = normal
        proj = mm(normal, weight, NN).astype(BF16)
        kv_ref[here, :] = proj[:, : 2 * span]
        q_ref[here, :] = proj[:, 2 * span :]
        rate_ref[here, :] = jax.nn.sigmoid(mm(x, tails, NN)[:, :1])


def project(place, x_blocks, pieces, span):
    slow, fast = fsdp_sizes()
    rows, width = x_blocks[0].shape
    total = rows * len(x_blocks)
    cols = pieces[0].shape[2] - span
    out_shape = [
        jax.ShapeDtypeStruct((slow * fast, width // (slow * fast * len(x_blocks)), width), BF16),
        jax.ShapeDtypeStruct((width, cols), BF16),
        jax.ShapeDtypeStruct((8, width), F32),
        jax.ShapeDtypeStruct((total, width), BF16),
        jax.ShapeDtypeStruct((total, span), BF16),
        jax.ShapeDtypeStruct((total, 2 * span), BF16),
        jax.ShapeDtypeStruct((total, 1), F32),
    ]
    kernel = partial(project_kernel, seqs=len(x_blocks), slow=slow, fast=fast)
    return one_step(
        kernel, "project", place, [*x_blocks, *pieces], out_shape, 2 * total * width * cols
    )


def branch_kernel(place_ref, *refs, seqs):
    x_refs, g_refs, att_refs = (refs[i * seqs : (i + 1) * seqs] for i in range(3))
    w_ref, vec_ref, rate_ref, branch_ref, normal_ref, carried_ref = refs[3 * seqs :]
    rows = x_refs[0].shape[0]
    span = att_refs[0].shape[1]
    gain = vec_ref[2:3, :]
    for j in range(seqs):
        here = slice(j * rows, (j + 1) * rows)
        branch = 0.0
        for b in range(seqs):
            there = slice((j ^ b) * rows, ((j ^ b) + 1) * rows)
            branch = branch + mm(att_refs[b][there, :], w_ref[b * span : (b + 1) * span, :], NN)
        if j == 0:
            branch_ref[...] = branch
        middle = x_refs[j][...].astype(F32) + branch
        normal_ref[here, :] = (middle * norm_scale(middle) * gain).astype(BF16)
        carried_ref[here, :] = (rate_ref[here, :] * g_refs[j][...].astype(F32)).astype(BF16)


def attention_branch(place, x_blocks, g_blocks, att_blocks, w_out, vectors, rate):
    rows, width = x_blocks[0].shape
    seqs = len(x_blocks)
    out_shape = [
        jax.ShapeDtypeStruct((rows, width), F32),
        jax.ShapeDtypeStruct((rows * seqs, width), BF16),
        jax.ShapeDtypeStruct((rows * seqs, width), BF16),
    ]
    args = [*x_blocks, *g_blocks, *att_blocks, w_out, vectors, rate]
    return one_step(
        partial(branch_kernel, seqs=seqs),
        "attention_branch",
        place,
        args,
        out_shape,
        2 * rows * seqs * width * width,
    )


def attention_grad_kernel(place_ref, *refs, seqs):
    w_ref, joined_ref, out_ref = refs[seqs:]
    rows = refs[0].shape[0]
    for j in range(seqs):
        here = slice(j * rows, (j + 1) * rows)
        block = refs[j][...]
        joined_ref[here, :] = block
        out_ref[here, :] = mm(block, w_ref[...], NT).astype(BF16)


def attention_grad(place, blocks, w_out):
    rows, width = blocks[0].shape
    total = rows * len(blocks)
    span = w_out.shape[0]
    out_shape = [jax.ShapeDtypeStruct((total, width), BF16), jax.ShapeDtypeStruct((total, span), BF16)]
    return one_step(
        partial(attention_grad_kernel, seqs=len(blocks)),
        "attention_grad",
        place,
        [*blocks, w_out],
        out_shape,
        2 * total * width * span,
    )


def norm_back(values, scale, gain, grad):
    weighted = grad * gain
    inner = jnp.mean(weighted * values, axis=1, keepdims=True)
    return scale * weighted - values * (scale * scale * scale) * inner


def shards(
    inputs,
    cotangent,
    routed,
    doc_starts,
    router,
    attn_gain,
    qkv_weight,
    out_weight,
    mlp_gain,
    up_weight,
    down_weight,
):
    seqs = lax.axis_size("seq")
    fsdps = lax.axis_size("fsdp")
    me = lax.axis_index("seq")
    width = inputs.shape[2]
    tok_count = inputs.shape[1]
    own_windows = tok_count // WIN
    windows = routed.shape[1]
    tile = routed.shape[2]
    own_rows = own_windows * tile
    rows = windows * tile
    heads_width = width // seqs
    hidden = up_weight.shape[1]
    own_hidden = hidden // seqs

    order = jnp.arange(seqs, dtype=jnp.int32) ^ me
    window_of = (order[:, None] * own_windows + jnp.arange(own_windows, dtype=jnp.int32)).reshape(-1)
    stream_pos = jnp.arange(windows, dtype=jnp.int32)[:, None] * WIN + routed[0]
    pos = stream_pos[window_of].reshape(-1)
    starts = doc_starts[0]
    start = jnp.max(jnp.where(starts[None, :] <= pos[:, None], starts[None, :], 0), axis=1)
    first_window = start.reshape(windows, tile)[:, 0] // WIN
    place_of = jnp.zeros((windows,), jnp.int32).at[window_of].set(jnp.arange(windows, dtype=jnp.int32))
    tables = (window_of, place_of, first_window)

    own_routes = lax.dynamic_slice_in_dim(routed[0], me * own_windows, own_windows, 0)
    row_ids = ((jnp.arange(own_windows, dtype=jnp.int32) * WIN)[:, None] + own_routes).reshape(-1)
    stream_in = inputs[0]
    grad_in = cotangent[0]

    place = jnp.stack([lax.axis_index("fsdp"), me])
    vectors = jnp.stack([router, attn_gain, mlp_gain], axis=1)
    tails = jnp.pad(vectors, ((0, 0), (0, LANES - vectors.shape[1])))
    first_own = first_shard(place, qkv_weight, tails, out_weight, heads_width)
    first_slow = gather_slow(first_own)
    first_got = own_fast(first_slow[0])
    x_own = pick_rows(stream_in, after(row_ids, first_own))
    x_blocks = gather_blocks(x_own, "seq")

    span = down_weight.shape[0] // seqs
    square = own_hidden == width and span % LANES == 0
    shard_rows = up_weight.shape[0]
    if square:
        hidden_own = hidden_shard(place, after(up_weight, x_own, *first_got), down_weight, span)
        hidden_late = after(hidden_own, *first_slow[1:])
        hidden_all = lax.all_gather(hidden_late, "fsdp", axis=0)
        w_up = hidden_all[:, :shard_rows].reshape(width, own_hidden)
        w_down = hidden_all[:, shard_rows:].reshape(own_hidden, width)
    else:
        hidden_own = lax.dynamic_index_in_dim(
            up_weight.reshape(-1, fsdps, seqs, span), me, axis=2, keepdims=False
        ).reshape(-1, own_hidden)
        down_own = lax.dynamic_slice_in_dim(down_weight, me * span, span, 0)
        w_up = lax.all_gather(hidden_own, "fsdp", axis=0, tiled=True)
        w_down = lax.all_gather(down_own, "fsdp", axis=0, tiled=True)
    first_pieces = gather_fast(first_slow[0], after(tuple(first_slow[1:]), hidden_own), first_got)
    g_own = pick_rows(grad_in, after(row_ids, x_blocks[seqs // 2]))
    g_blocks = gather_blocks(g_own, "seq")
    out_part, w_qkv, vectors, normal_a, q, kv, rate = project(
        place, x_blocks, first_pieces, heads_width
    )
    router_w, gain_a, gain_m = vectors[0:1], vectors[1:2], vectors[2:3]
    tail_at = 3 * heads_width // LANES
    att_own, lse = attention_forward(tables, q, kv, pos, start, tile)
    out_blocks = gather_blocks(out_part, "seq", att_own)
    out_ordered = order_out(place, out_blocks)
    att_blocks = gather_blocks(att_own, "seq", out_ordered)
    w_out = out_ordered[:heads_width]
    branch_o, normal_m, carried_b = attention_branch(
        place, x_blocks, g_blocks, att_blocks, out_ordered, vectors, rate
    )
    pre_act = mm(normal_m, w_up, NN)
    cdf = 0.5 * (1.0 + lax.erf(pre_act * (0.5**0.5)))
    activated = (pre_act * cdf).astype(BF16)
    slope = cdf + pre_act * (jnp.exp(-0.5 * pre_act * pre_act) * (2.0 * jnp.pi) ** -0.5)

    grad_act = mm(carried_b, w_down, NT)
    grad_pre = (grad_act * slope).astype(BF16)
    cut = lambda a, b: a[b * own_rows : (b + 1) * own_rows]
    normal_grads = [mm(cut(grad_pre, b), w_up, NT) for b in range(seqs)]
    grad_normal_m = scatter_blocks(normal_grads, "seq")
    flat = place * jnp.array([1, 0], jnp.int32)
    scatter = lambda g: lax.psum_scatter(g, "fsdp", scatter_dimension=0)
    activated_late = after(activated, *normal_grads)
    if square:
        both, gains = hidden_grads(
            place, activated_late, carried_b, normal_m, grad_pre, w_up, w_qkv, tail_at, 2
        )
        grad_normal_m = after(grad_normal_m, both)
        both = scatter(both)
        up_part, down_part = both[0].reshape(seqs, -1, own_hidden), both[1]
    else:
        (down_grad,) = weight_grad(flat, activated_late, carried_b, 1, None)
        up_grad, gains = weight_grad(
            place,
            normal_m,
            grad_pre,
            seqs,
            None,
            (w_up, 0, w_qkv, tail_at, 2, jnp.zeros((width, LANES), F32)),
        )
        up_part, down_part = scatter(up_grad), scatter(down_grad)[0]

    x_o = x_blocks[0].astype(F32)
    g_o = g_blocks[0].astype(F32)
    rate_o = cut(rate, 0)
    middle_o = x_o + branch_o
    grad_middle = norm_back(middle_o, norm_scale(middle_o), gain_m, grad_normal_m)
    grad_a_own = (rate_o * g_o + grad_middle).astype(BF16)
    grad_a_blocks = gather_blocks(grad_a_own, "seq")
    branch_parts = [mm(cut(after(activated, grad_a_blocks[1]), b), w_down, NN) for b in range(seqs)]
    branch_f = scatter_blocks(branch_parts, "seq", grad_a_blocks[-1])
    grad_a, grad_att = attention_grad(place, grad_a_blocks, w_out)
    fast = 1
    slow = fsdp_sizes()[1]
    out_send, out_keep = weight_grad(flat, att_own, after(grad_a, *branch_parts), 1, fast)
    grad_proj = attention_backward(
        tables, q, kv, after(grad_att, out_send), att_own, lse, pos, start, tile
    )
    kv_send, kv_keep, gains = weight_grad(
        place,
        normal_a,
        grad_proj,
        seqs,
        fast,
        (w_qkv, 0, w_qkv, tail_at, 1, gains),
        cols=2 * heads_width,
    )
    branch_sum = branch_o + branch_f
    result = x_o + rate_o * branch_sum
    grad_logit = jnp.sum(g_o * branch_sum, axis=1, keepdims=True) * rate_o * (1.0 - rate_o)
    logit_high = grad_logit.astype(BF16)
    logit_low = (grad_logit - logit_high.astype(F32)).astype(BF16)
    lane = jnp.arange(LANES)[None, :]
    logits = jnp.where(lane == 0, logit_high, jnp.where(lane == 3, logit_low, jnp.zeros((), BF16)))
    q_send, q_keep = weight_grad(
        place,
        after(normal_a, kv_send),
        grad_proj,
        seqs,
        slow,
        (w_qkv, 2, w_qkv, tail_at, 1, gains),
        (x_own, logits),
        cols=heads_width,
        at_b=2,
    )
    out_sum = reduce_blocks(out_send, out_keep, fast, [(q_send,)])[0]
    kv_part = reduce_blocks(kv_send, kv_keep, fast, [()])
    q_part = reduce_blocks(q_send, q_keep, slow, [()])
    proj_late = after(grad_proj, q_send)
    w_proj = w_qkv[:, : 3 * heads_width]
    grad_normal_a = scatter_blocks([mm(cut(proj_late, b), w_proj, NT) for b in range(seqs)], "seq")
    output = place_rows(stream_in, row_ids, after(result.astype(BF16), q_send))
    grad_norm_x = norm_back(x_o, norm_scale(x_o), gain_a, grad_normal_a)
    grad_picked = g_o + grad_middle + grad_norm_x + grad_logit * router_w
    input_grad = place_rows(grad_in, row_ids, grad_picked.astype(BF16))
    down_sum = lax.ppermute(
        down_part,
        ("seq", "fsdp"),
        [(s * fsdps + f, f * seqs + s) for s in range(seqs) for f in range(fsdps)],
    ).astype(F32)
    qkv_part = jnp.concatenate(
        [q_part[:, :, :heads_width], kv_part, q_part[:, :, heads_width:]], axis=2
    )
    up_sum, qkv_sum, tiny = exchange_columns(up_part, qkv_part, span, heads_width)
    return (
        output[None],
        input_grad[None],
        tiny[:, 0] + tiny[:, 3],
        tiny[:, 1],
        qkv_sum,
        out_sum,
        tiny[:, 2],
        up_sum,
        down_sum,
    )


def solution(mesh):
    return jax.shard_map(
        shards,
        mesh=mesh,
        in_specs=(
            P("fsdp", "seq", None),
            P("fsdp", "seq", None),
            P("fsdp", None, None),
            P("fsdp", None),
            P("fsdp"),
            P("fsdp"),
            P("fsdp", None),
            P("fsdp", None),
            P("fsdp"),
            P("fsdp", None),
            P("fsdp", None),
        ),
        out_specs=(
            P("fsdp", "seq", None),
            P("fsdp", "seq", None),
            P(("seq", "fsdp")),
            P(("seq", "fsdp")),
            P(("seq", "fsdp"), None),
            P(("seq", "fsdp"), None),
            P(("seq", "fsdp")),
            P(("seq", "fsdp"), None),
            P(("seq", "fsdp"), None),
        ),
        check_vma=False,
    )
```

```python
from functools import partial

import jax
import jax.numpy as jnp
from jax import lax
from jax.experimental import pallas as pl
from jax.experimental.pallas import tpu as pltpu
from jax.sharding import PartitionSpec as P

H = 16
HD = 64
WIN = 2048
EPS = 1e-05
NEG_FILL = -1e30
PAIR = 2 * HD
LANES = 128
BF16 = jnp.bfloat16
F32 = jnp.float32
VMEM_LIMIT = 48 * 1024 * 1024


def mm(a, b, dims):
    return lax.dot_general(a, b, (dims, ((), ())), preferred_element_type=F32)


NN = ((1,), (0,))
NT = ((1,), (1,))
TN = ((0,), (0,))


def flip(values, axis, bit):
    count = lax.axis_size(axis)
    return lax.ppermute(values, axis, [(j, j ^ bit) for j in range(count)])


def bits_down(count):
    bit = count // 2
    while bit:
        yield bit
        bit //= 2


def gather_blocks(own, axis, *waits):
    blocks = {0: own}
    top = lax.axis_size(axis) // 2
    for bit in bits_down(lax.axis_size(axis)):
        for key in list(blocks):
            block = after(blocks[key], *waits) if key else blocks[key]
            blocks[key ^ bit] = flip(block, axis, bit)
    return [blocks[key] for key in sorted(blocks)]


def scatter_blocks(blocks, axis, *waits):
    parts = dict(enumerate(blocks))
    bit = 1
    while bit < lax.axis_size(axis):
        for key in [k for k in parts if k & bit]:
            part = parts.pop(key).astype(BF16)
            got = flip(part if bit == 1 else after(part, *waits), axis, bit)
            parts[key ^ bit] = parts[key ^ bit] + got.astype(F32)
        bit *= 2
    return parts[0]


def after(values, *earlier):
    earlier = [e for e in earlier if e is not None]
    return lax.optimization_barrier((values, *earlier))[0] if earlier else values


def fsdp_sizes():
    count = lax.axis_size("fsdp")
    fast = 2 ** ((count.bit_length() - 1) // 2)
    return count // fast, fast


def gather_slow(own, *waits):
    slow, fast = fsdp_sizes()
    own_late = after(own, *waits)
    return [own_late] + [flip(own_late, "fsdp", k * fast) for k in range(1, slow)]


def own_fast(own):
    _, fast = fsdp_sizes()
    return [flip(own[None], "fsdp", k) for k in range(1, fast)]


def gather_fast(own, others, own_got):
    _, fast = fsdp_sizes()
    others = jnp.stack(others)
    pieces = [own[None], others]
    for k in range(1, fast):
        pieces += [own_got[k - 1], flip(others, "fsdp", k)]
    return pieces


def low_bits(count):
    bit = 1
    while bit < count:
        yield bit
        bit *= 2


def reduce_blocks(send, keep, first, waits):
    bits = [first] + [b for b in low_bits(lax.axis_size("fsdp")) if b != first]
    total = None
    for i, bit in enumerate(bits):
        got = flip(send, "fsdp", bit)
        total = keep.astype(F32) + got.astype(F32)
        if bit != bits[-1]:
            send = after(total[1::2].astype(BF16), *waits[min(i, len(waits) - 1)])
            keep = total[0::2]
    return total[0]


def join_columns_kernel(me_ref, *refs, up_span, span):
    up_ref, qkv_ref, tail_ref = refs[-3:]
    count = len(refs) - 3
    own_hidden = up_ref.shape[1] // count
    tail = 0.0
    for k in range(count):
        block = refs[k][...].astype(F32)
        at = me_ref[0] ^ k
        for ref, first, groups, cols in ((up_ref, 0, own_hidden // up_span, up_span), (qkv_ref, own_hidden, 3, span)):
            for g in range(groups):
                start = pl.multiple_of((g * count + at) * cols, cols)
                ref[:, pl.ds(start, cols)] = block[:, first + g * cols : first + (g + 1) * cols]
        tail = tail + block[:, own_hidden + 3 * span :]
    tail_ref[...] = tail


def exchange_columns(up, qkv, up_span, span):
    count, rows, own_hidden = up.shape
    both = jnp.concatenate([up.astype(BF16), qkv.astype(BF16)], axis=2)
    got = [both[0]] + [flip(both[k], "seq", k) for k in range(1, count)]
    shapes = [(rows, count * own_hidden), (rows, 3 * count * span), (rows, LANES)]
    if up_span % LANES:
        me = lax.axis_index("seq")
        groups = own_hidden // up_span
        joined = jnp.zeros((rows, groups, count, up_span), F32)
        for k in range(count):
            part = got[k][:, :own_hidden].astype(F32).reshape(rows, groups, 1, up_span)
            joined = lax.dynamic_update_slice_in_dim(joined, part, me ^ k, axis=2)
        alone = [g[:, own_hidden:] for g in got]
        zero = [jnp.concatenate([jnp.zeros((rows, LANES), BF16), a], axis=1) for a in alone]
        rest = join_columns(zero, [(rows, count * LANES), *shapes[1:]], LANES, span)
        return (joined.reshape(rows, -1), *rest[1:])
    return join_columns(got, shapes, up_span, span)


def join_columns(got, shapes, up_span, span):
    whole = lambda shape: pl.BlockSpec(shape, lambda i, *_: (0, 0))
    return pl.pallas_call(
        partial(join_columns_kernel, up_span=up_span, span=span),
        grid_spec=pltpu.PrefetchScalarGridSpec(
            num_scalar_prefetch=1,
            grid=(1,),
            in_specs=[whole(got[0].shape)] * len(got),
            out_specs=[whole(shape) for shape in shapes],
        ),
        out_shape=[jax.ShapeDtypeStruct(shape, F32) for shape in shapes],
        compiler_params=pltpu.CompilerParams(vmem_limit_bytes=VMEM_LIMIT),
        name="join_columns",
    )(lax.axis_index("seq")[None], *got)


GRAD_TILE = 512


def down_slot(shard, fsdps, seqs):
    group = fsdps // seqs
    return shard % group * seqs + shard // group


def store_blocks(product, tail, column, place_ref, per, fsdps, seqs, first, refs):
    whole = product.astype(BF16)
    cols = product.shape[1]
    pieces = product.shape[0] // per
    for t in range(pieces):
        piece = column * pieces + t
        block = lax.rem(piece, fsdps)
        part = lax.div(piece, fsdps) ^ place_ref[1]
        rows = slice(t * per, (t + 1) * per)

        def store(ref, slot):
            ref[slot, part, :, :cols] = whole[rows]
            if tail is not None:
                ref[slot, part, :, cols:] = tail[rows]

        if first is None:
            alone = refs[0].shape[1] == 1
            store(refs[0], down_slot(block, fsdps, seqs) if alone else block)
            continue
        block = block ^ place_ref[0]
        slot = lax.div(block, 2 * first) * first + lax.rem(block, first)
        sent = lax.rem(lax.div(block, first), 2)
        pl.when(sent == 1)(partial(store, refs[0], slot))
        pl.when(sent == 0)(partial(store, refs[1], slot))


def weight_grad_kernel(place_ref, a_ref, b_ref, *refs, per, fsdps, seqs, first, gain_lane, with_logits, tail_out):
    column = pl.program_id(0)
    product = mm(a_ref[...], b_ref[...], TN)
    refs = list(refs)
    tail = None
    if gain_lane is not None:
        w_ref, vec_ref, other_ref = refs[:3]
        refs = refs[3:]
        lane = lax.broadcasted_iota(jnp.int32, (product.shape[0], LANES), 1)
        gain = vec_ref[...].astype(F32)[:, gain_lane : gain_lane + 1]
        gain_grad = jnp.sum(product * w_ref[...].astype(F32), axis=1, keepdims=True) / gain
        tail = jnp.where(lane == gain_lane, gain_grad, 0.0) + other_ref[...]
    if with_logits:
        x_ref, logit_ref = refs[:2]
        refs = refs[2:]
        tail = tail + mm(x_ref[...], logit_ref[...], TN)
    if tail_out:
        refs.pop()[...] = tail
    tail = tail.astype(BF16) if with_logits else None
    store_blocks(product, tail, column, place_ref, per, fsdps, seqs, first, refs)


def weight_grad(place, a, b, parts, first, gain=None, logits=None, cols=None, at_b=0):
    rows, total = a.shape
    cols = cols or b.shape[1]
    fsdps = lax.axis_size("fsdp")
    per = total // (parts * fsdps)
    tile = min(GRAD_TILE, total)
    wide = cols + (LANES if logits is not None else 0)
    columns = lambda n: pl.BlockSpec((n, tile), lambda c, *_: (0, c))
    lines = lambda n, at=0: pl.BlockSpec((tile, n), lambda c, *_: (c, at))
    whole = lambda *dims: pl.BlockSpec(dims, lambda c, *_: (0,) * len(dims))
    args, in_specs = [a, b], [columns(rows), pl.BlockSpec((rows, cols), lambda c, *_: (0, at_b))]
    copies = 1 if first is None else 2
    block = (fsdps // copies, parts, per, wide)
    out_shape = [jax.ShapeDtypeStruct(block, BF16)] * copies
    out_specs = [whole(*block)] * copies
    lane = None
    if gain is not None:
        weight, weight_at, vectors, at, lane, other = gain
        args += [weight, vectors, other]
        in_specs += [lines(cols, weight_at), lines(LANES, at), lines(LANES)]
    tail_out = gain is not None and logits is None
    if tail_out:
        out_shape = out_shape + [jax.ShapeDtypeStruct((total, LANES), F32)]
        out_specs = out_specs + [lines(LANES)]
    if logits is not None:
        args += list(logits)
        in_specs += [columns(logits[0].shape[0]), whole(*logits[1].shape)]
    return pl.pallas_call(
        partial(
            weight_grad_kernel,
            per=per,
            fsdps=fsdps,
            seqs=lax.axis_size("seq"),
            first=first,
            gain_lane=lane,
            with_logits=logits is not None,
            tail_out=tail_out,
        ),
        grid_spec=pltpu.PrefetchScalarGridSpec(
            num_scalar_prefetch=1,
            grid=(total // tile,),
            in_specs=in_specs,
            out_specs=out_specs,
        ),
        out_shape=out_shape,
        compiler_params=pltpu.CompilerParams(vmem_limit_bytes=VMEM_LIMIT),
        cost_estimate=pl.CostEstimate(
            flops=2 * rows * total * cols,
            transcendentals=0,
            bytes_accessed=2 * (rows * total + rows * cols + total * wide),
        ),
        name="weight_grad",
    )(place, *args)


def hidden_grads_kernel(
    place_ref, act_ref, carried_ref, norm_ref, pre_ref, w_ref, vec_ref, both_ref, tail_ref, *, per, down_per, fsdps, seqs, gain_lane
):
    column = pl.program_id(0)
    down = mm(act_ref[...], carried_ref[...], TN).astype(BF16)
    for t in range(down.shape[0] // down_per):
        slot = down_slot(column * (down.shape[0] // down_per) + t, fsdps, seqs)
        both_ref[slot, 1] = down[t * down_per : (t + 1) * down_per]
    product = mm(norm_ref[...], pre_ref[...], TN)
    lane = lax.broadcasted_iota(jnp.int32, (product.shape[0], LANES), 1)
    gain = vec_ref[...].astype(F32)[:, gain_lane : gain_lane + 1]
    gain_grad = jnp.sum(product * w_ref[...].astype(F32), axis=1, keepdims=True) / gain
    tail_ref[...] = jnp.where(lane == gain_lane, gain_grad, 0.0)
    up = product.astype(BF16)
    pieces = product.shape[0] // per
    for t in range(pieces):
        piece = column * pieces + t
        part = lax.div(piece, fsdps) ^ place_ref[1]
        line = pl.multiple_of(part * per, per)
        both_ref[lax.rem(piece, fsdps), 0, pl.ds(line, per), :] = up[t * per : (t + 1) * per]


def hidden_grads(place, activated, carried_b, normal_m, grad_pre, w_up, vectors, at, lane):
    rows, total = activated.shape
    cols = carried_b.shape[1]
    fsdps = lax.axis_size("fsdp")
    seqs = lax.axis_size("seq")
    tile = min(GRAD_TILE, total)
    columns = pl.BlockSpec((rows, tile), lambda c, *_: (0, c))
    lines = lambda n, at=0: pl.BlockSpec((tile, n), lambda c, *_: (c, at))
    whole = lambda *dims: pl.BlockSpec(dims, lambda c, *_: (0,) * len(dims))
    both = (fsdps, 2, total // fsdps, cols)
    return pl.pallas_call(
        partial(
            hidden_grads_kernel,
            per=total // (seqs * fsdps),
            down_per=total // fsdps,
            fsdps=fsdps,
            seqs=seqs,
            gain_lane=lane,
        ),
        grid_spec=pltpu.PrefetchScalarGridSpec(
            num_scalar_prefetch=1,
            grid=(total // tile,),
            in_specs=[columns, whole(rows, cols), columns, whole(rows, cols), lines(cols), lines(LANES, at)],
            out_specs=[whole(*both), lines(LANES)],
        ),
        out_shape=[jax.ShapeDtypeStruct(both, BF16), jax.ShapeDtypeStruct((total, LANES), F32)],
        compiler_params=pltpu.CompilerParams(vmem_limit_bytes=VMEM_LIMIT),
        cost_estimate=pl.CostEstimate(
            flops=4 * rows * total * cols,
            transcendentals=0,
            bytes_accessed=4 * (rows * total + rows * cols + total * cols),
        ),
        name="hidden_grads",
    )(place, activated, carried_b, normal_m, grad_pre, w_up, vectors)


def order_out_kernel(place_ref, *refs):
    out_ref = refs[-1]
    group, seqs = out_ref.shape[1:3]
    for k in range(seqs):
        for block in range(refs[k].shape[0]):
            shard = place_ref[0] ^ block
            at = lax.div(shard, group) ^ place_ref[1]
            out_ref[at, lax.rem(shard, group), place_ref[1] ^ k] = refs[k][block]


def order_out(place, blocks):
    seqs = len(blocks)
    fsdps, per, width = blocks[0].shape
    full = (seqs, fsdps // seqs, seqs, per, width)
    whole = lambda shape: pl.BlockSpec(shape, lambda i, *_: (0,) * len(shape))
    out = pl.pallas_call(
        order_out_kernel,
        grid_spec=pltpu.PrefetchScalarGridSpec(
            num_scalar_prefetch=1,
            grid=(1,),
            in_specs=[whole(blocks[0].shape)] * seqs,
            out_specs=whole(full),
        ),
        out_shape=jax.ShapeDtypeStruct(full, BF16),
        compiler_params=pltpu.CompilerParams(vmem_limit_bytes=VMEM_LIMIT),
        cost_estimate=pl.CostEstimate(flops=0, transcendentals=0, bytes_accessed=4 * width * width),
        name="order_out",
    )(place, *blocks)
    return out.reshape(-1, width)


ROW_TILE = 512


def pick_rows_kernel(ids_ref, *refs):
    count = len(refs) - 2
    to_ref, total = refs[count:]
    chunk = pl.program_id(0)
    ids = ids_ref[...] - chunk * ROW_TILE
    hit = ids == lax.broadcasted_iota(jnp.int32, (ids.shape[0], ROW_TILE), 1)
    ones = jnp.where(hit, 1.0, 0.0).astype(BF16)
    for i in range(count):
        found = mm(ones, refs[i][...], NN)

        @pl.when(chunk == 0)
        def _():
            total[i] = found

        @pl.when(chunk > 0)
        def _():
            total[i] += found

        @pl.when(chunk == pl.num_programs(0) - 1)
        def _():
            to_ref[i] = total[i].astype(BF16)


def pick_rows(sources, ids):
    length, width = sources[0].shape
    rows = ids.shape[0]
    count = len(sources)
    return pl.pallas_call(
        pick_rows_kernel,
        grid=(length // ROW_TILE,),
        in_specs=[pl.BlockSpec((rows, 1), lambda c: (0, 0))]
        + [pl.BlockSpec((ROW_TILE, width), lambda c: (c, 0))] * count,
        out_specs=pl.BlockSpec((count, rows, width), lambda c: (0, 0, 0)),
        out_shape=jax.ShapeDtypeStruct((count, rows, width), BF16),
        scratch_shapes=[pltpu.VMEM((count, rows, width), F32)],
        compiler_params=pltpu.CompilerParams(vmem_limit_bytes=VMEM_LIMIT),
        cost_estimate=pl.CostEstimate(
            flops=2 * count * rows * length * width,
            transcendentals=0,
            bytes_accessed=2 * count * length * width,
        ),
        name="pick_rows",
    )(ids[:, None], *sources)


def place_rows_kernel(ids_ref, new_ref, from_ref, to_ref):
    ids = ids_ref[...] - pl.program_id(0) * ROW_TILE
    hit = ids == lax.broadcasted_iota(jnp.int32, (ROW_TILE, ids.shape[1]), 0)
    ones = jnp.where(hit, 1.0, 0.0)
    routed = jnp.max(ones, axis=1, keepdims=True) > 0.0
    new = mm(ones.astype(BF16), new_ref[...], NN).astype(BF16)
    to_ref[...] = jnp.where(routed, new, from_ref[...])


def place_rows(source, ids, new):
    length, width = source.shape
    rows = ids.shape[0]
    tiles = pl.BlockSpec((ROW_TILE, width), lambda c: (c, 0))
    return pl.pallas_call(
        place_rows_kernel,
        grid=(length // ROW_TILE,),
        in_specs=[
            pl.BlockSpec((1, rows), lambda c: (0, 0)),
            pl.BlockSpec((rows, width), lambda c: (0, 0)),
            tiles,
        ],
        out_specs=tiles,
        out_shape=jax.ShapeDtypeStruct((length, width), BF16),
        compiler_params=pltpu.CompilerParams(vmem_limit_bytes=VMEM_LIMIT),
        cost_estimate=pl.CostEstimate(
            flops=2 * rows * length * width, transcendentals=0, bytes_accessed=4 * length * width
        ),
        name="place_rows",
    )(ids[None, :], new, source)


def half_lanes(values, half):
    lane = lax.broadcasted_iota(jnp.int32, values.shape, 1)
    keep = lane < HD if half == 0 else lane >= HD
    return jnp.where(keep, values, jnp.zeros_like(values))


def allowed_tile(keys_ref, where, pos_row, start_row):
    keys = keys_ref[where]
    return (keys <= pos_row) & (keys >= start_row)


def attention_forward_kernel(
    window_ref, place_ref, first_ref, q_ref, k_ref, v_ref, pos_ref, start_ref, keys_ref, o_ref, lse_ref
):
    block = pl.program_id(0)
    tile, width = q_ref.shape
    heads = width // HD
    pos_row, start_row = pos_ref[0], start_ref[0]
    last = window_ref[block]
    count = last - first_ref[block] + 1
    lanes = [slice(h // 2 * PAIR, (h // 2 + 1) * PAIR) for h in range(heads)]
    scale = jnp.asarray(HD**-0.5, BF16)
    queries = [half_lanes(q_ref[:, lanes[h]] * scale, h % 2) for h in range(heads)]

    def step(i, carry):
        where = place_ref[last - i]
        allowed = allowed_tile(keys_ref, where, pos_row, start_row)
        each = range(heads)
        raw = [mm(k_ref[where, :, lanes[h]], queries[h], NT) for h in each]
        scores = [jnp.where(allowed, raw[h], NEG_FILL) for h in each]
        tops = [jnp.maximum(carry[h][0], jnp.max(scores[h], axis=0, keepdims=True)) for h in each]
        exponents = [jnp.exp(scores[h] - tops[h]) for h in each]
        values = [mm(v_ref[where, :, lanes[h]], exponents[h].astype(BF16), TN) for h in each]
        shrinks = [jnp.exp(carry[h][0] - tops[h]) for h in each]
        sums = [jnp.sum(exponents[h], axis=0, keepdims=True) for h in each]
        return tuple(
            (tops[h], carry[h][1] * shrinks[h] + sums[h], carry[h][2] * shrinks[h] + values[h])
            for h in each
        )

    empty = (jnp.full((1, tile), NEG_FILL, F32), jnp.zeros((1, tile), F32), jnp.zeros((PAIR, tile), F32))
    done = lax.fori_loop(0, count, step, (empty,) * heads)
    for h in range(0, heads, 2):
        pair = [acc * (1.0 / total) for _, total, acc in done[h : h + 2]]
        joined = jnp.concatenate([pair[0][:HD], pair[1][HD:]], axis=0)
        o_ref[:, lanes[h]] = joined.T.astype(BF16)
    row = lax.broadcasted_iota(jnp.int32, (8, tile), 0)
    lse = jnp.zeros((8, tile), F32)
    for h, (top, total, _) in enumerate(done):
        lse = jnp.where(row == h, top + jnp.log(total), lse)
    lse_ref[...] = lse


def attention_backward_kernel(
    window_ref,
    place_ref,
    first_ref,
    q_ref,
    k_ref,
    v_ref,
    g_ref,
    o_ref,
    lse_ref,
    pos_ref,
    start_ref,
    keys_ref,
    grad_ref,
    dk_sum,
    dv_sum,
):
    block = pl.program_id(0)
    tile, width = q_ref.shape
    heads = width // HD
    pos_row, start_row = pos_ref[0], start_ref[0]
    last = window_ref[block]
    count = last - first_ref[block] + 1
    lanes = [slice(h // 2 * PAIR, (h // 2 + 1) * PAIR) for h in range(heads)]
    scale = HD**-0.5

    @pl.when(block == 0)
    def _():
        dk_sum[...] = jnp.zeros_like(dk_sum)
        dv_sum[...] = jnp.zeros_like(dv_sum)

    queries = [half_lanes(q_ref[:, lanes[h]] * jnp.asarray(scale, BF16), h % 2) for h in range(heads)]
    grads = [half_lanes(g_ref[:, lanes[h]], h % 2) for h in range(heads)]
    inner = []
    for h in range(0, heads, 2):
        both = (g_ref[:, lanes[h]].astype(F32) * o_ref[:, lanes[h]].astype(F32)).T
        inner += [jnp.sum(part, axis=0, keepdims=True) for part in (both[:HD], both[HD:])]

    def step(i, carry):
        where = place_ref[last - i]
        allowed = allowed_tile(keys_ref, where, pos_row, start_row)
        each = range(heads)
        keys = [k_ref[where, :, lanes[h]] for h in each]
        scores = [mm(keys[h], queries[h], NT) for h in each]
        grad_prob = [mm(v_ref[where, :, lanes[h]], grads[h], NT) for h in each]
        prob = [jnp.where(allowed, jnp.exp(scores[h] - lse_ref[h : h + 1, :]), 0.0) for h in each]
        grad_scores = [(prob[h] * (grad_prob[h] - inner[h])).astype(BF16) for h in each]
        values = [mm(prob[h].astype(BF16), grads[h], NN) for h in each]
        moved = [mm(grad_scores[h], queries[h], NN) for h in each]
        for h in range(0, heads, 2):
            dv_sum[where, :, lanes[h]] += values[h] + values[h + 1]
            dk_sum[where, :, lanes[h]] += moved[h] + moved[h + 1]
        return tuple(carry[h] + mm(keys[h], grad_scores[h], TN) for h in each)

    done = lax.fori_loop(0, count, step, (jnp.zeros((PAIR, tile), F32),) * heads)
    for h in range(0, heads, 2):
        joined = jnp.concatenate([done[h][:HD], done[h + 1][HD:]], axis=0) * scale
        at = 2 * width + h * HD
        grad_ref[block, :, at : at + PAIR] = joined.T.astype(BF16)

    @pl.when(block == pl.num_programs(0) - 1)
    def _():
        grad_ref[:, :, :width] = dk_sum[...].astype(BF16)
        grad_ref[:, :, width : 2 * width] = dv_sum[...].astype(BF16)


def attention_specs(blocks, tile, width):
    by_rows = pl.BlockSpec((tile, width), lambda b, *_: (b, 0))
    keys = lambda at: pl.BlockSpec((blocks, tile, width), lambda b, *_: (0, 0, at))
    row = pl.BlockSpec((1, 1, tile), lambda b, *_: (b, 0, 0))
    lse = pl.BlockSpec((8, tile), lambda b, *_: (0, b))
    return by_rows, keys, row, lse, pl.BlockSpec((blocks, tile, 1), lambda b, *_: (0, 0, 0))


def attention_forward(tables, q, kv, pos, start, tile):
    rows, width = q.shape
    blocks = rows // tile
    by_rows, keys, row, lse, cols = attention_specs(blocks, tile, width)
    return pl.pallas_call(
        attention_forward_kernel,
        grid_spec=pltpu.PrefetchScalarGridSpec(
            num_scalar_prefetch=3,
            grid=(blocks,),
            in_specs=[by_rows, keys(0), keys(1), row, row, cols],
            out_specs=[by_rows, lse],
        ),
        out_shape=[jax.ShapeDtypeStruct((rows, width), BF16), jax.ShapeDtypeStruct((8, rows), F32)],
        compiler_params=pltpu.CompilerParams(vmem_limit_bytes=VMEM_LIMIT),
        cost_estimate=pl.CostEstimate(
            flops=2 * rows * rows * width,
            transcendentals=rows * rows * width // HD // 2,
            bytes_accessed=8 * rows * width,
        ),
        name="attention_forward",
    )(
        *tables,
        q,
        kv.reshape(blocks, tile, 2 * width),
        kv.reshape(blocks, tile, 2 * width),
        pos.reshape(blocks, 1, tile),
        start.reshape(blocks, 1, tile),
        pos.reshape(blocks, tile, 1),
    )


def attention_backward(tables, q, kv, grad, out, lse_rows, pos, start, tile):
    rows, width = q.shape
    blocks = rows // tile
    by_rows, keys, row, lse, cols = attention_specs(blocks, tile, width)
    grads = pl.pallas_call(
        attention_backward_kernel,
        grid_spec=pltpu.PrefetchScalarGridSpec(
            num_scalar_prefetch=3,
            grid=(blocks,),
            in_specs=[by_rows, keys(0), keys(1), by_rows, by_rows, lse, row, row, cols],
            out_specs=pl.BlockSpec((blocks, tile, 3 * width), lambda b, *_: (0, 0, 0)),
            scratch_shapes=[pltpu.VMEM((blocks, tile, width), F32)] * 2,
        ),
        out_shape=jax.ShapeDtypeStruct((blocks, tile, 3 * width), BF16),
        compiler_params=pltpu.CompilerParams(vmem_limit_bytes=VMEM_LIMIT),
        cost_estimate=pl.CostEstimate(
            flops=5 * rows * rows * width,
            transcendentals=rows * rows * width // HD // 2,
            bytes_accessed=14 * rows * width,
        ),
        name="attention_backward",
    )(
        *tables,
        q,
        kv.reshape(blocks, tile, 2 * width),
        kv.reshape(blocks, tile, 2 * width),
        grad,
        out,
        lse_rows,
        pos.reshape(blocks, 1, tile),
        start.reshape(blocks, 1, tile),
        pos.reshape(blocks, tile, 1),
    )
    return grads.reshape(rows, 3 * width)


def whole_spec(shape):
    return pl.BlockSpec(shape, lambda i, *_: (0,) * len(shape))


def one_step(kernel, name, place, args, out_shape, flops):
    size = lambda x: x.size * x.dtype.itemsize
    return pl.pallas_call(
        kernel,
        grid_spec=pltpu.PrefetchScalarGridSpec(
            num_scalar_prefetch=1,
            grid=(1,),
            in_specs=[whole_spec(x.shape) for x in args],
            out_specs=[whole_spec(x.shape) for x in out_shape],
        ),
        out_shape=out_shape,
        compiler_params=pltpu.CompilerParams(vmem_limit_bytes=VMEM_LIMIT),
        cost_estimate=pl.CostEstimate(
            flops=flops, transcendentals=0, bytes_accessed=sum(size(x) for x in (*args, *out_shape))
        ),
        name=name,
    )(place, *args)


def norm_scale(values):
    return lax.rsqrt(jnp.mean(values * values, axis=1, keepdims=True) + EPS)


def first_shard_kernel(place_ref, q_ref, k_ref, v_ref, tails_ref, out_ref, own_ref):
    span = q_ref.shape[1]
    for i, ref in enumerate((k_ref, v_ref, q_ref)):
        own_ref[:, i * span : (i + 1) * span] = ref[...]
    own_ref[:, 3 * span : 3 * span + LANES] = tails_ref[...]
    lines = out_ref.shape[1]
    for j in range(out_ref.shape[2] // span):
        own_ref[j * lines : (j + 1) * lines, 3 * span + LANES :] = out_ref[0, :, j * span : (j + 1) * span]


def first_shard(place, qkv, tails, out, span):
    rows, width = out.shape
    seqs = width // span
    out = out.reshape(seqs, rows // seqs, width)
    heads = lambda i: pl.BlockSpec((rows, span), lambda g, at: (0, i * seqs + at[1]))
    cols = 4 * span + LANES
    return pl.pallas_call(
        first_shard_kernel,
        grid_spec=pltpu.PrefetchScalarGridSpec(
            num_scalar_prefetch=1,
            grid=(1,),
            in_specs=[
                heads(0),
                heads(1),
                heads(2),
                pl.BlockSpec((rows, LANES), lambda g, at: (0, 0)),
                pl.BlockSpec((1, rows // seqs, width), lambda g, at: (at[1], 0, 0)),
            ],
            out_specs=pl.BlockSpec((rows, cols), lambda g, at: (0, 0)),
        ),
        out_shape=jax.ShapeDtypeStruct((rows, cols), BF16),
        compiler_params=pltpu.CompilerParams(vmem_limit_bytes=VMEM_LIMIT),
        cost_estimate=pl.CostEstimate(flops=0, transcendentals=0, bytes_accessed=4 * rows * cols),
        name="first_shard",
    )(place, qkv, qkv, qkv, tails, out)


def hidden_shard_kernel(place_ref, up_ref, down_ref, both_ref):
    rows = up_ref.shape[0]
    both_ref[:rows, :] = up_ref[...]
    both_ref[rows:, :] = down_ref[...]


def hidden_shard(place, up, down, span):
    rows, width = up.shape[0], down.shape[1]
    seqs = lax.axis_size("seq")
    return pl.pallas_call(
        hidden_shard_kernel,
        grid_spec=pltpu.PrefetchScalarGridSpec(
            num_scalar_prefetch=1,
            grid=(width // span,),
            in_specs=[
                pl.BlockSpec((rows, span), lambda i, at: (0, i * seqs + at[1])),
                pl.BlockSpec((span, span), lambda i, at: (at[1], i)),
            ],
            out_specs=pl.BlockSpec((rows + span, span), lambda i, at: (0, i)),
        ),
        out_shape=jax.ShapeDtypeStruct((rows + span, width), BF16),
        compiler_params=pltpu.CompilerParams(vmem_limit_bytes=VMEM_LIMIT),
        cost_estimate=pl.CostEstimate(flops=0, transcendentals=0, bytes_accessed=8 * rows * width),
        name="hidden_shard",
    )(place, up, down)


def project_kernel(place_ref, *refs, seqs, slow, fast):
    x_refs, pieces = refs[:seqs], refs[seqs:-7]
    out_ref, w_ref, vec_ref, normal_ref, q_ref, kv_ref, rate_ref = refs[-7:]
    per, cols = pieces[0].shape[1], w_ref.shape[1]
    span = q_ref.shape[1]
    lines = out_ref.shape[1]
    done = 0
    for ref in pieces:
        for i in range(ref.shape[0]):
            block = done % slow * fast + done // slow
            shard = place_ref[0] ^ block
            w_ref[pl.ds(pl.multiple_of(shard * per, per), per), :] = ref[i, :, :cols]
            for j in range(seqs):
                out_ref[block, :, j * span : (j + 1) * span] = ref[i, j * lines : (j + 1) * lines, cols:]
            done += 1
    tails = w_ref[:, 3 * span :]
    vec = tails.astype(F32).T
    vec_ref[...] = vec[:8]
    gain = vec[1:2]
    weight = w_ref[:, : 3 * span]
    rows = x_refs[0].shape[1]
    for k in range(seqs):
        here = slice(k * rows, (k + 1) * rows)
        x = x_refs[k][0]
        x_f = x.astype(F32)
        normal = (x_f * norm_scale(x_f) * gain).astype(BF16)
        normal_ref[here, :] = normal
        proj = mm(normal, weight, NN).astype(BF16)
        kv_ref[here, :] = proj[:, : 2 * span]
        q_ref[here, :] = proj[:, 2 * span :]
        rate_ref[here, :] = jax.nn.sigmoid(mm(x, tails, NN)[:, :1])


def project(place, x_blocks, pieces, span):
    slow, fast = fsdp_sizes()
    _, rows, width = x_blocks[0].shape
    total = rows * len(x_blocks)
    cols = pieces[0].shape[2] - span
    out_shape = [
        jax.ShapeDtypeStruct((slow * fast, width // (slow * fast * len(x_blocks)), width), BF16),
        jax.ShapeDtypeStruct((width, cols), BF16),
        jax.ShapeDtypeStruct((8, width), F32),
        jax.ShapeDtypeStruct((total, width), BF16),
        jax.ShapeDtypeStruct((total, span), BF16),
        jax.ShapeDtypeStruct((total, 2 * span), BF16),
        jax.ShapeDtypeStruct((total, 1), F32),
    ]
    kernel = partial(project_kernel, seqs=len(x_blocks), slow=slow, fast=fast)
    return one_step(
        kernel, "project", place, [*x_blocks, *pieces], out_shape, 2 * total * width * cols
    )


def branch_kernel(place_ref, *refs, seqs):
    x_refs, att_refs = refs[:seqs], refs[seqs : 2 * seqs]
    w_ref, vec_ref, rate_ref, branch_ref, normal_ref, carried_ref = refs[2 * seqs :]
    rows = x_refs[0].shape[1]
    span = att_refs[0].shape[1]
    gain = vec_ref[2:3, :]
    for j in range(seqs):
        here = slice(j * rows, (j + 1) * rows)
        branch = 0.0
        for b in range(seqs):
            there = slice((j ^ b) * rows, ((j ^ b) + 1) * rows)
            branch = branch + mm(att_refs[b][there, :], w_ref[b * span : (b + 1) * span, :], NN)
        if j == 0:
            branch_ref[...] = branch
        middle = x_refs[j][0].astype(F32) + branch
        normal_ref[here, :] = (middle * norm_scale(middle) * gain).astype(BF16)
        carried_ref[here, :] = (rate_ref[here, :] * x_refs[j][1].astype(F32)).astype(BF16)


def attention_branch(place, blocks, att_blocks, w_out, vectors, rate):
    _, rows, width = blocks[0].shape
    seqs = len(blocks)
    out_shape = [
        jax.ShapeDtypeStruct((rows, width), F32),
        jax.ShapeDtypeStruct((rows * seqs, width), BF16),
        jax.ShapeDtypeStruct((rows * seqs, width), BF16),
    ]
    args = [*blocks, *att_blocks, w_out, vectors, rate]
    return one_step(
        partial(branch_kernel, seqs=seqs),
        "attention_branch",
        place,
        args,
        out_shape,
        2 * rows * seqs * width * width,
    )


def attention_grad_kernel(place_ref, *refs, seqs):
    w_ref, joined_ref, out_ref = refs[seqs:]
    rows = refs[0].shape[0]
    for j in range(seqs):
        here = slice(j * rows, (j + 1) * rows)
        block = refs[j][...]
        joined_ref[here, :] = block
        out_ref[here, :] = mm(block, w_ref[...], NT).astype(BF16)


def attention_grad(place, blocks, w_out):
    rows, width = blocks[0].shape
    total = rows * len(blocks)
    span = w_out.shape[0]
    out_shape = [jax.ShapeDtypeStruct((total, width), BF16), jax.ShapeDtypeStruct((total, span), BF16)]
    return one_step(
        partial(attention_grad_kernel, seqs=len(blocks)),
        "attention_grad",
        place,
        [*blocks, w_out],
        out_shape,
        2 * total * width * span,
    )


def norm_back(values, scale, gain, grad):
    weighted = grad * gain
    inner = jnp.mean(weighted * values, axis=1, keepdims=True)
    return scale * weighted - values * (scale * scale * scale) * inner


def shards(
    inputs,
    cotangent,
    routed,
    doc_starts,
    router,
    attn_gain,
    qkv_weight,
    out_weight,
    mlp_gain,
    up_weight,
    down_weight,
):
    seqs = lax.axis_size("seq")
    fsdps = lax.axis_size("fsdp")
    me = lax.axis_index("seq")
    width = inputs.shape[2]
    tok_count = inputs.shape[1]
    own_windows = tok_count // WIN
    windows = routed.shape[1]
    tile = routed.shape[2]
    own_rows = own_windows * tile
    rows = windows * tile
    heads_width = width // seqs
    hidden = up_weight.shape[1]
    own_hidden = hidden // seqs

    order = jnp.arange(seqs, dtype=jnp.int32) ^ me
    window_of = (order[:, None] * own_windows + jnp.arange(own_windows, dtype=jnp.int32)).reshape(-1)
    stream_pos = jnp.arange(windows, dtype=jnp.int32)[:, None] * WIN + routed[0]
    pos = stream_pos[window_of].reshape(-1)
    starts = doc_starts[0]
    start = jnp.max(jnp.where(starts[None, :] <= pos[:, None], starts[None, :], 0), axis=1)
    first_window = start.reshape(windows, tile)[:, 0] // WIN
    place_of = jnp.zeros((windows,), jnp.int32).at[window_of].set(jnp.arange(windows, dtype=jnp.int32))
    tables = (window_of, place_of, first_window)

    own_routes = lax.dynamic_slice_in_dim(routed[0], me * own_windows, own_windows, 0)
    row_ids = ((jnp.arange(own_windows, dtype=jnp.int32) * WIN)[:, None] + own_routes).reshape(-1)
    stream_in = inputs[0]
    grad_in = cotangent[0]

    place = jnp.stack([lax.axis_index("fsdp"), me])
    vectors = jnp.stack([router, attn_gain, mlp_gain], axis=1)
    tails = jnp.pad(vectors, ((0, 0), (0, LANES - vectors.shape[1])))
    first_own = first_shard(place, qkv_weight, tails, out_weight, heads_width)
    first_slow = gather_slow(first_own)
    first_got = own_fast(first_slow[0])
    picked = pick_rows([stream_in, grad_in], after(row_ids, first_own))

    span = down_weight.shape[0] // seqs
    square = own_hidden == width and span % LANES == 0
    shard_rows = up_weight.shape[0]
    if square:
        hidden_own = hidden_shard(place, after(up_weight, picked, *first_got), down_weight, span)
        hidden_late = after(hidden_own, *first_slow[1:])
        hidden_all = lax.all_gather(hidden_late, "fsdp", axis=0)
        w_up = hidden_all[:, :shard_rows].reshape(width, own_hidden)
        w_down = hidden_all[:, shard_rows:].reshape(own_hidden, width)
    else:
        hidden_own = lax.dynamic_index_in_dim(
            up_weight.reshape(-1, fsdps, seqs, span), me, axis=2, keepdims=False
        ).reshape(-1, own_hidden)
        down_own = lax.dynamic_slice_in_dim(down_weight, me * span, span, 0)
        w_up = lax.all_gather(hidden_own, "fsdp", axis=0, tiled=True)
        w_down = lax.all_gather(down_own, "fsdp", axis=0, tiled=True)
    first_pieces = gather_fast(first_slow[0], after(tuple(first_slow[1:]), hidden_own), first_got)
    blocks = gather_blocks(picked, "seq", first_pieces[-1])
    out_part, w_qkv, vectors, normal_a, q, kv, rate = project(
        place, blocks, first_pieces, heads_width
    )
    router_w, gain_a, gain_m = vectors[0:1], vectors[1:2], vectors[2:3]
    tail_at = 3 * heads_width // LANES
    att_own, lse = attention_forward(tables, q, kv, pos, start, tile)
    out_blocks = gather_blocks(out_part, "seq", att_own)
    out_ordered = order_out(place, out_blocks)
    att_blocks = gather_blocks(att_own, "seq", out_ordered)
    w_out = out_ordered[:heads_width]
    branch_o, normal_m, carried_b = attention_branch(
        place, blocks, att_blocks, out_ordered, vectors, rate
    )
    pre_act = mm(normal_m, w_up, NN)
    cdf = 0.5 * (1.0 + lax.erf(pre_act * (0.5**0.5)))
    activated = (pre_act * cdf).astype(BF16)
    slope = cdf + pre_act * (jnp.exp(-0.5 * pre_act * pre_act) * (2.0 * jnp.pi) ** -0.5)

    grad_act = mm(carried_b, w_down, NT)
    grad_pre = (grad_act * slope).astype(BF16)
    cut = lambda a, b: a[b * own_rows : (b + 1) * own_rows]
    normal_grads = [mm(cut(grad_pre, b), w_up, NT) for b in range(seqs)]
    grad_normal_m = scatter_blocks(normal_grads, "seq")
    flat = place * jnp.array([1, 0], jnp.int32)
    scatter = lambda g: lax.psum_scatter(g, "fsdp", scatter_dimension=0)
    activated_late = after(activated, *normal_grads)
    if square:
        both, gains = hidden_grads(
            place, activated_late, carried_b, normal_m, grad_pre, w_up, w_qkv, tail_at, 2
        )
        grad_normal_m = after(grad_normal_m, both)
        both = scatter(both)
        up_part, down_part = both[0].reshape(seqs, -1, own_hidden), both[1]
    else:
        (down_grad,) = weight_grad(flat, activated_late, carried_b, 1, None)
        up_grad, gains = weight_grad(
            place,
            normal_m,
            grad_pre,
            seqs,
            None,
            (w_up, 0, w_qkv, tail_at, 2, jnp.zeros((width, LANES), F32)),
        )
        up_part, down_part = scatter(up_grad), scatter(down_grad)[0]

    x_o = picked[0].astype(F32)
    g_o = picked[1].astype(F32)
    rate_o = cut(rate, 0)
    middle_o = x_o + branch_o
    grad_middle = norm_back(middle_o, norm_scale(middle_o), gain_m, grad_normal_m)
    grad_a_own = (rate_o * g_o + grad_middle).astype(BF16)
    grad_a_blocks = gather_blocks(grad_a_own, "seq")
    branch_parts = [mm(cut(after(activated, grad_a_blocks[1]), b), w_down, NN) for b in range(seqs)]
    branch_f = scatter_blocks(branch_parts, "seq", grad_a_blocks[-1])
    grad_a, grad_att = attention_grad(place, grad_a_blocks, w_out)
    fast = 1
    slow = fsdp_sizes()[1]
    out_send, out_keep = weight_grad(flat, att_own, after(grad_a, *branch_parts), 1, fast)
    grad_proj = attention_backward(
        tables, q, kv, after(grad_att, out_send), att_own, lse, pos, start, tile
    )
    kv_send, kv_keep, gains = weight_grad(
        place,
        normal_a,
        grad_proj,
        seqs,
        fast,
        (w_qkv, 0, w_qkv, tail_at, 1, gains),
        cols=2 * heads_width,
    )
    branch_sum = branch_o + branch_f
    result = x_o + rate_o * branch_sum
    grad_logit = jnp.sum(g_o * branch_sum, axis=1, keepdims=True) * rate_o * (1.0 - rate_o)
    logit_high = grad_logit.astype(BF16)
    logit_low = (grad_logit - logit_high.astype(F32)).astype(BF16)
    lane = jnp.arange(LANES)[None, :]
    logits = jnp.where(lane == 0, logit_high, jnp.where(lane == 3, logit_low, jnp.zeros((), BF16)))
    q_send, q_keep = weight_grad(
        place,
        after(normal_a, kv_send),
        grad_proj,
        seqs,
        slow,
        (w_qkv, 2, w_qkv, tail_at, 1, gains),
        (picked[0], logits),
        cols=heads_width,
        at_b=2,
    )
    out_sum = reduce_blocks(out_send, out_keep, fast, [(q_send,)])[0]
    kv_part = reduce_blocks(kv_send, kv_keep, fast, [()])
    q_part = reduce_blocks(q_send, q_keep, slow, [()])
    proj_late = after(grad_proj, q_send)
    w_proj = w_qkv[:, : 3 * heads_width]
    grad_normal_a = scatter_blocks([mm(cut(proj_late, b), w_proj, NT) for b in range(seqs)], "seq")
    output = place_rows(stream_in, row_ids, after(result.astype(BF16), q_send))
    grad_norm_x = norm_back(x_o, norm_scale(x_o), gain_a, grad_normal_a)
    grad_picked = g_o + grad_middle + grad_norm_x + grad_logit * router_w
    input_grad = place_rows(grad_in, row_ids, grad_picked.astype(BF16))
    down_sum = lax.ppermute(
        down_part,
        ("seq", "fsdp"),
        [
            (s * fsdps + down_slot(f, fsdps, seqs), f * seqs + s)
            for s in range(seqs)
            for f in range(fsdps)
        ],
    ).astype(F32)
    qkv_part = jnp.concatenate(
        [q_part[:, :, :heads_width], kv_part, q_part[:, :, heads_width:]], axis=2
    )
    up_sum, qkv_sum, tiny = exchange_columns(up_part, qkv_part, span, heads_width)
    return (
        output[None],
        input_grad[None],
        tiny[:, 0] + tiny[:, 3],
        tiny[:, 1],
        qkv_sum,
        out_sum,
        tiny[:, 2],
        up_sum,
        down_sum,
    )


def solution(mesh):
    return jax.shard_map(
        shards,
        mesh=mesh,
        in_specs=(
            P("fsdp", "seq", None),
            P("fsdp", "seq", None),
            P("fsdp", None, None),
            P("fsdp", None),
            P("fsdp"),
            P("fsdp"),
            P("fsdp", None),
            P("fsdp", None),
            P("fsdp"),
            P("fsdp", None),
            P("fsdp", None),
        ),
        out_specs=(
            P("fsdp", "seq", None),
            P("fsdp", "seq", None),
            P(("seq", "fsdp")),
            P(("seq", "fsdp")),
            P(("seq", "fsdp"), None),
            P(("seq", "fsdp"), None),
            P(("seq", "fsdp")),
            P(("seq", "fsdp"), None),
            P(("seq", "fsdp"), None),
        ),
        check_vma=False,
    )
```

```python
from functools import partial

import jax
import jax.numpy as jnp
from jax import lax
from jax.experimental import pallas as pl
from jax.experimental.pallas import tpu as pltpu
from jax.sharding import PartitionSpec as P

H = 16
HD = 64
WIN = 2048
EPS = 1e-05
NEG_FILL = -1e30
PAIR = 2 * HD
LANES = 128
BF16 = jnp.bfloat16
F32 = jnp.float32
VMEM_LIMIT = 48 * 1024 * 1024
GRAD_LIMIT = 28 * 1024 * 1024


def mm(a, b, dims):
    return lax.dot_general(a, b, (dims, ((), ())), preferred_element_type=F32)


NN = ((1,), (0,))
NT = ((1,), (1,))
TN = ((0,), (0,))


def flip(values, axis, bit):
    count = lax.axis_size(axis)
    return lax.ppermute(values, axis, [(j, j ^ bit) for j in range(count)])


def bits_down(count):
    bit = count // 2
    while bit:
        yield bit
        bit //= 2


def gather_blocks(own, axis, *waits):
    blocks = {0: own}
    top = lax.axis_size(axis) // 2
    for bit in bits_down(lax.axis_size(axis)):
        for key in list(blocks):
            block = after(blocks[key], *waits) if key else blocks[key]
            blocks[key ^ bit] = flip(block, axis, bit)
    return [blocks[key] for key in sorted(blocks)]


def scatter_blocks(blocks, axis, *waits):
    parts = dict(enumerate(blocks))
    bit = 1
    while bit < lax.axis_size(axis):
        for key in [k for k in parts if k & bit]:
            part = parts.pop(key).astype(BF16)
            got = flip(part if bit == 1 else after(part, *waits), axis, bit)
            parts[key ^ bit] = parts[key ^ bit] + got.astype(F32)
        bit *= 2
    return parts[0]


def after(values, *earlier):
    earlier = [e for e in earlier if e is not None]
    return lax.optimization_barrier((values, *earlier))[0] if earlier else values


def fsdp_sizes():
    count = lax.axis_size("fsdp")
    fast = 2 ** ((count.bit_length() - 1) // 2)
    return count // fast, fast


def gather_slow(own, *waits):
    slow, fast = fsdp_sizes()
    own_late = after(own, *waits)
    return [own_late] + [flip(own_late, "fsdp", k * fast) for k in range(1, slow)]


def own_fast(own):
    _, fast = fsdp_sizes()
    return [flip(own[None], "fsdp", k) for k in range(1, fast)]


def gather_fast(own, others, own_got):
    _, fast = fsdp_sizes()
    others = jnp.stack(others)
    pieces = [own[None], others]
    for k in range(1, fast):
        pieces += [own_got[k - 1], flip(others, "fsdp", k)]
    return pieces


def low_bits(count):
    bit = 1
    while bit < count:
        yield bit
        bit *= 2


def reduce_blocks(send, keep, first, waits):
    bits = [first] + [b for b in low_bits(lax.axis_size("fsdp")) if b != first]
    total = None
    for i, bit in enumerate(bits):
        got = flip(send, "fsdp", bit)
        total = keep.astype(F32) + got.astype(F32)
        if bit != bits[-1]:
            send = after(total[1::2].astype(BF16), *waits[min(i, len(waits) - 1)])
            keep = total[0::2]
    return total[0]


def join_columns_kernel(me_ref, *refs, up_span, span):
    up_ref, qkv_ref, tail_ref = refs[-3:]
    count = len(refs) - 3
    own_hidden = up_ref.shape[1] // count
    tail = 0.0
    for k in range(count):
        block = refs[k][...].astype(F32)
        at = me_ref[0] ^ k
        for ref, first, groups, cols in ((up_ref, 0, own_hidden // up_span, up_span), (qkv_ref, own_hidden, 3, span)):
            for g in range(groups):
                start = pl.multiple_of((g * count + at) * cols, cols)
                ref[:, pl.ds(start, cols)] = block[:, first + g * cols : first + (g + 1) * cols]
        tail = tail + block[:, own_hidden + 3 * span :]
    tail_ref[...] = tail


def exchange_columns(up, qkv, up_span, span):
    count, rows, own_hidden = up.shape
    both = jnp.concatenate([up.astype(BF16), qkv.astype(BF16)], axis=2)
    got = [both[0]] + [flip(both[k], "seq", k) for k in range(1, count)]
    shapes = [(rows, count * own_hidden), (rows, 3 * count * span), (rows, LANES)]
    if up_span % LANES:
        me = lax.axis_index("seq")
        groups = own_hidden // up_span
        joined = jnp.zeros((rows, groups, count, up_span), F32)
        for k in range(count):
            part = got[k][:, :own_hidden].astype(F32).reshape(rows, groups, 1, up_span)
            joined = lax.dynamic_update_slice_in_dim(joined, part, me ^ k, axis=2)
        alone = [g[:, own_hidden:] for g in got]
        zero = [jnp.concatenate([jnp.zeros((rows, LANES), BF16), a], axis=1) for a in alone]
        rest = join_columns(zero, [(rows, count * LANES), *shapes[1:]], LANES, span)
        return (joined.reshape(rows, -1), *rest[1:])
    return join_columns(got, shapes, up_span, span)


def join_columns(got, shapes, up_span, span):
    whole = lambda shape: pl.BlockSpec(shape, lambda i, *_: (0, 0))
    return pl.pallas_call(
        partial(join_columns_kernel, up_span=up_span, span=span),
        grid_spec=pltpu.PrefetchScalarGridSpec(
            num_scalar_prefetch=1,
            grid=(1,),
            in_specs=[whole(got[0].shape)] * len(got),
            out_specs=[whole(shape) for shape in shapes],
        ),
        out_shape=[jax.ShapeDtypeStruct(shape, F32) for shape in shapes],
        compiler_params=pltpu.CompilerParams(vmem_limit_bytes=VMEM_LIMIT),
        name="join_columns",
    )(lax.axis_index("seq")[None], *got)


GRAD_TILE = 512


def down_slot(shard, fsdps, seqs):
    group = fsdps // seqs
    return shard % group * seqs + shard // group


def store_blocks(product, tail, column, place_ref, per, fsdps, seqs, first, refs):
    whole = product.astype(BF16)
    cols = product.shape[1]
    pieces = product.shape[0] // per
    for t in range(pieces):
        piece = column * pieces + t
        block = lax.rem(piece, fsdps)
        part = lax.div(piece, fsdps) ^ place_ref[1]
        rows = slice(t * per, (t + 1) * per)

        def store(ref, slot):
            ref[slot, part, :, :cols] = whole[rows]
            if tail is not None:
                ref[slot, part, :, cols:] = tail[rows]

        if first is None:
            alone = refs[0].shape[1] == 1
            store(refs[0], down_slot(block, fsdps, seqs) if alone else block)
            continue
        block = block ^ place_ref[0]
        slot = lax.div(block, 2 * first) * first + lax.rem(block, first)
        sent = lax.rem(lax.div(block, first), 2)
        pl.when(sent == 1)(partial(store, refs[0], slot))
        pl.when(sent == 0)(partial(store, refs[1], slot))


def weight_grad_kernel(place_ref, a_ref, b_ref, *refs, per, fsdps, seqs, first, gain_lane, with_logits, tail_out):
    column = pl.program_id(0)
    product = mm(a_ref[...], b_ref[...], TN)
    refs = list(refs)
    tail = None
    if gain_lane is not None:
        w_ref, vec_ref, other_ref = refs[:3]
        refs = refs[3:]
        lane = lax.broadcasted_iota(jnp.int32, (product.shape[0], LANES), 1)
        gain = vec_ref[...].astype(F32)[:, gain_lane : gain_lane + 1]
        gain_grad = jnp.sum(product * w_ref[...].astype(F32), axis=1, keepdims=True) / gain
        tail = jnp.where(lane == gain_lane, gain_grad, 0.0) + other_ref[...]
    if with_logits:
        x_ref, logit_ref = refs[:2]
        refs = refs[2:]
        tail = tail + mm(x_ref[...], logit_ref[...], TN)
    if tail_out:
        refs.pop()[...] = tail
    tail = tail.astype(BF16) if with_logits else None
    store_blocks(product, tail, column, place_ref, per, fsdps, seqs, first, refs)


def weight_grad(place, a, b, parts, first, gain=None, logits=None, cols=None, at_b=0):
    rows, total = a.shape
    cols = cols or b.shape[1]
    fsdps = lax.axis_size("fsdp")
    per = total // (parts * fsdps)
    tile = min(GRAD_TILE, total)
    wide = cols + (LANES if logits is not None else 0)
    columns = lambda n: pl.BlockSpec((n, tile), lambda c, *_: (0, c))
    lines = lambda n, at=0: pl.BlockSpec((tile, n), lambda c, *_: (c, at))
    whole = lambda *dims: pl.BlockSpec(dims, lambda c, *_: (0,) * len(dims))
    args, in_specs = [a, b], [columns(rows), pl.BlockSpec((rows, cols), lambda c, *_: (0, at_b))]
    copies = 1 if first is None else 2
    block = (fsdps // copies, parts, per, wide)
    out_shape = [jax.ShapeDtypeStruct(block, BF16)] * copies
    out_specs = [whole(*block)] * copies
    lane = None
    if gain is not None:
        weight, weight_at, vectors, at, lane, other = gain
        args += [weight, vectors, other]
        in_specs += [lines(cols, weight_at), lines(LANES, at), lines(LANES)]
    tail_out = gain is not None and logits is None
    if tail_out:
        out_shape = out_shape + [jax.ShapeDtypeStruct((total, LANES), F32)]
        out_specs = out_specs + [lines(LANES)]
    if logits is not None:
        args += list(logits)
        in_specs += [columns(logits[0].shape[0]), whole(*logits[1].shape)]
    return pl.pallas_call(
        partial(
            weight_grad_kernel,
            per=per,
            fsdps=fsdps,
            seqs=lax.axis_size("seq"),
            first=first,
            gain_lane=lane,
            with_logits=logits is not None,
            tail_out=tail_out,
        ),
        grid_spec=pltpu.PrefetchScalarGridSpec(
            num_scalar_prefetch=1,
            grid=(total // tile,),
            in_specs=in_specs,
            out_specs=out_specs,
        ),
        out_shape=out_shape,
        compiler_params=pltpu.CompilerParams(vmem_limit_bytes=GRAD_LIMIT),
        cost_estimate=pl.CostEstimate(
            flops=2 * rows * total * cols,
            transcendentals=0,
            bytes_accessed=2 * (rows * total + rows * cols + total * wide),
        ),
        name="weight_grad",
    )(place, *args)


def hidden_grads_kernel(
    place_ref, act_ref, carried_ref, norm_ref, pre_ref, w_ref, vec_ref, both_ref, tail_ref, *, per, down_per, fsdps, seqs, gain_lane
):
    column = pl.program_id(0)
    down = mm(act_ref[...], carried_ref[...], TN).astype(BF16)
    for t in range(down.shape[0] // down_per):
        slot = down_slot(column * (down.shape[0] // down_per) + t, fsdps, seqs)
        both_ref[slot, 1] = down[t * down_per : (t + 1) * down_per]
    product = mm(norm_ref[...], pre_ref[...], TN)
    lane = lax.broadcasted_iota(jnp.int32, (product.shape[0], LANES), 1)
    gain = vec_ref[...].astype(F32)[:, gain_lane : gain_lane + 1]
    gain_grad = jnp.sum(product * w_ref[...].astype(F32), axis=1, keepdims=True) / gain
    tail_ref[...] = jnp.where(lane == gain_lane, gain_grad, 0.0)
    up = product.astype(BF16)
    pieces = product.shape[0] // per
    for t in range(pieces):
        piece = column * pieces + t
        part = lax.div(piece, fsdps) ^ place_ref[1]
        line = pl.multiple_of(part * per, per)
        both_ref[lax.rem(piece, fsdps), 0, pl.ds(line, per), :] = up[t * per : (t + 1) * per]


def hidden_grads(place, activated, carried_b, normal_m, grad_pre, w_up, vectors, at, lane):
    rows, total = activated.shape
    cols = carried_b.shape[1]
    fsdps = lax.axis_size("fsdp")
    seqs = lax.axis_size("seq")
    tile = min(GRAD_TILE, total)
    columns = pl.BlockSpec((rows, tile), lambda c, *_: (0, c))
    lines = lambda n, at=0: pl.BlockSpec((tile, n), lambda c, *_: (c, at))
    whole = lambda *dims: pl.BlockSpec(dims, lambda c, *_: (0,) * len(dims))
    both = (fsdps, 2, total // fsdps, cols)
    return pl.pallas_call(
        partial(
            hidden_grads_kernel,
            per=total // (seqs * fsdps),
            down_per=total // fsdps,
            fsdps=fsdps,
            seqs=seqs,
            gain_lane=lane,
        ),
        grid_spec=pltpu.PrefetchScalarGridSpec(
            num_scalar_prefetch=1,
            grid=(total // tile,),
            in_specs=[columns, whole(rows, cols), columns, whole(rows, cols), lines(cols), lines(LANES, at)],
            out_specs=[whole(*both), lines(LANES)],
        ),
        out_shape=[jax.ShapeDtypeStruct(both, BF16), jax.ShapeDtypeStruct((total, LANES), F32)],
        compiler_params=pltpu.CompilerParams(vmem_limit_bytes=GRAD_LIMIT),
        cost_estimate=pl.CostEstimate(
            flops=4 * rows * total * cols,
            transcendentals=0,
            bytes_accessed=4 * (rows * total + rows * cols + total * cols),
        ),
        name="hidden_grads",
    )(place, activated, carried_b, normal_m, grad_pre, w_up, vectors)


def order_out_kernel(place_ref, *refs):
    out_ref = refs[-1]
    group, seqs = out_ref.shape[1:3]
    for k in range(seqs):
        for block in range(refs[k].shape[0]):
            shard = place_ref[0] ^ block
            at = lax.div(shard, group) ^ place_ref[1]
            out_ref[at, lax.rem(shard, group), place_ref[1] ^ k] = refs[k][block]


def order_out(place, blocks):
    seqs = len(blocks)
    fsdps, per, width = blocks[0].shape
    full = (seqs, fsdps // seqs, seqs, per, width)
    whole = lambda shape: pl.BlockSpec(shape, lambda i, *_: (0,) * len(shape))
    out = pl.pallas_call(
        order_out_kernel,
        grid_spec=pltpu.PrefetchScalarGridSpec(
            num_scalar_prefetch=1,
            grid=(1,),
            in_specs=[whole(blocks[0].shape)] * seqs,
            out_specs=whole(full),
        ),
        out_shape=jax.ShapeDtypeStruct(full, BF16),
        compiler_params=pltpu.CompilerParams(vmem_limit_bytes=VMEM_LIMIT),
        cost_estimate=pl.CostEstimate(flops=0, transcendentals=0, bytes_accessed=4 * width * width),
        name="order_out",
    )(place, *blocks)
    return out.reshape(-1, width)


ROW_TILE = 512


def pick_rows_kernel(ids_ref, *refs):
    count = len(refs) - 2
    to_ref, total = refs[count:]
    chunk = pl.program_id(0)
    ids = ids_ref[...] - chunk * ROW_TILE
    hit = ids == lax.broadcasted_iota(jnp.int32, (ids.shape[0], ROW_TILE), 1)
    ones = jnp.where(hit, 1.0, 0.0).astype(BF16)
    for i in range(count):
        found = mm(ones, refs[i][...], NN)

        @pl.when(chunk == 0)
        def _():
            total[i] = found

        @pl.when(chunk > 0)
        def _():
            total[i] += found

        @pl.when(chunk == pl.num_programs(0) - 1)
        def _():
            to_ref[i] = total[i].astype(BF16)


def pick_rows(sources, ids):
    length, width = sources[0].shape
    rows = ids.shape[0]
    count = len(sources)
    return pl.pallas_call(
        pick_rows_kernel,
        grid=(length // ROW_TILE,),
        in_specs=[pl.BlockSpec((rows, 1), lambda c: (0, 0))]
        + [pl.BlockSpec((ROW_TILE, width), lambda c: (c, 0))] * count,
        out_specs=pl.BlockSpec((count, rows, width), lambda c: (0, 0, 0)),
        out_shape=jax.ShapeDtypeStruct((count, rows, width), BF16),
        scratch_shapes=[pltpu.VMEM((count, rows, width), F32)],
        compiler_params=pltpu.CompilerParams(vmem_limit_bytes=VMEM_LIMIT),
        cost_estimate=pl.CostEstimate(
            flops=2 * count * rows * length * width,
            transcendentals=0,
            bytes_accessed=2 * count * length * width,
        ),
        name="pick_rows",
    )(ids[:, None], *sources)


def place_rows_kernel(ids_ref, new_ref, from_ref, to_ref):
    ids = ids_ref[...] - pl.program_id(0) * ROW_TILE
    hit = ids == lax.broadcasted_iota(jnp.int32, (ROW_TILE, ids.shape[1]), 0)
    ones = jnp.where(hit, 1.0, 0.0)
    routed = jnp.max(ones, axis=1, keepdims=True) > 0.0
    new = mm(ones.astype(BF16), new_ref[...], NN).astype(BF16)
    to_ref[...] = jnp.where(routed, new, from_ref[...])


def place_rows(source, ids, new):
    length, width = source.shape
    rows = ids.shape[0]
    tiles = pl.BlockSpec((ROW_TILE, width), lambda c: (c, 0))
    return pl.pallas_call(
        place_rows_kernel,
        grid=(length // ROW_TILE,),
        in_specs=[
            pl.BlockSpec((1, rows), lambda c: (0, 0)),
            pl.BlockSpec((rows, width), lambda c: (0, 0)),
            tiles,
        ],
        out_specs=tiles,
        out_shape=jax.ShapeDtypeStruct((length, width), BF16),
        compiler_params=pltpu.CompilerParams(vmem_limit_bytes=VMEM_LIMIT),
        cost_estimate=pl.CostEstimate(
            flops=2 * rows * length * width, transcendentals=0, bytes_accessed=4 * length * width
        ),
        name="place_rows",
    )(ids[None, :], new, source)


def half_lanes(values, half):
    lane = lax.broadcasted_iota(jnp.int32, values.shape, 1)
    keep = lane < HD if half == 0 else lane >= HD
    return jnp.where(keep, values, jnp.zeros_like(values))


def allowed_tile(keys_ref, where, pos_row, start_row):
    keys = keys_ref[where]
    return (keys <= pos_row) & (keys >= start_row)


def attention_forward_kernel(
    window_ref, place_ref, first_ref, q_ref, k_ref, v_ref, pos_ref, start_ref, keys_ref, o_ref, lse_ref
):
    block = pl.program_id(0)
    tile, width = q_ref.shape
    heads = width // HD
    pos_row, start_row = pos_ref[0], start_ref[0]
    last = window_ref[block]
    count = last - first_ref[block] + 1
    lanes = [slice(h // 2 * PAIR, (h // 2 + 1) * PAIR) for h in range(heads)]
    scale = jnp.asarray(HD**-0.5, BF16)
    queries = [half_lanes(q_ref[:, lanes[h]] * scale, h % 2) for h in range(heads)]

    def step(i, carry):
        where = place_ref[last - i]
        allowed = allowed_tile(keys_ref, where, pos_row, start_row)
        each = range(heads)
        raw = [mm(k_ref[where, :, lanes[h]], queries[h], NT) for h in each]
        scores = [jnp.where(allowed, raw[h], NEG_FILL) for h in each]
        tops = [jnp.maximum(carry[h][0], jnp.max(scores[h], axis=0, keepdims=True)) for h in each]
        exponents = [jnp.exp(scores[h] - tops[h]) for h in each]
        values = [mm(v_ref[where, :, lanes[h]], exponents[h].astype(BF16), TN) for h in each]
        shrinks = [jnp.exp(carry[h][0] - tops[h]) for h in each]
        sums = [jnp.sum(exponents[h], axis=0, keepdims=True) for h in each]
        return tuple(
            (tops[h], carry[h][1] * shrinks[h] + sums[h], carry[h][2] * shrinks[h] + values[h])
            for h in each
        )

    empty = (jnp.full((1, tile), NEG_FILL, F32), jnp.zeros((1, tile), F32), jnp.zeros((PAIR, tile), F32))
    done = lax.fori_loop(0, count, step, (empty,) * heads)
    for h in range(0, heads, 2):
        pair = [acc * (1.0 / total) for _, total, acc in done[h : h + 2]]
        joined = jnp.concatenate([pair[0][:HD], pair[1][HD:]], axis=0)
        o_ref[:, lanes[h]] = joined.T.astype(BF16)
    row = lax.broadcasted_iota(jnp.int32, (8, tile), 0)
    lse = jnp.zeros((8, tile), F32)
    for h, (top, total, _) in enumerate(done):
        lse = jnp.where(row == h, top + jnp.log(total), lse)
    lse_ref[...] = lse


def attention_backward_kernel(
    window_ref,
    place_ref,
    first_ref,
    q_ref,
    k_ref,
    v_ref,
    g_ref,
    o_ref,
    lse_ref,
    pos_ref,
    start_ref,
    keys_ref,
    grad_ref,
    dk_sum,
    dv_sum,
):
    block = pl.program_id(0)
    tile, width = q_ref.shape
    heads = width // HD
    pos_row, start_row = pos_ref[0], start_ref[0]
    last = window_ref[block]
    count = last - first_ref[block] + 1
    lanes = [slice(h // 2 * PAIR, (h // 2 + 1) * PAIR) for h in range(heads)]
    scale = HD**-0.5

    @pl.when(block == 0)
    def _():
        dk_sum[...] = jnp.zeros_like(dk_sum)
        dv_sum[...] = jnp.zeros_like(dv_sum)

    queries = [half_lanes(q_ref[:, lanes[h]] * jnp.asarray(scale, BF16), h % 2) for h in range(heads)]
    grads = [half_lanes(g_ref[:, lanes[h]], h % 2) for h in range(heads)]
    inner = []
    for h in range(0, heads, 2):
        both = (g_ref[:, lanes[h]].astype(F32) * o_ref[:, lanes[h]].astype(F32)).T
        inner += [jnp.sum(part, axis=0, keepdims=True) for part in (both[:HD], both[HD:])]

    def step(i, carry):
        where = place_ref[last - i]
        allowed = allowed_tile(keys_ref, where, pos_row, start_row)
        each = range(heads)
        keys = [k_ref[where, :, lanes[h]] for h in each]
        scores = [mm(keys[h], queries[h], NT) for h in each]
        grad_prob = [mm(v_ref[where, :, lanes[h]], grads[h], NT) for h in each]
        prob = [jnp.where(allowed, jnp.exp(scores[h] - lse_ref[h : h + 1, :]), 0.0) for h in each]
        grad_scores = [(prob[h] * (grad_prob[h] - inner[h])).astype(BF16) for h in each]
        values = [mm(prob[h].astype(BF16), grads[h], NN) for h in each]
        moved = [mm(grad_scores[h], queries[h], NN) for h in each]
        for h in range(0, heads, 2):
            dv_sum[where, :, lanes[h]] += values[h] + values[h + 1]
            dk_sum[where, :, lanes[h]] += moved[h] + moved[h + 1]
        return tuple(carry[h] + mm(keys[h], grad_scores[h], TN) for h in each)

    done = lax.fori_loop(0, count, step, (jnp.zeros((PAIR, tile), F32),) * heads)
    for h in range(0, heads, 2):
        joined = jnp.concatenate([done[h][:HD], done[h + 1][HD:]], axis=0) * scale
        at = 2 * width + h * HD
        grad_ref[block, :, at : at + PAIR] = joined.T.astype(BF16)

    @pl.when(block == pl.num_programs(0) - 1)
    def _():
        grad_ref[:, :, :width] = dk_sum[...].astype(BF16)
        grad_ref[:, :, width : 2 * width] = dv_sum[...].astype(BF16)


def attention_specs(blocks, tile, width):
    by_rows = pl.BlockSpec((tile, width), lambda b, *_: (b, 0))
    keys = lambda at: pl.BlockSpec((blocks, tile, width), lambda b, *_: (0, 0, at))
    row = pl.BlockSpec((1, 1, tile), lambda b, *_: (b, 0, 0))
    lse = pl.BlockSpec((8, tile), lambda b, *_: (0, b))
    return by_rows, keys, row, lse, pl.BlockSpec((blocks, tile, 1), lambda b, *_: (0, 0, 0))


def attention_forward(tables, q, kv, pos, start, tile):
    rows, width = q.shape
    blocks = rows // tile
    by_rows, keys, row, lse, cols = attention_specs(blocks, tile, width)
    return pl.pallas_call(
        attention_forward_kernel,
        grid_spec=pltpu.PrefetchScalarGridSpec(
            num_scalar_prefetch=3,
            grid=(blocks,),
            in_specs=[by_rows, keys(0), keys(1), row, row, cols],
            out_specs=[by_rows, lse],
        ),
        out_shape=[jax.ShapeDtypeStruct((rows, width), BF16), jax.ShapeDtypeStruct((8, rows), F32)],
        compiler_params=pltpu.CompilerParams(vmem_limit_bytes=VMEM_LIMIT),
        cost_estimate=pl.CostEstimate(
            flops=2 * rows * rows * width,
            transcendentals=rows * rows * width // HD // 2,
            bytes_accessed=8 * rows * width,
        ),
        name="attention_forward",
    )(
        *tables,
        q,
        kv.reshape(blocks, tile, 2 * width),
        kv.reshape(blocks, tile, 2 * width),
        pos.reshape(blocks, 1, tile),
        start.reshape(blocks, 1, tile),
        pos.reshape(blocks, tile, 1),
    )


def attention_backward(tables, q, kv, grad, out, lse_rows, pos, start, tile):
    rows, width = q.shape
    blocks = rows // tile
    by_rows, keys, row, lse, cols = attention_specs(blocks, tile, width)
    grads = pl.pallas_call(
        attention_backward_kernel,
        grid_spec=pltpu.PrefetchScalarGridSpec(
            num_scalar_prefetch=3,
            grid=(blocks,),
            in_specs=[by_rows, keys(0), keys(1), by_rows, by_rows, lse, row, row, cols],
            out_specs=pl.BlockSpec((blocks, tile, 3 * width), lambda b, *_: (0, 0, 0)),
            scratch_shapes=[pltpu.VMEM((blocks, tile, width), F32)] * 2,
        ),
        out_shape=jax.ShapeDtypeStruct((blocks, tile, 3 * width), BF16),
        compiler_params=pltpu.CompilerParams(vmem_limit_bytes=VMEM_LIMIT),
        cost_estimate=pl.CostEstimate(
            flops=5 * rows * rows * width,
            transcendentals=rows * rows * width // HD // 2,
            bytes_accessed=14 * rows * width,
        ),
        name="attention_backward",
    )(
        *tables,
        q,
        kv.reshape(blocks, tile, 2 * width),
        kv.reshape(blocks, tile, 2 * width),
        grad,
        out,
        lse_rows,
        pos.reshape(blocks, 1, tile),
        start.reshape(blocks, 1, tile),
        pos.reshape(blocks, tile, 1),
    )
    return grads.reshape(rows, 3 * width)


def whole_spec(shape):
    return pl.BlockSpec(shape, lambda i, *_: (0,) * len(shape))


def one_step(kernel, name, place, args, out_shape, flops):
    size = lambda x: x.size * x.dtype.itemsize
    return pl.pallas_call(
        kernel,
        grid_spec=pltpu.PrefetchScalarGridSpec(
            num_scalar_prefetch=1,
            grid=(1,),
            in_specs=[whole_spec(x.shape) for x in args],
            out_specs=[whole_spec(x.shape) for x in out_shape],
        ),
        out_shape=out_shape,
        compiler_params=pltpu.CompilerParams(vmem_limit_bytes=VMEM_LIMIT),
        cost_estimate=pl.CostEstimate(
            flops=flops, transcendentals=0, bytes_accessed=sum(size(x) for x in (*args, *out_shape))
        ),
        name=name,
    )(place, *args)


def norm_scale(values):
    return lax.rsqrt(jnp.mean(values * values, axis=1, keepdims=True) + EPS)


def first_shard_kernel(place_ref, q_ref, k_ref, v_ref, vec_ref, out_ref, own_ref):
    rows, span = q_ref.shape
    for i, ref in enumerate((k_ref, v_ref, q_ref)):
        own_ref[:rows, i * span : (i + 1) * span] = ref[...]
    lines = out_ref.shape[1]
    for j in range(out_ref.shape[2] // span):
        own_ref[j * lines : (j + 1) * lines, 3 * span :] = out_ref[0, :, j * span : (j + 1) * span]
    own_ref[rows:, :] = jnp.zeros((own_ref.shape[0] - rows, own_ref.shape[1]), BF16)
    own_ref[rows:, : vec_ref.shape[1]] = vec_ref[...]


def first_shard(place, qkv, vectors, out, span):
    rows, width = out.shape
    seqs = width // span
    out = out.reshape(seqs, rows // seqs, width)
    heads = lambda i: pl.BlockSpec((rows, span), lambda g, at: (0, i * seqs + at[1]))
    shape = (rows + vectors.shape[0], 4 * span)
    return pl.pallas_call(
        first_shard_kernel,
        grid_spec=pltpu.PrefetchScalarGridSpec(
            num_scalar_prefetch=1,
            grid=(1,),
            in_specs=[
                heads(0),
                heads(1),
                heads(2),
                pl.BlockSpec(vectors.shape, lambda g, at: (0, 0)),
                pl.BlockSpec((1, rows // seqs, width), lambda g, at: (at[1], 0, 0)),
            ],
            out_specs=pl.BlockSpec(shape, lambda g, at: (0, 0)),
        ),
        out_shape=jax.ShapeDtypeStruct(shape, BF16),
        compiler_params=pltpu.CompilerParams(vmem_limit_bytes=VMEM_LIMIT),
        cost_estimate=pl.CostEstimate(
            flops=0, transcendentals=0, bytes_accessed=4 * shape[0] * shape[1]
        ),
        name="first_shard",
    )(place, qkv, qkv, qkv, vectors, out)


def hidden_shard_kernel(place_ref, up_ref, down_ref, both_ref):
    rows = up_ref.shape[0]
    both_ref[:rows, :] = up_ref[...]
    both_ref[rows:, :] = down_ref[...]


def hidden_shard(place, up, down, span):
    rows, width = up.shape[0], down.shape[1]
    seqs = lax.axis_size("seq")
    return pl.pallas_call(
        hidden_shard_kernel,
        grid_spec=pltpu.PrefetchScalarGridSpec(
            num_scalar_prefetch=1,
            grid=(width // span,),
            in_specs=[
                pl.BlockSpec((rows, span), lambda i, at: (0, i * seqs + at[1])),
                pl.BlockSpec((span, span), lambda i, at: (at[1], i)),
            ],
            out_specs=pl.BlockSpec((rows + span, span), lambda i, at: (0, i)),
        ),
        out_shape=jax.ShapeDtypeStruct((rows + span, width), BF16),
        compiler_params=pltpu.CompilerParams(vmem_limit_bytes=VMEM_LIMIT),
        cost_estimate=pl.CostEstimate(flops=0, transcendentals=0, bytes_accessed=8 * rows * width),
        name="hidden_shard",
    )(place, up, down)


def project_kernel(place_ref, *refs, seqs, slow, fast):
    x_refs, pieces = refs[:seqs], refs[seqs:-7]
    out_ref, w_ref, vec_ref, normal_ref, q_ref, kv_ref, rate_ref = refs[-7:]
    span = q_ref.shape[1]
    per = w_ref.shape[0] // (slow * fast)
    lines = out_ref.shape[1]
    done = 0
    for ref in pieces:
        for i in range(ref.shape[0]):
            block = done % slow * fast + done // slow
            shard = place_ref[0] ^ block
            here = pl.ds(pl.multiple_of(shard * per, per), per)
            w_ref[here, : 3 * span] = ref[i, :per, : 3 * span]
            extra = ref[i, per:, :LANES].astype(F32)
            square = jnp.concatenate([extra, jnp.zeros((LANES - extra.shape[0], LANES), F32)], axis=0)
            w_ref[here, 3 * span :] = square.T[:per].astype(BF16)
            for j in range(seqs):
                out_ref[block, :, j * span : (j + 1) * span] = ref[i, j * lines : (j + 1) * lines, 3 * span :]
            done += 1
    tails = w_ref[:, 3 * span :]
    vec = tails.astype(F32).T
    vec_ref[...] = vec[:8]
    gain = vec[1:2]
    weight = w_ref[:, : 3 * span]
    rows = x_refs[0].shape[1]
    for k in range(seqs):
        here = slice(k * rows, (k + 1) * rows)
        x = x_refs[k][0]
        x_f = x.astype(F32)
        normal = (x_f * norm_scale(x_f) * gain).astype(BF16)
        normal_ref[here, :] = normal
        proj = mm(normal, weight, NN).astype(BF16)
        kv_ref[here, :] = proj[:, : 2 * span]
        q_ref[here, :] = proj[:, 2 * span :]
        rate_ref[here, :] = jax.nn.sigmoid(mm(x, tails, NN)[:, :1])


def project(place, x_blocks, pieces, span):
    slow, fast = fsdp_sizes()
    _, rows, width = x_blocks[0].shape
    total = rows * len(x_blocks)
    cols = 3 * span + LANES
    out_shape = [
        jax.ShapeDtypeStruct((slow * fast, width // (slow * fast * len(x_blocks)), width), BF16),
        jax.ShapeDtypeStruct((width, cols), BF16),
        jax.ShapeDtypeStruct((8, width), F32),
        jax.ShapeDtypeStruct((total, width), BF16),
        jax.ShapeDtypeStruct((total, span), BF16),
        jax.ShapeDtypeStruct((total, 2 * span), BF16),
        jax.ShapeDtypeStruct((total, 1), F32),
    ]
    kernel = partial(project_kernel, seqs=len(x_blocks), slow=slow, fast=fast)
    return one_step(
        kernel, "project", place, [*x_blocks, *pieces], out_shape, 2 * total * width * cols
    )


def branch_kernel(place_ref, *refs, seqs):
    x_refs, att_refs = refs[:seqs], refs[seqs : 2 * seqs]
    w_ref, vec_ref, rate_ref, branch_ref, normal_ref, carried_ref = refs[2 * seqs :]
    rows = x_refs[0].shape[1]
    span = att_refs[0].shape[1]
    gain = vec_ref[2:3, :]
    for j in range(seqs):
        here = slice(j * rows, (j + 1) * rows)
        branch = 0.0
        for b in range(seqs):
            there = slice((j ^ b) * rows, ((j ^ b) + 1) * rows)
            branch = branch + mm(att_refs[b][there, :], w_ref[b * span : (b + 1) * span, :], NN)
        if j == 0:
            branch_ref[...] = branch
        middle = x_refs[j][0].astype(F32) + branch
        normal_ref[here, :] = (middle * norm_scale(middle) * gain).astype(BF16)
        carried_ref[here, :] = (rate_ref[here, :] * x_refs[j][1].astype(F32)).astype(BF16)


def attention_branch(place, blocks, att_blocks, w_out, vectors, rate):
    _, rows, width = blocks[0].shape
    seqs = len(blocks)
    out_shape = [
        jax.ShapeDtypeStruct((rows, width), F32),
        jax.ShapeDtypeStruct((rows * seqs, width), BF16),
        jax.ShapeDtypeStruct((rows * seqs, width), BF16),
    ]
    args = [*blocks, *att_blocks, w_out, vectors, rate]
    return one_step(
        partial(branch_kernel, seqs=seqs),
        "attention_branch",
        place,
        args,
        out_shape,
        2 * rows * seqs * width * width,
    )


def attention_grad_kernel(place_ref, *refs, seqs):
    w_ref, joined_ref, out_ref = refs[seqs:]
    rows = refs[0].shape[0]
    for j in range(seqs):
        here = slice(j * rows, (j + 1) * rows)
        block = refs[j][...]
        joined_ref[here, :] = block
        out_ref[here, :] = mm(block, w_ref[...], NT).astype(BF16)


def attention_grad(place, blocks, w_out):
    rows, width = blocks[0].shape
    total = rows * len(blocks)
    span = w_out.shape[0]
    out_shape = [jax.ShapeDtypeStruct((total, width), BF16), jax.ShapeDtypeStruct((total, span), BF16)]
    return one_step(
        partial(attention_grad_kernel, seqs=len(blocks)),
        "attention_grad",
        place,
        [*blocks, w_out],
        out_shape,
        2 * total * width * span,
    )


def norm_back(values, scale, gain, grad):
    weighted = grad * gain
    inner = jnp.mean(weighted * values, axis=1, keepdims=True)
    return scale * weighted - values * (scale * scale * scale) * inner


def shards(
    inputs,
    cotangent,
    routed,
    doc_starts,
    router,
    attn_gain,
    qkv_weight,
    out_weight,
    mlp_gain,
    up_weight,
    down_weight,
):
    seqs = lax.axis_size("seq")
    fsdps = lax.axis_size("fsdp")
    me = lax.axis_index("seq")
    width = inputs.shape[2]
    tok_count = inputs.shape[1]
    own_windows = tok_count // WIN
    windows = routed.shape[1]
    tile = routed.shape[2]
    own_rows = own_windows * tile
    rows = windows * tile
    heads_width = width // seqs
    hidden = up_weight.shape[1]
    own_hidden = hidden // seqs

    order = jnp.arange(seqs, dtype=jnp.int32) ^ me
    window_of = (order[:, None] * own_windows + jnp.arange(own_windows, dtype=jnp.int32)).reshape(-1)
    stream_pos = jnp.arange(windows, dtype=jnp.int32)[:, None] * WIN + routed[0]
    pos = stream_pos[window_of].reshape(-1)
    starts = doc_starts[0]
    start = jnp.max(jnp.where(starts[None, :] <= pos[:, None], starts[None, :], 0), axis=1)
    first_window = start.reshape(windows, tile)[:, 0] // WIN
    place_of = jnp.zeros((windows,), jnp.int32).at[window_of].set(jnp.arange(windows, dtype=jnp.int32))
    tables = (window_of, place_of, first_window)

    own_routes = lax.dynamic_slice_in_dim(routed[0], me * own_windows, own_windows, 0)
    row_ids = ((jnp.arange(own_windows, dtype=jnp.int32) * WIN)[:, None] + own_routes).reshape(-1)
    stream_in = inputs[0]
    grad_in = cotangent[0]

    place = jnp.stack([lax.axis_index("fsdp"), me])
    vectors = jnp.stack([router, attn_gain, mlp_gain])
    vectors = jnp.pad(vectors, ((0, 8 - vectors.shape[0]), (0, LANES - vectors.shape[1])))
    first_own = first_shard(place, qkv_weight, vectors, out_weight, heads_width)
    first_slow = gather_slow(first_own)
    first_got = own_fast(first_slow[0])
    picked = pick_rows([stream_in, grad_in], after(row_ids, first_own))

    span = down_weight.shape[0] // seqs
    square = own_hidden == width and span % LANES == 0
    shard_rows = up_weight.shape[0]
    if square:
        hidden_own = hidden_shard(place, after(up_weight, picked, *first_got), down_weight, span)
        hidden_late = after(hidden_own, *first_slow[1:])
        hidden_all = lax.all_gather(hidden_late, "fsdp", axis=0)
        w_up = hidden_all[:, :shard_rows].reshape(width, own_hidden)
        w_down = hidden_all[:, shard_rows:].reshape(own_hidden, width)
    else:
        hidden_own = lax.dynamic_index_in_dim(
            up_weight.reshape(-1, fsdps, seqs, span), me, axis=2, keepdims=False
        ).reshape(-1, own_hidden)
        down_own = lax.dynamic_slice_in_dim(down_weight, me * span, span, 0)
        w_up = lax.all_gather(hidden_own, "fsdp", axis=0, tiled=True)
        w_down = lax.all_gather(down_own, "fsdp", axis=0, tiled=True)
    first_pieces = gather_fast(first_slow[0], after(tuple(first_slow[1:]), hidden_own), first_got)
    blocks = gather_blocks(picked, "seq", first_pieces[-1])
    out_part, w_qkv, vectors, normal_a, q, kv, rate = project(
        place, blocks, first_pieces, heads_width
    )
    router_w, gain_a, gain_m = vectors[0:1], vectors[1:2], vectors[2:3]
    tail_at = 3 * heads_width // LANES
    att_own, lse = attention_forward(tables, q, kv, pos, start, tile)
    out_blocks = gather_blocks(out_part, "seq", att_own)
    out_ordered = order_out(place, out_blocks)
    att_blocks = gather_blocks(att_own, "seq", out_ordered)
    w_out = out_ordered[:heads_width]
    branch_o, normal_m, carried_b = attention_branch(
        place, blocks, att_blocks, out_ordered, vectors, rate
    )
    pre_act = mm(normal_m, w_up, NN)
    cdf = 0.5 * (1.0 + lax.erf(pre_act * (0.5**0.5)))
    activated = (pre_act * cdf).astype(BF16)
    slope = cdf + pre_act * (jnp.exp(-0.5 * pre_act * pre_act) * (2.0 * jnp.pi) ** -0.5)

    grad_act = mm(carried_b, w_down, NT)
    grad_pre = (grad_act * slope).astype(BF16)
    cut = lambda a, b: a[b * own_rows : (b + 1) * own_rows]
    normal_grads = [mm(cut(grad_pre, b), w_up, NT) for b in range(seqs)]
    grad_normal_m = scatter_blocks(normal_grads, "seq")
    flat = place * jnp.array([1, 0], jnp.int32)
    scatter = lambda g: lax.psum_scatter(g, "fsdp", scatter_dimension=0)
    activated_late = after(activated, *normal_grads)
    if square:
        both, gains = hidden_grads(
            place, activated_late, carried_b, normal_m, grad_pre, w_up, w_qkv, tail_at, 2
        )
        grad_normal_m = after(grad_normal_m, both)
        both = scatter(both)
        up_part, down_part = both[0].reshape(seqs, -1, own_hidden), both[1]
    else:
        (down_grad,) = weight_grad(flat, activated_late, carried_b, 1, None)
        up_grad, gains = weight_grad(
            place,
            normal_m,
            grad_pre,
            seqs,
            None,
            (w_up, 0, w_qkv, tail_at, 2, jnp.zeros((width, LANES), F32)),
        )
        up_part, down_part = scatter(up_grad), scatter(down_grad)[0]

    x_o = picked[0].astype(F32)
    g_o = picked[1].astype(F32)
    rate_o = cut(rate, 0)
    middle_o = x_o + branch_o
    grad_middle = norm_back(middle_o, norm_scale(middle_o), gain_m, grad_normal_m)
    grad_a_own = (rate_o * g_o + grad_middle).astype(BF16)
    grad_a_blocks = gather_blocks(grad_a_own, "seq")
    branch_parts = [mm(cut(after(activated, grad_a_blocks[1]), b), w_down, NN) for b in range(seqs)]
    branch_f = scatter_blocks(branch_parts, "seq", grad_a_blocks[-1])
    grad_a, grad_att = attention_grad(place, grad_a_blocks, w_out)
    fast = 1
    slow = fsdp_sizes()[1]
    out_send, out_keep = weight_grad(flat, att_own, after(grad_a, *branch_parts), 1, fast)
    grad_proj = attention_backward(
        tables, q, kv, after(grad_att, out_send), att_own, lse, pos, start, tile
    )
    kv_send, kv_keep, gains = weight_grad(
        place,
        normal_a,
        grad_proj,
        seqs,
        fast,
        (w_qkv, 0, w_qkv, tail_at, 1, gains),
        cols=2 * heads_width,
    )
    branch_sum = branch_o + branch_f
    result = x_o + rate_o * branch_sum
    grad_logit = jnp.sum(g_o * branch_sum, axis=1, keepdims=True) * rate_o * (1.0 - rate_o)
    logit_high = grad_logit.astype(BF16)
    logit_low = (grad_logit - logit_high.astype(F32)).astype(BF16)
    lane = jnp.arange(LANES)[None, :]
    logits = jnp.where(lane == 0, logit_high, jnp.where(lane == 3, logit_low, jnp.zeros((), BF16)))
    q_send, q_keep = weight_grad(
        place,
        after(normal_a, kv_send),
        grad_proj,
        seqs,
        slow,
        (w_qkv, 2, w_qkv, tail_at, 1, gains),
        (picked[0], logits),
        cols=heads_width,
        at_b=2,
    )
    out_sum = reduce_blocks(out_send, out_keep, fast, [(q_send,)])[0]
    kv_part = reduce_blocks(kv_send, kv_keep, fast, [()])
    q_part = reduce_blocks(q_send, q_keep, slow, [()])
    proj_late = after(grad_proj, q_send)
    w_proj = w_qkv[:, : 3 * heads_width]
    grad_normal_a = scatter_blocks([mm(cut(proj_late, b), w_proj, NT) for b in range(seqs)], "seq")
    output = place_rows(stream_in, row_ids, after(result.astype(BF16), q_send))
    grad_norm_x = norm_back(x_o, norm_scale(x_o), gain_a, grad_normal_a)
    grad_picked = g_o + grad_middle + grad_norm_x + grad_logit * router_w
    input_grad = place_rows(grad_in, row_ids, grad_picked.astype(BF16))
    down_sum = lax.ppermute(
        down_part,
        ("seq", "fsdp"),
        [
            (s * fsdps + down_slot(f, fsdps, seqs), f * seqs + s)
            for s in range(seqs)
            for f in range(fsdps)
        ],
    ).astype(F32)
    qkv_part = jnp.concatenate(
        [q_part[:, :, :heads_width], kv_part, q_part[:, :, heads_width:]], axis=2
    )
    up_sum, qkv_sum, tiny = exchange_columns(up_part, qkv_part, span, heads_width)
    return (
        output[None],
        input_grad[None],
        tiny[:, 0] + tiny[:, 3],
        tiny[:, 1],
        qkv_sum,
        out_sum,
        tiny[:, 2],
        up_sum,
        down_sum,
    )


def solution(mesh):
    return jax.shard_map(
        shards,
        mesh=mesh,
        in_specs=(
            P("fsdp", "seq", None),
            P("fsdp", "seq", None),
            P("fsdp", None, None),
            P("fsdp", None),
            P("fsdp"),
            P("fsdp"),
            P("fsdp", None),
            P("fsdp", None),
            P("fsdp"),
            P("fsdp", None),
            P("fsdp", None),
        ),
        out_specs=(
            P("fsdp", "seq", None),
            P("fsdp", "seq", None),
            P(("seq", "fsdp")),
            P(("seq", "fsdp")),
            P(("seq", "fsdp"), None),
            P(("seq", "fsdp"), None),
            P(("seq", "fsdp")),
            P(("seq", "fsdp"), None),
            P(("seq", "fsdp"), None),
        ),
        check_vma=False,
    )
```

```python
from functools import partial

import jax
import jax.numpy as jnp
from jax import lax
from jax.experimental import pallas as pl
from jax.experimental.pallas import tpu as pltpu
from jax.sharding import PartitionSpec as P

H = 16
HD = 64
WIN = 2048
EPS = 1e-05
NEG_FILL = -1e30
PAIR = 2 * HD
LANES = 128
BF16 = jnp.bfloat16
F32 = jnp.float32
VMEM_LIMIT = 48 * 1024 * 1024
GRAD_LIMIT = 28 * 1024 * 1024


def mm(a, b, dims):
    return lax.dot_general(a, b, (dims, ((), ())), preferred_element_type=F32)


NN = ((1,), (0,))
NT = ((1,), (1,))
TN = ((0,), (0,))


def flip(values, axis, bit):
    count = lax.axis_size(axis)
    return lax.ppermute(values, axis, [(j, j ^ bit) for j in range(count)])


def bits_down(count):
    bit = count // 2
    while bit:
        yield bit
        bit //= 2


def gather_blocks(own, axis, *waits):
    blocks = {0: own}
    top = lax.axis_size(axis) // 2
    for bit in bits_down(lax.axis_size(axis)):
        for key in list(blocks):
            block = after(blocks[key], *waits) if key else blocks[key]
            blocks[key ^ bit] = flip(block, axis, bit)
    return [blocks[key] for key in sorted(blocks)]


def scatter_blocks(blocks, axis, *waits):
    parts = dict(enumerate(blocks))
    bit = 1
    while bit < lax.axis_size(axis):
        for key in [k for k in parts if k & bit]:
            part = parts.pop(key).astype(BF16)
            got = flip(part if bit == 1 else after(part, *waits), axis, bit)
            parts[key ^ bit] = parts[key ^ bit] + got.astype(F32)
        bit *= 2
    return parts[0]


def after(values, *earlier):
    earlier = [e for e in earlier if e is not None]
    return lax.optimization_barrier((values, *earlier))[0] if earlier else values


def fsdp_sizes():
    count = lax.axis_size("fsdp")
    fast = 2 ** ((count.bit_length() - 1) // 2)
    return count // fast, fast


def gather_slow(own, *waits):
    slow, fast = fsdp_sizes()
    own_late = after(own, *waits)
    return [own_late] + [flip(own_late, "fsdp", k * fast) for k in range(1, slow)]


def own_fast(own):
    _, fast = fsdp_sizes()
    return [flip(own[None], "fsdp", k) for k in range(1, fast)]


def gather_fast(own, others, own_got):
    _, fast = fsdp_sizes()
    others = jnp.stack(others)
    pieces = [own[None], others]
    for k in range(1, fast):
        pieces += [own_got[k - 1], flip(others, "fsdp", k)]
    return pieces


def low_bits(count):
    bit = 1
    while bit < count:
        yield bit
        bit *= 2


def reduce_blocks(send, keep, first, waits):
    bits = [first] + [b for b in low_bits(lax.axis_size("fsdp")) if b != first]
    total = None
    for i, bit in enumerate(bits):
        got = flip(send, "fsdp", bit)
        total = keep.astype(F32) + got.astype(F32)
        if bit != bits[-1]:
            send = after(total[1::2].astype(BF16), *waits[min(i, len(waits) - 1)])
            keep = total[0::2]
    return total[0]


def join_columns_kernel(me_ref, *refs, up_span, span):
    up_ref, qkv_ref, tail_ref = refs[-3:]
    count = len(refs) - 3
    own_hidden = up_ref.shape[1] // count
    tail = 0.0
    for k in range(count):
        block = refs[k][...].astype(F32)
        at = me_ref[0] ^ k
        for ref, first, groups, cols in ((up_ref, 0, own_hidden // up_span, up_span), (qkv_ref, own_hidden, 3, span)):
            for g in range(groups):
                start = pl.multiple_of((g * count + at) * cols, cols)
                ref[:, pl.ds(start, cols)] = block[:, first + g * cols : first + (g + 1) * cols]
        tail = tail + block[:, own_hidden + 3 * span :]
    tail_ref[...] = tail


def exchange_columns(up, qkv, up_span, span):
    count, rows, own_hidden = up.shape
    both = jnp.concatenate([up.astype(BF16), qkv.astype(BF16)], axis=2)
    got = [both[0]] + [flip(both[k], "seq", k) for k in range(1, count)]
    shapes = [(rows, count * own_hidden), (rows, 3 * count * span), (rows, LANES)]
    if up_span % LANES:
        me = lax.axis_index("seq")
        groups = own_hidden // up_span
        joined = jnp.zeros((rows, groups, count, up_span), F32)
        for k in range(count):
            part = got[k][:, :own_hidden].astype(F32).reshape(rows, groups, 1, up_span)
            joined = lax.dynamic_update_slice_in_dim(joined, part, me ^ k, axis=2)
        alone = [g[:, own_hidden:] for g in got]
        zero = [jnp.concatenate([jnp.zeros((rows, LANES), BF16), a], axis=1) for a in alone]
        rest = join_columns(zero, [(rows, count * LANES), *shapes[1:]], LANES, span)
        return (joined.reshape(rows, -1), *rest[1:])
    return join_columns(got, shapes, up_span, span)


def join_columns(got, shapes, up_span, span):
    whole = lambda shape: pl.BlockSpec(shape, lambda i, *_: (0, 0))
    return pl.pallas_call(
        partial(join_columns_kernel, up_span=up_span, span=span),
        grid_spec=pltpu.PrefetchScalarGridSpec(
            num_scalar_prefetch=1,
            grid=(1,),
            in_specs=[whole(got[0].shape)] * len(got),
            out_specs=[whole(shape) for shape in shapes],
        ),
        out_shape=[jax.ShapeDtypeStruct(shape, F32) for shape in shapes],
        compiler_params=pltpu.CompilerParams(vmem_limit_bytes=VMEM_LIMIT),
        name="join_columns",
    )(lax.axis_index("seq")[None], *got)


GRAD_TILE = 512


def down_slot(shard, fsdps, seqs):
    group = fsdps // seqs
    return shard % group * seqs + shard // group


def store_blocks(product, tail, column, place_ref, per, fsdps, seqs, first, refs):
    whole = product.astype(BF16)
    cols = product.shape[1]
    pieces = product.shape[0] // per
    for t in range(pieces):
        piece = column * pieces + t
        block = lax.rem(piece, fsdps)
        part = lax.div(piece, fsdps) ^ place_ref[1]
        rows = slice(t * per, (t + 1) * per)

        def store(ref, slot):
            ref[slot, part, :, :cols] = whole[rows]
            if tail is not None:
                ref[slot, part, :, cols:] = tail[rows]

        if first is None:
            alone = refs[0].shape[1] == 1
            store(refs[0], down_slot(block, fsdps, seqs) if alone else block)
            continue
        block = block ^ place_ref[0]
        slot = lax.div(block, 2 * first) * first + lax.rem(block, first)
        sent = lax.rem(lax.div(block, first), 2)
        pl.when(sent == 1)(partial(store, refs[0], slot))
        pl.when(sent == 0)(partial(store, refs[1], slot))


def weight_grad_kernel(place_ref, a_ref, b_ref, *refs, per, fsdps, seqs, first, gain_lane, with_logits, tail_out):
    column = pl.program_id(0)
    product = mm(a_ref[...], b_ref[...], TN)
    refs = list(refs)
    tail = None
    if gain_lane is not None:
        w_ref, vec_ref, other_ref = refs[:3]
        refs = refs[3:]
        lane = lax.broadcasted_iota(jnp.int32, (product.shape[0], LANES), 1)
        gain = vec_ref[...].astype(F32)[:, gain_lane : gain_lane + 1]
        gain_grad = jnp.sum(product * w_ref[...].astype(F32), axis=1, keepdims=True) / gain
        tail = jnp.where(lane == gain_lane, gain_grad, 0.0) + other_ref[...]
    if with_logits:
        x_ref, logit_ref = refs[:2]
        refs = refs[2:]
        tail = tail + mm(x_ref[...], logit_ref[...], TN)
    if tail_out:
        refs.pop()[...] = tail
    tail = tail.astype(BF16) if with_logits else None
    store_blocks(product, tail, column, place_ref, per, fsdps, seqs, first, refs)


def weight_grad(place, a, b, parts, first, gain=None, logits=None, cols=None, at_b=0):
    rows, total = a.shape
    cols = cols or b.shape[1]
    fsdps = lax.axis_size("fsdp")
    per = total // (parts * fsdps)
    tile = min(GRAD_TILE, total)
    wide = cols + (LANES if logits is not None else 0)
    columns = lambda n: pl.BlockSpec((n, tile), lambda c, *_: (0, c))
    lines = lambda n, at=0: pl.BlockSpec((tile, n), lambda c, *_: (c, at))
    whole = lambda *dims: pl.BlockSpec(dims, lambda c, *_: (0,) * len(dims))
    args, in_specs = [a, b], [columns(rows), pl.BlockSpec((rows, cols), lambda c, *_: (0, at_b))]
    copies = 1 if first is None else 2
    block = (fsdps // copies, parts, per, wide)
    out_shape = [jax.ShapeDtypeStruct(block, BF16)] * copies
    out_specs = [whole(*block)] * copies
    lane = None
    if gain is not None:
        weight, weight_at, vectors, at, lane, other = gain
        args += [weight, vectors, other]
        in_specs += [lines(cols, weight_at), lines(LANES, at), lines(LANES)]
    tail_out = gain is not None and logits is None
    if tail_out:
        out_shape = out_shape + [jax.ShapeDtypeStruct((total, LANES), F32)]
        out_specs = out_specs + [lines(LANES)]
    if logits is not None:
        args += list(logits)
        in_specs += [columns(logits[0].shape[0]), whole(*logits[1].shape)]
    return pl.pallas_call(
        partial(
            weight_grad_kernel,
            per=per,
            fsdps=fsdps,
            seqs=lax.axis_size("seq"),
            first=first,
            gain_lane=lane,
            with_logits=logits is not None,
            tail_out=tail_out,
        ),
        grid_spec=pltpu.PrefetchScalarGridSpec(
            num_scalar_prefetch=1,
            grid=(total // tile,),
            in_specs=in_specs,
            out_specs=out_specs,
        ),
        out_shape=out_shape,
        compiler_params=pltpu.CompilerParams(vmem_limit_bytes=GRAD_LIMIT),
        cost_estimate=pl.CostEstimate(
            flops=2 * rows * total * cols,
            transcendentals=0,
            bytes_accessed=2 * (rows * total + rows * cols + total * wide),
        ),
        name="weight_grad",
    )(place, *args)


def hidden_grads_kernel(
    place_ref, act_ref, carried_ref, norm_ref, pre_ref, w_ref, vec_ref, both_ref, tail_ref, *, per, down_per, fsdps, seqs, gain_lane
):
    column = pl.program_id(0)
    down = mm(act_ref[...], carried_ref[...], TN).astype(BF16)
    for t in range(down.shape[0] // down_per):
        slot = down_slot(column * (down.shape[0] // down_per) + t, fsdps, seqs)
        both_ref[slot, 1] = down[t * down_per : (t + 1) * down_per]
    product = mm(norm_ref[...], pre_ref[...], TN)
    lane = lax.broadcasted_iota(jnp.int32, (product.shape[0], LANES), 1)
    gain = vec_ref[...].astype(F32)[:, gain_lane : gain_lane + 1]
    gain_grad = jnp.sum(product * w_ref[...].astype(F32), axis=1, keepdims=True) / gain
    tail_ref[...] = jnp.where(lane == gain_lane, gain_grad, 0.0)
    up = product.astype(BF16)
    pieces = product.shape[0] // per
    for t in range(pieces):
        piece = column * pieces + t
        part = lax.div(piece, fsdps) ^ place_ref[1]
        line = pl.multiple_of(part * per, per)
        both_ref[lax.rem(piece, fsdps), 0, pl.ds(line, per), :] = up[t * per : (t + 1) * per]


def hidden_grads(place, activated, carried_b, normal_m, grad_pre, w_up, vectors, at, lane):
    rows, total = activated.shape
    cols = carried_b.shape[1]
    fsdps = lax.axis_size("fsdp")
    seqs = lax.axis_size("seq")
    tile = min(GRAD_TILE, total)
    columns = pl.BlockSpec((rows, tile), lambda c, *_: (0, c))
    lines = lambda n, at=0: pl.BlockSpec((tile, n), lambda c, *_: (c, at))
    whole = lambda *dims: pl.BlockSpec(dims, lambda c, *_: (0,) * len(dims))
    both = (fsdps, 2, total // fsdps, cols)
    return pl.pallas_call(
        partial(
            hidden_grads_kernel,
            per=total // (seqs * fsdps),
            down_per=total // fsdps,
            fsdps=fsdps,
            seqs=seqs,
            gain_lane=lane,
        ),
        grid_spec=pltpu.PrefetchScalarGridSpec(
            num_scalar_prefetch=1,
            grid=(total // tile,),
            in_specs=[columns, whole(rows, cols), columns, whole(rows, cols), lines(cols), lines(LANES, at)],
            out_specs=[whole(*both), lines(LANES)],
        ),
        out_shape=[jax.ShapeDtypeStruct(both, BF16), jax.ShapeDtypeStruct((total, LANES), F32)],
        compiler_params=pltpu.CompilerParams(vmem_limit_bytes=GRAD_LIMIT),
        cost_estimate=pl.CostEstimate(
            flops=4 * rows * total * cols,
            transcendentals=0,
            bytes_accessed=4 * (rows * total + rows * cols + total * cols),
        ),
        name="hidden_grads",
    )(place, activated, carried_b, normal_m, grad_pre, w_up, vectors)


def order_out_kernel(place_ref, *refs):
    out_ref = refs[-1]
    group, seqs = out_ref.shape[1:3]
    for k in range(seqs):
        for block in range(refs[k].shape[0]):
            shard = place_ref[0] ^ block
            at = lax.div(shard, group) ^ place_ref[1]
            out_ref[at, lax.rem(shard, group), place_ref[1] ^ k] = refs[k][block]


def order_out(place, blocks):
    seqs = len(blocks)
    fsdps, per, width = blocks[0].shape
    full = (seqs, fsdps // seqs, seqs, per, width)
    whole = lambda shape: pl.BlockSpec(shape, lambda i, *_: (0,) * len(shape))
    out = pl.pallas_call(
        order_out_kernel,
        grid_spec=pltpu.PrefetchScalarGridSpec(
            num_scalar_prefetch=1,
            grid=(1,),
            in_specs=[whole(blocks[0].shape)] * seqs,
            out_specs=whole(full),
        ),
        out_shape=jax.ShapeDtypeStruct(full, BF16),
        compiler_params=pltpu.CompilerParams(vmem_limit_bytes=VMEM_LIMIT),
        cost_estimate=pl.CostEstimate(flops=0, transcendentals=0, bytes_accessed=4 * width * width),
        name="order_out",
    )(place, *blocks)
    return out.reshape(-1, width)


ROW_TILE = 512


def pick_rows_kernel(ids_ref, *refs):
    count = len(refs) - 2
    to_ref, total = refs[count:]
    chunk = pl.program_id(0)
    ids = ids_ref[...] - chunk * ROW_TILE
    hit = ids == lax.broadcasted_iota(jnp.int32, (ids.shape[0], ROW_TILE), 1)
    ones = jnp.where(hit, 1.0, 0.0).astype(BF16)
    for i in range(count):
        found = mm(ones, refs[i][...], NN)

        @pl.when(chunk == 0)
        def _():
            total[i] = found

        @pl.when(chunk > 0)
        def _():
            total[i] += found

        @pl.when(chunk == pl.num_programs(0) - 1)
        def _():
            to_ref[i] = total[i].astype(BF16)


def pick_rows(sources, ids):
    length, width = sources[0].shape
    rows = ids.shape[0]
    count = len(sources)
    return pl.pallas_call(
        pick_rows_kernel,
        grid=(length // ROW_TILE,),
        in_specs=[pl.BlockSpec((rows, 1), lambda c: (0, 0))]
        + [pl.BlockSpec((ROW_TILE, width), lambda c: (c, 0))] * count,
        out_specs=pl.BlockSpec((count, rows, width), lambda c: (0, 0, 0)),
        out_shape=jax.ShapeDtypeStruct((count, rows, width), BF16),
        scratch_shapes=[pltpu.VMEM((count, rows, width), F32)],
        compiler_params=pltpu.CompilerParams(vmem_limit_bytes=VMEM_LIMIT),
        cost_estimate=pl.CostEstimate(
            flops=2 * count * rows * length * width,
            transcendentals=0,
            bytes_accessed=2 * count * length * width,
        ),
        name="pick_rows",
    )(ids[:, None], *sources)


def place_rows_kernel(ids_ref, new_ref, from_ref, to_ref):
    ids = ids_ref[...] - pl.program_id(0) * ROW_TILE
    hit = ids == lax.broadcasted_iota(jnp.int32, (ROW_TILE, ids.shape[1]), 0)
    ones = jnp.where(hit, 1.0, 0.0)
    routed = jnp.max(ones, axis=1, keepdims=True) > 0.0
    new = mm(ones.astype(BF16), new_ref[...], NN).astype(BF16)
    to_ref[...] = jnp.where(routed, new, from_ref[...])


def place_rows(source, ids, new):
    length, width = source.shape
    rows = ids.shape[0]
    tiles = pl.BlockSpec((ROW_TILE, width), lambda c: (c, 0))
    return pl.pallas_call(
        place_rows_kernel,
        grid=(length // ROW_TILE,),
        in_specs=[
            pl.BlockSpec((1, rows), lambda c: (0, 0)),
            pl.BlockSpec((rows, width), lambda c: (0, 0)),
            tiles,
        ],
        out_specs=tiles,
        out_shape=jax.ShapeDtypeStruct((length, width), BF16),
        compiler_params=pltpu.CompilerParams(vmem_limit_bytes=VMEM_LIMIT),
        cost_estimate=pl.CostEstimate(
            flops=2 * rows * length * width, transcendentals=0, bytes_accessed=4 * length * width
        ),
        name="place_rows",
    )(ids[None, :], new, source)


def half_lanes(values, half):
    lane = lax.broadcasted_iota(jnp.int32, values.shape, 1)
    keep = lane < HD if half == 0 else lane >= HD
    return jnp.where(keep, values, jnp.zeros_like(values))


def allowed_tile(keys_ref, where, pos_row, start_row):
    keys = keys_ref[where]
    return (keys <= pos_row) & (keys >= start_row)


def attention_forward_kernel(
    window_ref, place_ref, first_ref, q_ref, k_ref, v_ref, pos_ref, start_ref, keys_ref, o_ref, lse_ref
):
    block = pl.program_id(0)
    tile, width = q_ref.shape
    heads = width // HD
    pos_row, start_row = pos_ref[0], start_ref[0]
    last = window_ref[block]
    count = last - first_ref[block] + 1
    lanes = [slice(h // 2 * PAIR, (h // 2 + 1) * PAIR) for h in range(heads)]
    scale = jnp.asarray(HD**-0.5, BF16)
    queries = [half_lanes(q_ref[:, lanes[h]] * scale, h % 2) for h in range(heads)]

    def step(i, carry):
        where = place_ref[last - i]
        allowed = allowed_tile(keys_ref, where, pos_row, start_row)
        each = range(heads)
        raw = [mm(k_ref[where, :, lanes[h]], queries[h], NT) for h in each]
        scores = [jnp.where(allowed, raw[h], NEG_FILL) for h in each]
        tops = [jnp.maximum(carry[h][0], jnp.max(scores[h], axis=0, keepdims=True)) for h in each]
        exponents = [jnp.exp(scores[h] - tops[h]) for h in each]
        values = [mm(v_ref[where, :, lanes[h]], exponents[h].astype(BF16), TN) for h in each]
        shrinks = [jnp.exp(carry[h][0] - tops[h]) for h in each]
        sums = [jnp.sum(exponents[h], axis=0, keepdims=True) for h in each]
        return tuple(
            (tops[h], carry[h][1] * shrinks[h] + sums[h], carry[h][2] * shrinks[h] + values[h])
            for h in each
        )

    empty = (jnp.full((1, tile), NEG_FILL, F32), jnp.zeros((1, tile), F32), jnp.zeros((PAIR, tile), F32))
    done = lax.fori_loop(0, count, step, (empty,) * heads)
    for h in range(0, heads, 2):
        pair = [acc * (1.0 / total) for _, total, acc in done[h : h + 2]]
        joined = jnp.concatenate([pair[0][:HD], pair[1][HD:]], axis=0)
        o_ref[:, lanes[h]] = joined.T.astype(BF16)
    row = lax.broadcasted_iota(jnp.int32, (8, tile), 0)
    lse = jnp.zeros((8, tile), F32)
    for h, (top, total, _) in enumerate(done):
        lse = jnp.where(row == h, top + jnp.log(total), lse)
    lse_ref[...] = lse


def attention_backward_kernel(
    window_ref,
    place_ref,
    first_ref,
    q_ref,
    k_ref,
    v_ref,
    g_ref,
    o_ref,
    lse_ref,
    pos_ref,
    start_ref,
    keys_ref,
    grad_ref,
    dk_sum,
    dv_sum,
):
    block = pl.program_id(0)
    tile, width = q_ref.shape
    heads = width // HD
    pos_row, start_row = pos_ref[0], start_ref[0]
    last = window_ref[block]
    count = last - first_ref[block] + 1
    lanes = [slice(h // 2 * PAIR, (h // 2 + 1) * PAIR) for h in range(heads)]
    scale = HD**-0.5

    @pl.when(block == 0)
    def _():
        dk_sum[...] = jnp.zeros_like(dk_sum)
        dv_sum[...] = jnp.zeros_like(dv_sum)

    queries = [half_lanes(q_ref[:, lanes[h]] * jnp.asarray(scale, BF16), h % 2) for h in range(heads)]
    grads = [half_lanes(g_ref[:, lanes[h]], h % 2) for h in range(heads)]
    inner = []
    for h in range(0, heads, 2):
        both = (g_ref[:, lanes[h]].astype(F32) * o_ref[:, lanes[h]].astype(F32)).T
        inner += [jnp.sum(part, axis=0, keepdims=True) for part in (both[:HD], both[HD:])]

    def step(i, carry):
        where = place_ref[last - i]
        allowed = allowed_tile(keys_ref, where, pos_row, start_row)
        each = range(heads)
        keys = [k_ref[where, :, lanes[h]] for h in each]
        scores = [mm(keys[h], queries[h], NT) for h in each]
        grad_prob = [mm(v_ref[where, :, lanes[h]], grads[h], NT) for h in each]
        prob = [jnp.where(allowed, jnp.exp(scores[h] - lse_ref[h : h + 1, :]), 0.0) for h in each]
        grad_scores = [(prob[h] * (grad_prob[h] - inner[h])).astype(BF16) for h in each]
        values = [mm(prob[h].astype(BF16), grads[h], NN) for h in each]
        moved = [mm(grad_scores[h], queries[h], NN) for h in each]
        for h in range(0, heads, 2):
            dv_sum[where, :, lanes[h]] += values[h] + values[h + 1]
            dk_sum[where, :, lanes[h]] += moved[h] + moved[h + 1]
        return tuple(carry[h] + mm(keys[h], grad_scores[h], TN) for h in each)

    done = lax.fori_loop(0, count, step, (jnp.zeros((PAIR, tile), F32),) * heads)
    for h in range(0, heads, 2):
        joined = jnp.concatenate([done[h][:HD], done[h + 1][HD:]], axis=0) * scale
        at = 2 * width + h * HD
        grad_ref[block, :, at : at + PAIR] = joined.T.astype(BF16)

    @pl.when(block == pl.num_programs(0) - 1)
    def _():
        grad_ref[:, :, :width] = dk_sum[...].astype(BF16)
        grad_ref[:, :, width : 2 * width] = dv_sum[...].astype(BF16)


def attention_specs(blocks, tile, width):
    by_rows = pl.BlockSpec((tile, width), lambda b, *_: (b, 0))
    keys = lambda at: pl.BlockSpec((blocks, tile, width), lambda b, *_: (0, 0, at))
    row = pl.BlockSpec((1, 1, tile), lambda b, *_: (b, 0, 0))
    lse = pl.BlockSpec((8, tile), lambda b, *_: (0, b))
    return by_rows, keys, row, lse, pl.BlockSpec((blocks, tile, 1), lambda b, *_: (0, 0, 0))


def attention_forward(tables, q, kv, pos, start, tile):
    rows, width = q.shape
    blocks = rows // tile
    by_rows, keys, row, lse, cols = attention_specs(blocks, tile, width)
    return pl.pallas_call(
        attention_forward_kernel,
        grid_spec=pltpu.PrefetchScalarGridSpec(
            num_scalar_prefetch=3,
            grid=(blocks,),
            in_specs=[by_rows, keys(0), keys(1), row, row, cols],
            out_specs=[by_rows, lse],
        ),
        out_shape=[jax.ShapeDtypeStruct((rows, width), BF16), jax.ShapeDtypeStruct((8, rows), F32)],
        compiler_params=pltpu.CompilerParams(vmem_limit_bytes=GRAD_LIMIT),
        cost_estimate=pl.CostEstimate(
            flops=2 * rows * rows * width,
            transcendentals=rows * rows * width // HD // 2,
            bytes_accessed=8 * rows * width,
        ),
        name="attention_forward",
    )(
        *tables,
        q,
        kv.reshape(blocks, tile, 2 * width),
        kv.reshape(blocks, tile, 2 * width),
        pos.reshape(blocks, 1, tile),
        start.reshape(blocks, 1, tile),
        pos.reshape(blocks, tile, 1),
    )


def attention_backward(tables, q, kv, grad, out, lse_rows, pos, start, tile):
    rows, width = q.shape
    blocks = rows // tile
    by_rows, keys, row, lse, cols = attention_specs(blocks, tile, width)
    grads = pl.pallas_call(
        attention_backward_kernel,
        grid_spec=pltpu.PrefetchScalarGridSpec(
            num_scalar_prefetch=3,
            grid=(blocks,),
            in_specs=[by_rows, keys(0), keys(1), by_rows, by_rows, lse, row, row, cols],
            out_specs=pl.BlockSpec((blocks, tile, 3 * width), lambda b, *_: (0, 0, 0)),
            scratch_shapes=[pltpu.VMEM((blocks, tile, width), F32)] * 2,
        ),
        out_shape=jax.ShapeDtypeStruct((blocks, tile, 3 * width), BF16),
        compiler_params=pltpu.CompilerParams(vmem_limit_bytes=GRAD_LIMIT),
        cost_estimate=pl.CostEstimate(
            flops=5 * rows * rows * width,
            transcendentals=rows * rows * width // HD // 2,
            bytes_accessed=14 * rows * width,
        ),
        name="attention_backward",
    )(
        *tables,
        q,
        kv.reshape(blocks, tile, 2 * width),
        kv.reshape(blocks, tile, 2 * width),
        grad,
        out,
        lse_rows,
        pos.reshape(blocks, 1, tile),
        start.reshape(blocks, 1, tile),
        pos.reshape(blocks, tile, 1),
    )
    return grads.reshape(rows, 3 * width)


def whole_spec(shape):
    return pl.BlockSpec(shape, lambda i, *_: (0,) * len(shape))


def one_step(kernel, name, place, args, out_shape, flops):
    size = lambda x: x.size * x.dtype.itemsize
    return pl.pallas_call(
        kernel,
        grid_spec=pltpu.PrefetchScalarGridSpec(
            num_scalar_prefetch=1,
            grid=(1,),
            in_specs=[whole_spec(x.shape) for x in args],
            out_specs=[whole_spec(x.shape) for x in out_shape],
        ),
        out_shape=out_shape,
        compiler_params=pltpu.CompilerParams(vmem_limit_bytes=VMEM_LIMIT),
        cost_estimate=pl.CostEstimate(
            flops=flops, transcendentals=0, bytes_accessed=sum(size(x) for x in (*args, *out_shape))
        ),
        name=name,
    )(place, *args)


def norm_scale(values):
    return lax.rsqrt(jnp.mean(values * values, axis=1, keepdims=True) + EPS)


def first_shard_kernel(place_ref, q_ref, k_ref, v_ref, vec_ref, out_ref, own_ref):
    rows, span = q_ref.shape
    for i, ref in enumerate((k_ref, v_ref, q_ref)):
        own_ref[:rows, i * span : (i + 1) * span] = ref[...]
    lines = out_ref.shape[1]
    for j in range(out_ref.shape[2] // span):
        own_ref[j * lines : (j + 1) * lines, 3 * span :] = out_ref[0, :, j * span : (j + 1) * span]
    own_ref[rows:, :] = jnp.zeros((own_ref.shape[0] - rows, own_ref.shape[1]), BF16)
    own_ref[rows:, : vec_ref.shape[1]] = vec_ref[...]


def first_shard(place, qkv, vectors, out, span):
    rows, width = out.shape
    seqs = width // span
    out = out.reshape(seqs, rows // seqs, width)
    heads = lambda i: pl.BlockSpec((rows, span), lambda g, at: (0, i * seqs + at[1]))
    shape = (rows + vectors.shape[0], 4 * span)
    return pl.pallas_call(
        first_shard_kernel,
        grid_spec=pltpu.PrefetchScalarGridSpec(
            num_scalar_prefetch=1,
            grid=(1,),
            in_specs=[
                heads(0),
                heads(1),
                heads(2),
                pl.BlockSpec(vectors.shape, lambda g, at: (0, 0)),
                pl.BlockSpec((1, rows // seqs, width), lambda g, at: (at[1], 0, 0)),
            ],
            out_specs=pl.BlockSpec(shape, lambda g, at: (0, 0)),
        ),
        out_shape=jax.ShapeDtypeStruct(shape, BF16),
        compiler_params=pltpu.CompilerParams(vmem_limit_bytes=VMEM_LIMIT),
        cost_estimate=pl.CostEstimate(
            flops=0, transcendentals=0, bytes_accessed=4 * shape[0] * shape[1]
        ),
        name="first_shard",
    )(place, qkv, qkv, qkv, vectors, out)


def hidden_shard_kernel(place_ref, up_ref, down_ref, both_ref):
    rows = up_ref.shape[0]
    both_ref[:rows, :] = up_ref[...]
    both_ref[rows:, :] = down_ref[...]


def hidden_shard(place, up, down, span):
    rows, width = up.shape[0], down.shape[1]
    seqs = lax.axis_size("seq")
    return pl.pallas_call(
        hidden_shard_kernel,
        grid_spec=pltpu.PrefetchScalarGridSpec(
            num_scalar_prefetch=1,
            grid=(width // span,),
            in_specs=[
                pl.BlockSpec((rows, span), lambda i, at: (0, i * seqs + at[1])),
                pl.BlockSpec((span, span), lambda i, at: (at[1], i)),
            ],
            out_specs=pl.BlockSpec((rows + span, span), lambda i, at: (0, i)),
        ),
        out_shape=jax.ShapeDtypeStruct((rows + span, width), BF16),
        compiler_params=pltpu.CompilerParams(vmem_limit_bytes=VMEM_LIMIT),
        cost_estimate=pl.CostEstimate(flops=0, transcendentals=0, bytes_accessed=8 * rows * width),
        name="hidden_shard",
    )(place, up, down)


def project_kernel(place_ref, *refs, seqs, slow, fast):
    x_refs, pieces = refs[:seqs], refs[seqs:-7]
    out_ref, w_ref, vec_ref, normal_ref, q_ref, kv_ref, rate_ref = refs[-7:]
    span = q_ref.shape[1]
    per = w_ref.shape[0] // (slow * fast)
    lines = out_ref.shape[1]
    done = 0
    for ref in pieces:
        for i in range(ref.shape[0]):
            block = done % slow * fast + done // slow
            shard = place_ref[0] ^ block
            here = pl.ds(pl.multiple_of(shard * per, per), per)
            w_ref[here, : 3 * span] = ref[i, :per, : 3 * span]
            extra = ref[i, per:, :LANES].astype(F32)
            square = jnp.concatenate([extra, jnp.zeros((LANES - extra.shape[0], LANES), F32)], axis=0)
            w_ref[here, 3 * span :] = square.T[:per].astype(BF16)
            for j in range(seqs):
                out_ref[block, :, j * span : (j + 1) * span] = ref[i, j * lines : (j + 1) * lines, 3 * span :]
            done += 1
    tails = w_ref[:, 3 * span :]
    vec = tails.astype(F32).T
    vec_ref[...] = vec[:8]
    gain = vec[1:2]
    weight = w_ref[:, : 3 * span]
    rows = x_refs[0].shape[1]
    for k in range(seqs):
        here = slice(k * rows, (k + 1) * rows)
        x = x_refs[k][0]
        x_f = x.astype(F32)
        normal = (x_f * norm_scale(x_f) * gain).astype(BF16)
        normal_ref[here, :] = normal
        proj = mm(normal, weight, NN).astype(BF16)
        kv_ref[here, :] = proj[:, : 2 * span]
        q_ref[here, :] = proj[:, 2 * span :]
        rate_ref[here, :] = jax.nn.sigmoid(mm(x, tails, NN)[:, :1])


def project(place, x_blocks, pieces, span):
    slow, fast = fsdp_sizes()
    _, rows, width = x_blocks[0].shape
    total = rows * len(x_blocks)
    cols = 3 * span + LANES
    out_shape = [
        jax.ShapeDtypeStruct((slow * fast, width // (slow * fast * len(x_blocks)), width), BF16),
        jax.ShapeDtypeStruct((width, cols), BF16),
        jax.ShapeDtypeStruct((8, width), F32),
        jax.ShapeDtypeStruct((total, width), BF16),
        jax.ShapeDtypeStruct((total, span), BF16),
        jax.ShapeDtypeStruct((total, 2 * span), BF16),
        jax.ShapeDtypeStruct((total, 1), F32),
    ]
    kernel = partial(project_kernel, seqs=len(x_blocks), slow=slow, fast=fast)
    return one_step(
        kernel, "project", place, [*x_blocks, *pieces], out_shape, 2 * total * width * cols
    )


def branch_kernel(place_ref, *refs, seqs):
    x_refs, att_refs = refs[:seqs], refs[seqs : 2 * seqs]
    w_ref, vec_ref, rate_ref, branch_ref, normal_ref, carried_ref = refs[2 * seqs :]
    rows = x_refs[0].shape[1]
    span = att_refs[0].shape[1]
    gain = vec_ref[2:3, :]
    for j in range(seqs):
        here = slice(j * rows, (j + 1) * rows)
        branch = 0.0
        for b in range(seqs):
            there = slice((j ^ b) * rows, ((j ^ b) + 1) * rows)
            branch = branch + mm(att_refs[b][there, :], w_ref[b * span : (b + 1) * span, :], NN)
        if j == 0:
            branch_ref[...] = branch
        middle = x_refs[j][0].astype(F32) + branch
        normal_ref[here, :] = (middle * norm_scale(middle) * gain).astype(BF16)
        carried_ref[here, :] = (rate_ref[here, :] * x_refs[j][1].astype(F32)).astype(BF16)


def attention_branch(place, blocks, att_blocks, w_out, vectors, rate):
    _, rows, width = blocks[0].shape
    seqs = len(blocks)
    out_shape = [
        jax.ShapeDtypeStruct((rows, width), F32),
        jax.ShapeDtypeStruct((rows * seqs, width), BF16),
        jax.ShapeDtypeStruct((rows * seqs, width), BF16),
    ]
    args = [*blocks, *att_blocks, w_out, vectors, rate]
    return one_step(
        partial(branch_kernel, seqs=seqs),
        "attention_branch",
        place,
        args,
        out_shape,
        2 * rows * seqs * width * width,
    )


def attention_grad_kernel(place_ref, *refs, seqs):
    w_ref, joined_ref, out_ref = refs[seqs:]
    rows = refs[0].shape[0]
    for j in range(seqs):
        here = slice(j * rows, (j + 1) * rows)
        block = refs[j][...]
        joined_ref[here, :] = block
        out_ref[here, :] = mm(block, w_ref[...], NT).astype(BF16)


def attention_grad(place, blocks, w_out):
    rows, width = blocks[0].shape
    total = rows * len(blocks)
    span = w_out.shape[0]
    out_shape = [jax.ShapeDtypeStruct((total, width), BF16), jax.ShapeDtypeStruct((total, span), BF16)]
    return one_step(
        partial(attention_grad_kernel, seqs=len(blocks)),
        "attention_grad",
        place,
        [*blocks, w_out],
        out_shape,
        2 * total * width * span,
    )


def norm_back(values, scale, gain, grad):
    weighted = grad * gain
    inner = jnp.mean(weighted * values, axis=1, keepdims=True)
    return scale * weighted - values * (scale * scale * scale) * inner


def shards(
    inputs,
    cotangent,
    routed,
    doc_starts,
    router,
    attn_gain,
    qkv_weight,
    out_weight,
    mlp_gain,
    up_weight,
    down_weight,
):
    seqs = lax.axis_size("seq")
    fsdps = lax.axis_size("fsdp")
    me = lax.axis_index("seq")
    width = inputs.shape[2]
    tok_count = inputs.shape[1]
    own_windows = tok_count // WIN
    windows = routed.shape[1]
    tile = routed.shape[2]
    own_rows = own_windows * tile
    rows = windows * tile
    heads_width = width // seqs
    hidden = up_weight.shape[1]
    own_hidden = hidden // seqs

    order = jnp.arange(seqs, dtype=jnp.int32) ^ me
    window_of = (order[:, None] * own_windows + jnp.arange(own_windows, dtype=jnp.int32)).reshape(-1)
    stream_pos = jnp.arange(windows, dtype=jnp.int32)[:, None] * WIN + routed[0]
    pos = stream_pos[window_of].reshape(-1)
    starts = doc_starts[0]
    start = jnp.max(jnp.where(starts[None, :] <= pos[:, None], starts[None, :], 0), axis=1)
    first_window = start.reshape(windows, tile)[:, 0] // WIN
    place_of = jnp.zeros((windows,), jnp.int32).at[window_of].set(jnp.arange(windows, dtype=jnp.int32))
    tables = (window_of, place_of, first_window)

    own_routes = lax.dynamic_slice_in_dim(routed[0], me * own_windows, own_windows, 0)
    row_ids = ((jnp.arange(own_windows, dtype=jnp.int32) * WIN)[:, None] + own_routes).reshape(-1)
    stream_in = inputs[0]
    grad_in = cotangent[0]

    place = jnp.stack([lax.axis_index("fsdp"), me])
    vectors = jnp.stack([router, attn_gain, mlp_gain])
    vectors = jnp.pad(vectors, ((0, 8 - vectors.shape[0]), (0, LANES - vectors.shape[1])))
    first_own = first_shard(place, qkv_weight, vectors, out_weight, heads_width)
    first_slow = gather_slow(first_own)
    first_got = own_fast(first_slow[0])
    picked = pick_rows([stream_in, grad_in], after(row_ids, first_own))

    span = down_weight.shape[0] // seqs
    square = own_hidden == width and span % LANES == 0
    shard_rows = up_weight.shape[0]
    if square:
        hidden_own = hidden_shard(place, after(up_weight, picked, *first_got), down_weight, span)
        hidden_late = after(hidden_own, *first_slow[1:])
        hidden_all = lax.all_gather(hidden_late, "fsdp", axis=0)
        w_up = hidden_all[:, :shard_rows].reshape(width, own_hidden)
        w_down = hidden_all[:, shard_rows:].reshape(own_hidden, width)
    else:
        hidden_own = lax.dynamic_index_in_dim(
            up_weight.reshape(-1, fsdps, seqs, span), me, axis=2, keepdims=False
        ).reshape(-1, own_hidden)
        down_own = lax.dynamic_slice_in_dim(down_weight, me * span, span, 0)
        w_up = lax.all_gather(hidden_own, "fsdp", axis=0, tiled=True)
        w_down = lax.all_gather(down_own, "fsdp", axis=0, tiled=True)
    first_pieces = gather_fast(first_slow[0], after(tuple(first_slow[1:]), hidden_own), first_got)
    blocks = gather_blocks(picked, "seq", first_pieces[-1])
    out_part, w_qkv, vectors, normal_a, q, kv, rate = project(
        place, blocks, first_pieces, heads_width
    )
    router_w, gain_a, gain_m = vectors[0:1], vectors[1:2], vectors[2:3]
    tail_at = 3 * heads_width // LANES
    att_own, lse = attention_forward(tables, q, kv, pos, start, tile)
    out_blocks = gather_blocks(out_part, "seq", att_own)
    out_ordered = order_out(place, out_blocks)
    att_blocks = gather_blocks(att_own, "seq", out_ordered)
    w_out = out_ordered[:heads_width]
    branch_o, normal_m, carried_b = attention_branch(
        place, blocks, att_blocks, out_ordered, vectors, rate
    )
    pre_act = mm(normal_m, w_up, NN)
    cdf = 0.5 * (1.0 + lax.erf(pre_act * (0.5**0.5)))
    activated = (pre_act * cdf).astype(BF16)
    slope = cdf + pre_act * (jnp.exp(-0.5 * pre_act * pre_act) * (2.0 * jnp.pi) ** -0.5)

    grad_act = mm(carried_b, w_down, NT)
    grad_pre = (grad_act * slope).astype(BF16)
    cut = lambda a, b: a[b * own_rows : (b + 1) * own_rows]
    normal_grads = [mm(cut(grad_pre, b), w_up, NT) for b in range(seqs)]
    grad_normal_m = scatter_blocks(normal_grads, "seq")
    flat = place * jnp.array([1, 0], jnp.int32)
    scatter = lambda g: lax.psum_scatter(g, "fsdp", scatter_dimension=0)
    activated_late = after(activated, *normal_grads)
    if square:
        both, gains = hidden_grads(
            place, activated_late, carried_b, normal_m, grad_pre, w_up, w_qkv, tail_at, 2
        )
        grad_normal_m = after(grad_normal_m, both)
        both = scatter(both)
        up_part, down_part = both[0].reshape(seqs, -1, own_hidden), both[1]
    else:
        (down_grad,) = weight_grad(flat, activated_late, carried_b, 1, None)
        up_grad, gains = weight_grad(
            place,
            normal_m,
            grad_pre,
            seqs,
            None,
            (w_up, 0, w_qkv, tail_at, 2, jnp.zeros((width, LANES), F32)),
        )
        up_part, down_part = scatter(up_grad), scatter(down_grad)[0]

    x_o = picked[0].astype(F32)
    g_o = picked[1].astype(F32)
    rate_o = cut(rate, 0)
    middle_o = x_o + branch_o
    grad_middle = norm_back(middle_o, norm_scale(middle_o), gain_m, grad_normal_m)
    grad_a_own = (rate_o * g_o + grad_middle).astype(BF16)
    grad_a_blocks = gather_blocks(grad_a_own, "seq")
    branch_parts = [mm(cut(after(activated, grad_a_blocks[1]), b), w_down, NN) for b in range(seqs)]
    branch_f = scatter_blocks(branch_parts, "seq", grad_a_blocks[-1])
    grad_a, grad_att = attention_grad(place, grad_a_blocks, w_out)
    fast = 1
    slow = fsdp_sizes()[1]
    out_send, out_keep = weight_grad(flat, att_own, after(grad_a, *branch_parts), 1, fast)
    grad_proj = attention_backward(
        tables, q, kv, after(grad_att, out_send), att_own, lse, pos, start, tile
    )
    kv_send, kv_keep, gains = weight_grad(
        place,
        normal_a,
        grad_proj,
        seqs,
        fast,
        (w_qkv, 0, w_qkv, tail_at, 1, gains),
        cols=2 * heads_width,
    )
    branch_sum = branch_o + branch_f
    result = x_o + rate_o * branch_sum
    grad_logit = jnp.sum(g_o * branch_sum, axis=1, keepdims=True) * rate_o * (1.0 - rate_o)
    logit_high = grad_logit.astype(BF16)
    logit_low = (grad_logit - logit_high.astype(F32)).astype(BF16)
    lane = jnp.arange(LANES)[None, :]
    logits = jnp.where(lane == 0, logit_high, jnp.where(lane == 3, logit_low, jnp.zeros((), BF16)))
    q_send, q_keep = weight_grad(
        place,
        after(normal_a, kv_send),
        grad_proj,
        seqs,
        slow,
        (w_qkv, 2, w_qkv, tail_at, 1, gains),
        (picked[0], logits),
        cols=heads_width,
        at_b=2,
    )
    out_sum = reduce_blocks(out_send, out_keep, fast, [(q_send,)])[0]
    kv_part = reduce_blocks(kv_send, kv_keep, fast, [()])
    q_part = reduce_blocks(q_send, q_keep, slow, [()])
    proj_late = after(grad_proj, q_send)
    w_proj = w_qkv[:, : 3 * heads_width]
    grad_normal_a = scatter_blocks([mm(cut(proj_late, b), w_proj, NT) for b in range(seqs)], "seq")
    output = place_rows(stream_in, row_ids, after(result.astype(BF16), q_send))
    grad_norm_x = norm_back(x_o, norm_scale(x_o), gain_a, grad_normal_a)
    grad_picked = g_o + grad_middle + grad_norm_x + grad_logit * router_w
    input_grad = place_rows(grad_in, row_ids, grad_picked.astype(BF16))
    down_sum = lax.ppermute(
        down_part,
        ("seq", "fsdp"),
        [
            (s * fsdps + down_slot(f, fsdps, seqs), f * seqs + s)
            for s in range(seqs)
            for f in range(fsdps)
        ],
    ).astype(F32)
    qkv_part = jnp.concatenate(
        [q_part[:, :, :heads_width], kv_part, q_part[:, :, heads_width:]], axis=2
    )
    up_sum, qkv_sum, tiny = exchange_columns(up_part, qkv_part, span, heads_width)
    return (
        output[None],
        input_grad[None],
        tiny[:, 0] + tiny[:, 3],
        tiny[:, 1],
        qkv_sum,
        out_sum,
        tiny[:, 2],
        up_sum,
        down_sum,
    )


def solution(mesh):
    return jax.shard_map(
        shards,
        mesh=mesh,
        in_specs=(
            P("fsdp", "seq", None),
            P("fsdp", "seq", None),
            P("fsdp", None, None),
            P("fsdp", None),
            P("fsdp"),
            P("fsdp"),
            P("fsdp", None),
            P("fsdp", None),
            P("fsdp"),
            P("fsdp", None),
            P("fsdp", None),
        ),
        out_specs=(
            P("fsdp", "seq", None),
            P("fsdp", "seq", None),
            P(("seq", "fsdp")),
            P(("seq", "fsdp")),
            P(("seq", "fsdp"), None),
            P(("seq", "fsdp"), None),
            P(("seq", "fsdp")),
            P(("seq", "fsdp"), None),
            P(("seq", "fsdp"), None),
        ),
        check_vma=False,
    )
```
